32 devices in a mesh: pipe: 4 (over y, core), section: 4 (over z), tensor: 2 (over x).
Axes of the slice: x: 2, y: 2, z: 4, core: 2. Of those that a mesh axis runs over, the one named last changes fastest.
Arguments:
- bounds: int32 [2, 3], replicated, may hold values from 0 to 2, as said below
- saved_inputs: bfloat16 [4, 4, 2, 256, 1024], P('pipe', 'section', None, 'tensor')
- w_in: bfloat16 [4, 4, 2, 1024, 1024], P('pipe', 'section'), as said below
- w_out: bfloat16 [4, 4, 2, 1024, 1024], P('pipe', 'section')
- top_grad: bfloat16 [4, 2, 256, 1024], P('pipe', None, 'tensor'), may hold values from -0.125 to 0.125
Outputs:
- grad_in: float32 [4, 512, 1024], P('section', 'pipe', 'tensor')
- grad_out: float32 [4, 512, 1024], P('section', 'pipe', 'tensor')
The draws below stay inside these ranges and needn't reach their ends.
Inputs may be any that keep to these rules, and one draw needn't show every extreme that they name: Row p of bounds starts at 0 and never falls; each relay either uses all 2 sections with one layer each, or gives one or two layers to each of its first 1 section with its later entries equal to 2; at least one relay is of each kind. `w_in`: for k < bounds[p, s+1] - bounds[p, s], slot k of entries [2p + a, 2s + b] holds layer bounds[p, s] + k, the same for every a and b; a layer's weights are the same in every relay.
All inputs are finite; a program needn't handle non-finite values.
Results may differ from the reference program's by a relative error of at most 0.014.
Values may be sent and summed in bfloat16 or wider, within the bound.
No kernel may reach another device: no remote copies, remote signals or barrier semaphores. Data moves between devices by JAX's collectives and lax.ppermute only.
A program may use at most 64 MiB of HBM per device.

```python
import math
import jax
import jax.numpy as jnp
from jax import lax

D = 1024
ATT = 1024
SLOTS = 2
TOK = 1024
PIPES = 2
SECTIONS = 2
LAYERS = 2


def section_table(key):
    source = jax.random.fold_in(key, 1907)
    shorter = 3 * SECTIONS // 4
    coins = jax.random.randint(jax.random.fold_in(source, 5), (PIPES,), 0, 2)
    forced = jax.random.permutation(jax.random.fold_in(source, 6), PIPES)
    is_short = jnp.where(forced == 0, 1, jnp.where(forced == 1, 0, coins)) == 1
    positions = jnp.arange(SECTIONS)

    def counts_for(relay):
        picks = jax.random.permutation(jax.random.fold_in(jax.random.fold_in(source, 8), relay), shorter)
        doubled = jnp.concatenate([(picks < SECTIONS - shorter).astype(jnp.int32), jnp.zeros((SECTIONS - shorter,), jnp.int32)])
        short_counts = jnp.where(positions < shorter, 1 + doubled, 0)
        return jnp.where(is_short[relay], short_counts, jnp.ones((SECTIONS,), jnp.int32)).astype(jnp.int32)
    counts = jax.vmap(counts_for)(jnp.arange(PIPES))
    endings = jnp.cumsum(counts, axis=1).astype(jnp.int32)
    return jnp.concatenate([jnp.zeros((PIPES, 1), jnp.int32), endings], axis=1)


def draw_bounds(key, part):
    return section_table(key)


def layer_copies(key, salt, row_count, column_count, spread):
    boundary = section_table(key)
    layer_index = (boundary[:, :-1, None] + jnp.arange(SLOTS)[None, None, :]) % LAYERS
    widened = jnp.repeat(jnp.repeat(layer_index, 2, axis=0), 2, axis=1)
    noise_key = jax.random.fold_in(key, salt)
    layered = jax.random.normal(noise_key, (LAYERS, row_count, column_count), jnp.float32) * spread
    return layered.astype(jnp.bfloat16)[widened]


def draw_w_in(key, part):
    return layer_copies(key, 311, D, ATT, (D * math.sqrt(2.0 * LAYERS)) ** (-0.5))


def draw_w_out(key, part):
    return layer_copies(key, 523, ATT, D, (ATT * math.sqrt(2.0 * LAYERS)) ** (-0.5))


def draw_saved_inputs(key, part):
    source = jax.random.fold_in(key, 77)
    shape = (2 * PIPES, 2 * SECTIONS, SLOTS, TOK // 4, D)
    token_scale = jnp.exp(jax.random.uniform(jax.random.fold_in(source, 2), (2 * PIPES, 2 * SECTIONS, SLOTS, TOK // 4, 1), jnp.float32, math.log(0.3), math.log(3.0)))
    channel_scale = jnp.exp(jax.random.uniform(jax.random.fold_in(source, 3), (2 * PIPES, 2 * SECTIONS, SLOTS, 1, D), jnp.float32, -math.log(3.0), math.log(3.0)))
    noise = jnp.clip(jax.random.normal(jax.random.fold_in(source, 1), shape, jnp.float32), -4.0, 4.0)
    return (noise * token_scale * channel_scale).astype(jnp.bfloat16)


def block_levels(stream_key, shape, split, least, high):
    def one(position, shards_of):
        draws = jax.random.uniform(jax.random.fold_in(jax.random.fold_in(stream_key, 6), position), (shards_of,), jnp.float32, least / len(split), high / len(split))
        return jnp.repeat(jnp.exp(draws), shape[position] // shards_of).reshape((-1,) + (1,) * (len(shape) - position - 1))

    level = one(*split[0])
    for cut in split[1:]:
        level = level * one(*cut)
    return level


def bell_draw(stream_key, dims, width, reach, cuts=(), kind=jnp.bfloat16):
    loudness = block_levels(stream_key, dims, cuts, -0.22, 0.18) if cuts else 1.0
    drawn = jax.random.normal(stream_key, dims, jnp.float32) * width * loudness
    return jnp.minimum(jnp.maximum(drawn, -reach), reach).astype(kind)


def setup_inputs(seed: int = 0) -> dict:
    streams_of = jax.random.split(jax.random.key(seed), 6)
    return {
        "bounds": draw_bounds(jax.random.fold_in(streams_of[5], 71), 0),
        "saved_inputs": draw_saved_inputs(jax.random.fold_in(streams_of[5], 71), 0),
        "w_in": draw_w_in(jax.random.fold_in(streams_of[5], 71), 0),
        "w_out": draw_w_out(jax.random.fold_in(streams_of[5], 71), 0),
        "top_grad": bell_draw(streams_of[4], (2 * PIPES, 2, TOK // 4, D), (TOK * PIPES) ** -0.5, 0.125, ((0, 4), (2, 2))),
    }


EPS = 1e-05

def normalize(saved_rows):
    floats = saved_rows.astype(jnp.float32)
    row_scale = jnp.sqrt(lax.optimization_barrier(jnp.mean(floats * floats, axis=-1, keepdims=True)) + EPS)
    return (floats / row_scale, row_scale)

def relay_parts(boundary, saved_all, first_all, second_all, top_rows):
    layer_ids = jnp.arange(LAYERS, dtype=jnp.int32)
    section_of = lax.optimization_barrier(jnp.sum((boundary[None, 1:] <= layer_ids[:, None]).astype(jnp.int32), axis=1)).astype(jnp.int32)
    slot_of = (layer_ids - boundary[section_of]).astype(jnp.int32)
    inputs = saved_all[section_of, slot_of]
    firsts = first_all[section_of, slot_of]
    seconds = second_all[section_of, slot_of]

    def layer_step(grad_next, pieces):
        saved_rows, proj_in, proj_out = pieces
        unit_rows, row_scale = normalize(saved_rows)
        unit_low = unit_rows.astype(jnp.bfloat16)
        value_low = jnp.dot(unit_low, proj_in, preferred_element_type=jnp.float32).astype(jnp.bfloat16)
        err_low = jnp.dot(grad_next, proj_out.T, preferred_element_type=jnp.float32).astype(jnp.bfloat16)
        pulled = jnp.dot(err_low, proj_in.T, preferred_element_type=jnp.float32)
        inner_mean = lax.optimization_barrier(jnp.mean(pulled * unit_rows, axis=-1, keepdims=True))
        grad_here = (grad_next.astype(jnp.float32) + (pulled - unit_rows * inner_mean) / row_scale).astype(jnp.bfloat16)
        part_in = jnp.dot(unit_low.T, err_low, preferred_element_type=jnp.float32)
        part_out = jnp.dot(value_low.T, grad_next, preferred_element_type=jnp.float32)
        return (grad_here, (part_in, part_out))
    final_grad, parts = lax.scan(layer_step, top_rows, (inputs, firsts, seconds), reverse=True)
    return parts

def reference(bounds, saved_inputs, w_in, w_out, top_grad):
    quarter = saved_inputs.shape[3]

    def add_relay(relay, totals):
        first_row = (2 * relay).astype(jnp.int32)
        saved_pair = lax.dynamic_slice_in_dim(saved_inputs, first_row, 2, 0)
        saved_all = saved_pair.reshape(2, SECTIONS, 2, SLOTS, quarter, D).transpose(1, 3, 0, 2, 4, 5).reshape(SECTIONS, SLOTS, 4 * quarter, D)
        first_all = lax.dynamic_index_in_dim(w_in, first_row, 0, keepdims=False)[::2]
        second_all = lax.dynamic_index_in_dim(w_out, first_row, 0, keepdims=False)[::2]
        top_rows = lax.dynamic_slice_in_dim(top_grad, first_row, 2, 0).reshape(4 * quarter, D)
        boundary = lax.dynamic_index_in_dim(bounds, relay, 0, keepdims=False)
        parts_in, parts_out = relay_parts(boundary, saved_all, first_all, second_all, top_rows)
        return (totals[0] + parts_in, totals[1] + parts_out)
    zeros_in = jnp.zeros((LAYERS, D, ATT), jnp.float32)
    zeros_out = jnp.zeros((LAYERS, ATT, D), jnp.float32)
    grad_in, grad_out = lax.fori_loop(0, PIPES, add_relay, (zeros_in, zeros_out))
    grad_in = jnp.roll(grad_in, 1, axis=0)
    grad_out = jnp.roll(grad_out, 1, axis=0)
    return (grad_in.reshape(2 * LAYERS, D // 2, ATT), grad_out.reshape(2 * LAYERS, ATT // 2, D))
```

```python
import jax
import jax.numpy as jnp
from jax import lax
from jax.experimental import pallas as pl
from jax.experimental.pallas import tpu as pltpu
from jax.sharding import PartitionSpec as P

EPS = 1e-05


def shifted(value, axis, steps):
    count = lax.axis_size(axis)
    pairs = [(source, (source + steps) % count) for source in range(count)]
    return lax.ppermute(value, axis, pairs)


def for_sending(shard):

    def short(part):
        return part.astype(jnp.bfloat16) if part.dtype == jnp.float32 else part

    return jax.tree.map(short, shard)


def partner(block, axis, bit):
    count = lax.axis_size(axis)
    route = []
    for low in range(count):
        high = low | 1 << bit
        if high != low and high < count:
            route += [(low, high), (high, low)]
    return lax.ppermute(block, axis, route)


def normalize(saved_rows):
    floats = saved_rows.astype(jnp.float32)
    row_scale = jnp.sqrt(jnp.mean(floats * floats, axis=-1, keepdims=True) + EPS)
    return (floats / row_scale, row_scale)


def layer_back(grad_next, unit_rows, row_scale, proj_in, proj_out):
    err_low = jnp.dot(grad_next, proj_out.T, preferred_element_type=jnp.float32).astype(
        jnp.bfloat16
    )
    pulled = jnp.dot(err_low, proj_in.T, preferred_element_type=jnp.float32)
    inner_mean = jnp.mean(pulled * unit_rows, axis=-1, keepdims=True)
    grad_here = (
        grad_next.astype(jnp.float32) + (pulled - unit_rows * inner_mean) / row_scale
    ).astype(jnp.bfloat16)
    return (grad_here, err_low)


def route_items(members, shifter, offset, occupied, positions, here_section, levels, sections):
    for bit_level in reversed(range(levels)):
        stride = 2**bit_level
        passed = offset // (2 * stride) * (2 * stride)
        present = occupied & ((positions[:, None] + passed) % sections == here_section)
        rising = offset // stride % 2 == 1
        send_mask = jnp.any(present & rising, axis=0)
        keep_mask = jnp.any(present & jnp.logical_not(rising), axis=0)
        outgoing = tuple(
            (
                jnp.where(send_mask[:, None, None], member, jnp.zeros_like(member))
                for member in members
            )
        )
        arrived = shifter(outgoing, stride)
        members = tuple(
            (
                jnp.where(keep_mask[:, None, None], member, jnp.zeros_like(member)) + landed
                for member, landed in zip(members, arrived)
            )
        )
    return members


def general_body(bounds, saved_inputs, w_in, w_out, top_grad):
    sections = lax.axis_size("section") // 2
    tensors = lax.axis_size("tensor")
    pipe_index = lax.axis_index("pipe")
    section_index = lax.axis_index("section")
    tensor_index = lax.axis_index("tensor")
    position = section_index // 2
    token_half = section_index % 2
    boundary = lax.dynamic_index_in_dim(bounds, pipe_index // 2, 0, keepdims=False)
    counts = boundary[1:] - boundary[:-1]
    layers_here = lax.dynamic_index_in_dim(counts, position, 0, keepdims=False)
    saved_rows = saved_inputs[0, 0]
    proj_in = w_in[0, 0]
    proj_out = w_out[0, 0]
    slot_count = saved_rows.shape[0]
    row_count = saved_rows.shape[1]
    model_width = saved_rows.shape[2]
    inner_width = proj_in.shape[2]
    unit_rows, scales = normalize(saved_rows)
    unit_low = unit_rows.astype(jnp.bfloat16)
    value_low = jnp.einsum(
        "kre,kea->kra", unit_low, proj_in, preferred_element_type=jnp.float32
    ).astype(jnp.bfloat16)
    positions = jnp.arange(sections, dtype=jnp.int32)
    slot_ids = jnp.arange(slot_count, dtype=jnp.int32)
    occupied = slot_ids[None, :] < counts[:, None]
    layer_of = boundary[:-1, None] + slot_ids[None, :]
    offset = (layer_of + 1 - positions[:, None]) % sections
    levels = min((sections - 3 * sections // 4 + 1).bit_length(), (sections - 1).bit_length())
    top_rows = lax.dynamic_index_in_dim(top_grad[0], token_half, 0, keepdims=False)

    def run_section(incoming):

        def upper_layer(grad_top):
            return layer_back(grad_top, unit_rows[1], scales[1], proj_in[1], proj_out[1])

        def lower_layer(grad_top):
            return layer_back(grad_top, unit_rows[0], scales[0], proj_in[0], proj_out[0])

        def no_layer(grad_top):
            return (grad_top, jnp.zeros((row_count, inner_width), jnp.bfloat16))

        lower_start, upper_err = lax.cond(layers_here == 2, upper_layer, no_layer, incoming)
        result, lower_err = lax.cond(layers_here >= 1, lower_layer, no_layer, lower_start)
        return (result, jnp.stack([lower_start, incoming]), jnp.stack([lower_err, upper_err]))

    def loop_turn(turn_index, carried):
        incoming = shifted(carried[0], "section", -2)
        return lax.cond(
            position == sections - 1 - turn_index,
            lambda arriving, kept: run_section(arriving),
            lambda arriving, kept: kept,
            incoming,
            carried,
        )

    start_rows = jnp.where(position == 0, top_rows, jnp.zeros_like(top_rows))
    carried = (
        start_rows,
        jnp.zeros((slot_count, row_count, model_width), jnp.bfloat16),
        jnp.zeros((slot_count, row_count, inner_width), jnp.bfloat16),
    )
    carried = lax.fori_loop(0, sections, loop_turn, carried)
    grads_slots = carried[1]
    errors = carried[2]
    unit_got, value_got, err_got, grad_got = route_items(
        (unit_low, value_low, errors, grads_slots),
        lambda members, stride: jax.tree.map(
            lambda part, own: part.astype(own.dtype),
            shifted(for_sending(members), "section", 2 * stride),
            members,
        ),
        offset,
        occupied,
        positions,
        position,
        levels,
        sections,
    )
    owner_slot = jnp.sum(
        jnp.where(occupied & ((layer_of + 1) % sections == position), slot_ids[None, :], 0)
    )
    unit_own = lax.dynamic_index_in_dim(unit_got, owner_slot, 0, keepdims=False)
    value_own = lax.dynamic_index_in_dim(value_got, owner_slot, 0, keepdims=False)
    err_own = lax.dynamic_index_in_dim(err_got, owner_slot, 0, keepdims=False)
    grad_own = lax.dynamic_index_in_dim(grad_got, owner_slot, 0, keepdims=False)
    in_cols = inner_width // tensors
    out_cols = model_width // tensors
    unit_piece = lax.all_gather(unit_own, "tensor", axis=0, tiled=True)
    value_piece = lax.all_gather(value_own, "tensor", axis=0, tiled=True)
    err_piece = lax.all_gather(err_own, "tensor", axis=0, tiled=True)
    grad_piece = lax.all_gather(grad_own, "tensor", axis=0, tiled=True)
    err_cols = lax.dynamic_slice_in_dim(err_piece, tensor_index * in_cols, in_cols, 1)
    grad_cols = lax.dynamic_slice_in_dim(grad_piece, tensor_index * out_cols, out_cols, 1)
    totals = (
        jnp.dot(unit_piece.T, err_cols, preferred_element_type=jnp.float32),
        jnp.dot(value_piece.T, grad_cols, preferred_element_type=jnp.float32),
    )
    half_model = model_width // 2
    half_inner = inner_width // 2
    mine_in = lax.dynamic_slice_in_dim(totals[0], token_half * half_model, half_model, 0)
    other_in = lax.dynamic_slice_in_dim(totals[0], (1 - token_half) * half_model, half_model, 0)
    mine_out = lax.dynamic_slice_in_dim(totals[1], token_half * half_inner, half_inner, 0)
    other_out = lax.dynamic_slice_in_dim(totals[1], (1 - token_half) * half_inner, half_inner, 0)
    landed_in, landed_out = partner((other_in, other_out), "section", 0)
    grad_in_part, grad_out_part = (
        lax.psum_scatter(mine_in + landed_in, "pipe", scatter_dimension=0, tiled=True),
        lax.psum_scatter(mine_out + landed_out, "pipe", scatter_dimension=0, tiled=True),
    )
    return (grad_in_part[None], grad_out_part[None])


def norm_rows(saved):
    floats = saved.astype(jnp.float32)
    row_scale = jnp.sqrt(jnp.mean(floats * floats, axis=-1, keepdims=True) + EPS)
    return floats / row_scale, row_scale


def nt_dot(left, right):
    return lax.dot_general(left, right, (((1,), (1,)), ((), ())), preferred_element_type=jnp.float32)


def tn_dot(left, right):
    return lax.dot_general(left, right, (((0,), (0,)), ((), ())), preferred_element_type=jnp.float32)


def chain_kernel(pick, top_ref, saved_ref, w_in_ref, w_out_ref, grad_ref, q_buf, p_buf, err, pulled, sems):
    slot = pick[0]
    chunks = q_buf.shape[0]
    step = q_buf.shape[1]
    width = p_buf.shape[1]

    def q_copy(j):
        return pltpu.make_async_copy(w_out_ref.at[slot, pl.ds(j * step, step)], q_buf.at[j], sems.at[j])

    def p_copy(j):
        return pltpu.make_async_copy(w_in_ref.at[slot, pl.ds(j * width, width)], p_buf.at[j], sems.at[chunks + j])

    for j in range(chunks):
        q_copy(j).start()
    for j in range(chunks):
        p_copy(j).start()
    grad_next = top_ref[0]
    for j in range(chunks):
        q_copy(j).wait()
        err[:, j * step : (j + 1) * step] = nt_dot(grad_next, q_buf[j]).astype(jnp.bfloat16)
    unit, row_scale = norm_rows(saved_ref[0])
    for j in range(chunks):
        p_copy(j).wait()
        pulled[:, j * width : (j + 1) * width] = nt_dot(err[...], p_buf[j])
    back = pulled[...]
    inner_mean = jnp.mean(back * unit, axis=-1, keepdims=True)
    grad_ref[...] = (grad_next.astype(jnp.float32) + (back - unit * inner_mean) / row_scale).astype(jnp.bfloat16)


def chain(pick, tops, saved, w_in, w_out):
    rows, model = saved.shape[1:]
    inner = w_in.shape[2]
    chunks = 4
    return pl.pallas_call(
        chain_kernel,
        out_shape=jax.ShapeDtypeStruct((rows, model), jnp.bfloat16),
        grid_spec=pltpu.PrefetchScalarGridSpec(
            num_scalar_prefetch=1,
            grid=(1,),
            in_specs=[
                pl.BlockSpec((1, rows, model), lambda i, pick: (pick[1], 0, 0)),
                pl.BlockSpec((1, rows, model), lambda i, pick: (pick[0], 0, 0)),
                pl.BlockSpec(memory_space=pl.ANY),
                pl.BlockSpec(memory_space=pl.ANY),
            ],
            out_specs=pl.BlockSpec((rows, model), lambda i, pick: (0, 0)),
            scratch_shapes=[
                pltpu.VMEM((chunks, inner // chunks, model), jnp.bfloat16),
                pltpu.VMEM((chunks, model // chunks, inner), jnp.bfloat16),
                pltpu.VMEM((rows, inner), jnp.bfloat16),
                pltpu.VMEM((rows, model), jnp.float32),
                pltpu.SemaphoreType.DMA((2 * chunks,)),
            ],
        ),
        cost_estimate=pl.CostEstimate(
            flops=4 * rows * model * inner, bytes_accessed=4 * model * inner, transcendentals=0
        ),
        name="chain",
    )(pick, tops, saved, w_in, w_out)


def partial_kernel(
    pick, e1, e2, e3, late, f1, f2, f3, flate, w_in_ref, w_out_ref,
    in_send, in_keep, out_send, out_keep,
    q_buf, p_buf, unit, grads, err, value, unit_part, sems,
):
    slot, short, core, half, column = pick[0], pick[1], pick[2], pick[3], pick[4]
    rows = e1.shape[0]
    model = e1.shape[1]
    inner = err.shape[1]
    lanes = p_buf.shape[2]
    blocks = p_buf.shape[0]

    def first_of(j):
        return pl.multiple_of((2 * j + core) * lanes, lanes)

    q_copy = pltpu.make_async_copy(w_out_ref.at[slot], q_buf, sems.at[0])
    q_copy.start()
    p_copies = [
        pltpu.make_async_copy(w_in_ref.at[slot, :, pl.ds(first_of(j), lanes)], p_buf.at[j], sems.at[1 + j])
        for j in range(blocks)
    ]
    for copy in p_copies:
        copy.start()

    def put(place, units, tops):
        for n, (block, top) in enumerate(zip(units, tops)):
            where = pl.ds((2 * place + n) * rows, rows)
            unit[where, :] = norm_rows(block[...])[0].astype(jnp.bfloat16)
            grads[where, :] = top[...]

    @pl.when(short == 0)
    def _():
        put(0, (e1, e2), (late, e3))
        put(1, (f1, f2), (flate, f3))

    @pl.when(short != 0)
    def _():
        put(0, (late, e1), (e2, e3))
        put(1, (flate, f1), (f2, f3))

    for j in range(blocks):
        unit_part[:, j * lanes : (j + 1) * lanes] = unit[:, pl.ds(first_of(j), lanes)]
    q_copy.wait()
    err[...] = nt_dot(grads[...], q_buf[...]).astype(jnp.bfloat16)
    for j in range(blocks):
        p_copies[j].wait()
        value[:, j * lanes : (j + 1) * lanes] = jnp.dot(
            unit[...], p_buf[j], preferred_element_type=jnp.float32
        ).astype(jnp.bfloat16)
    half_cols = inner // 2
    mine = pl.ds(pl.multiple_of(column * half_cols, half_cols), half_cols)
    other = pl.ds(pl.multiple_of((1 - column) * half_cols, half_cols), half_cols)
    in_send[...] = tn_dot(unit_part[...], err[:, other]).astype(jnp.bfloat16)
    in_keep[...] = tn_dot(unit_part[...], err[:, mine])
    half_rows = value.shape[1] // 2
    upper = pl.ds(pl.multiple_of(half * half_rows, half_rows), half_rows)
    lower = pl.ds(pl.multiple_of((1 - half) * half_rows, half_rows), half_rows)
    out_send[...] = tn_dot(value[:, lower], grads[...]).astype(jnp.bfloat16)
    out_keep[...] = tn_dot(value[:, upper], grads[...])


def partials(pick, early, late, other_early, other_late, w_in, w_out):
    rows, model = late.shape
    inner = w_in.shape[2]
    blocks = 4
    tokens = 4 * rows
    lanes = model // (2 * blocks)
    part = blocks * lanes
    vmem = pl.BlockSpec(memory_space=pltpu.VMEM)
    hbm = pl.BlockSpec(memory_space=pl.ANY)
    return pl.pallas_call(
        partial_kernel,
        out_shape=(
            jax.ShapeDtypeStruct((part, inner // 2), jnp.bfloat16),
            jax.ShapeDtypeStruct((part, inner // 2), jnp.float32),
            jax.ShapeDtypeStruct((part // 2, model), jnp.bfloat16),
            jax.ShapeDtypeStruct((part // 2, model), jnp.float32),
        ),
        in_specs=[pl.BlockSpec(memory_space=pltpu.SMEM)] + [vmem] * 8 + [hbm] * 2,
        out_specs=(vmem,) * 4,
        scratch_shapes=[
            pltpu.VMEM((inner, model), jnp.bfloat16),
            pltpu.VMEM((blocks, model, lanes), jnp.bfloat16),
            pltpu.VMEM((tokens, model), jnp.bfloat16),
            pltpu.VMEM((tokens, model), jnp.bfloat16),
            pltpu.VMEM((tokens, inner), jnp.bfloat16),
            pltpu.VMEM((tokens, part), jnp.bfloat16),
            pltpu.VMEM((tokens, part), jnp.bfloat16),
            pltpu.SemaphoreType.DMA((1 + blocks,)),
        ],
        compiler_params=pltpu.CompilerParams(vmem_limit_bytes=40 * 2**20),
        cost_estimate=pl.CostEstimate(
            flops=10 * rows * model * inner, bytes_accessed=3 * model * inner, transcendentals=0
        ),
        name="partials",
    )(pick, *early, late, *other_early, other_late, w_in, w_out)


def moved(value, route):
    sections = lax.axis_size("section")
    pairs = []
    for source in range(lax.axis_size("pipe") * sections):
        target = route(source // sections, source % sections)
        if target is not None:
            pairs.append((source, target[0] * sections + target[1]))
    return lax.ppermute(value, ("pipe", "section"), pairs)


def two_section_body(bounds, saved_inputs, w_in, w_out, top_grad):
    pipe_index = lax.axis_index("pipe")
    section_index = lax.axis_index("section")
    column = lax.axis_index("tensor")
    relay = pipe_index // 2
    core = pipe_index % 2
    half = section_index % 2
    left = section_index // 2 == 0
    boundary = lax.dynamic_index_in_dim(bounds, relay, 0, keepdims=False)
    short = boundary[1] - boundary[0] == 2
    saved = saved_inputs[0, 0]
    proj_in = w_in[0, 0]
    proj_out = w_out[0, 0]
    tops = top_grad[0]
    model = saved.shape[2]
    inner = proj_in.shape[2]
    top_rows = lax.dynamic_index_in_dim(tops, half, 0, keepdims=False)

    def across(value):
        return moved(value, lambda p, s: (p ^ 2, s))

    def across_left(value):
        return moved(value, lambda p, s: (p ^ 2, s) if s < 2 else None)

    def core_swap(value):
        return moved(value, lambda p, s: (p ^ 1, s) if s < 2 else None)

    def half_swap(value):
        return moved(value, lambda p, s: (p, s ^ 1) if s < 2 else None)

    def column_swap(value):
        return lax.ppermute(value, "tensor", [(0, 1), (1, 0)])

    swapped = across(jnp.where(left & jnp.logical_not(short), top_rows, saved[0]))
    upper_slot = jnp.where(left, 1, 0).astype(jnp.int32)
    grad_low = chain(jnp.stack([upper_slot, half.astype(jnp.int32)]), tops, saved, proj_in, proj_out)
    grad_other = across_left(grad_low)
    late = moved(jnp.where(short, swapped, grad_low), lambda p, s: (p, s - 2) if s >= 2 else None)
    own_saved = jnp.where(short, saved[1], saved[0])
    early = (own_saved, swapped, jnp.where(short, top_rows, grad_other))
    other_early = tuple(core_swap(part) for part in early)
    other_late = core_swap(late)
    pick = jnp.stack(
        [part.astype(jnp.int32) for part in (short, short, core, half, column)]
    )
    in_send, in_keep, out_send, out_keep = partials(
        pick, early, late, other_early, other_late, proj_in, proj_out
    )
    in_landed = column_swap(in_send)
    out_landed = half_swap(out_send)
    in_sum = (in_keep + in_landed.astype(jnp.float32)).reshape(2, -1, inner // 2)
    out_sum = out_keep + out_landed.astype(jnp.float32)
    in_mine = lax.dynamic_index_in_dim(in_sum, half, 0, keepdims=False)
    in_next = lax.dynamic_index_in_dim(in_sum, 1 - half, 0, keepdims=False)
    out_mine = lax.dynamic_slice_in_dim(out_sum, column * (model // 2), model // 2, 1)
    out_next = lax.dynamic_slice_in_dim(out_sum, (1 - column) * (model // 2), model // 2, 1)
    in_landed = half_swap(in_next.astype(jnp.bfloat16))
    out_landed = column_swap(out_next.astype(jnp.bfloat16))
    results = []
    for mine, landed in ((in_mine, in_landed), (out_mine, out_landed)):
        total = (mine + landed.astype(jnp.float32)).reshape(2, -1, mine.shape[1])
        own = lax.dynamic_index_in_dim(total, relay, 0, keepdims=False)
        sent = lax.dynamic_index_in_dim(total, 1 - relay, 0, keepdims=False).astype(jnp.bfloat16)
        got = across_left(sent)
        onward = moved(
            jnp.where(short, got, own.astype(jnp.bfloat16)),
            lambda p, s: (p, s + 2) if s < 2 else None,
        )
        lower = jnp.where(short, own, got.astype(jnp.float32))
        results.append(jnp.where(left, lower, onward.astype(jnp.float32))[None])
    return tuple(results)


def body(bounds, saved_inputs, w_in, w_out, top_grad):
    two_sections = lax.axis_size("section") == 4 and lax.axis_size("pipe") == 4
    if two_sections and lax.axis_size("tensor") == 2:
        return two_section_body(bounds, saved_inputs, w_in, w_out, top_grad)
    return general_body(bounds, saved_inputs, w_in, w_out, top_grad)


def solution(mesh):
    placed = (
        P(),
        P("pipe", "section", None, "tensor", None),
        P("pipe", "section", None, None, None),
        P("pipe", "section", None, None, None),
        P("pipe", None, "tensor", None),
    )
    return jax.shard_map(
        body,
        mesh=mesh,
        in_specs=placed,
        out_specs=(P("section", "pipe", "tensor"), P("section", "pipe", "tensor")),
        check_vma=False,
    )
```

```python
import jax
import jax.numpy as jnp
from jax import lax
from jax.experimental import pallas as pl
from jax.experimental.pallas import tpu as pltpu
from jax.sharding import PartitionSpec as P

EPS = 1e-05


def shifted(value, axis, steps):
    count = lax.axis_size(axis)
    pairs = [(source, (source + steps) % count) for source in range(count)]
    return lax.ppermute(value, axis, pairs)


def for_sending(shard):

    def short(part):
        return part.astype(jnp.bfloat16) if part.dtype == jnp.float32 else part

    return jax.tree.map(short, shard)


def partner(block, axis, bit):
    count = lax.axis_size(axis)
    route = []
    for low in range(count):
        high = low | 1 << bit
        if high != low and high < count:
            route += [(low, high), (high, low)]
    return lax.ppermute(block, axis, route)


def normalize(saved_rows):
    floats = saved_rows.astype(jnp.float32)
    row_scale = jnp.sqrt(jnp.mean(floats * floats, axis=-1, keepdims=True) + EPS)
    return (floats / row_scale, row_scale)


def layer_back(grad_next, unit_rows, row_scale, proj_in, proj_out):
    err_low = jnp.dot(grad_next, proj_out.T, preferred_element_type=jnp.float32).astype(
        jnp.bfloat16
    )
    pulled = jnp.dot(err_low, proj_in.T, preferred_element_type=jnp.float32)
    inner_mean = jnp.mean(pulled * unit_rows, axis=-1, keepdims=True)
    grad_here = (
        grad_next.astype(jnp.float32) + (pulled - unit_rows * inner_mean) / row_scale
    ).astype(jnp.bfloat16)
    return (grad_here, err_low)


def route_items(members, shifter, offset, occupied, positions, here_section, levels, sections):
    for bit_level in reversed(range(levels)):
        stride = 2**bit_level
        passed = offset // (2 * stride) * (2 * stride)
        present = occupied & ((positions[:, None] + passed) % sections == here_section)
        rising = offset // stride % 2 == 1
        send_mask = jnp.any(present & rising, axis=0)
        keep_mask = jnp.any(present & jnp.logical_not(rising), axis=0)
        outgoing = tuple(
            (
                jnp.where(send_mask[:, None, None], member, jnp.zeros_like(member))
                for member in members
            )
        )
        arrived = shifter(outgoing, stride)
        members = tuple(
            (
                jnp.where(keep_mask[:, None, None], member, jnp.zeros_like(member)) + landed
                for member, landed in zip(members, arrived)
            )
        )
    return members


def general_body(bounds, saved_inputs, w_in, w_out, top_grad):
    sections = lax.axis_size("section") // 2
    tensors = lax.axis_size("tensor")
    pipe_index = lax.axis_index("pipe")
    section_index = lax.axis_index("section")
    tensor_index = lax.axis_index("tensor")
    position = section_index // 2
    token_half = section_index % 2
    boundary = lax.dynamic_index_in_dim(bounds, pipe_index // 2, 0, keepdims=False)
    counts = boundary[1:] - boundary[:-1]
    layers_here = lax.dynamic_index_in_dim(counts, position, 0, keepdims=False)
    saved_rows = saved_inputs[0, 0]
    proj_in = w_in[0, 0]
    proj_out = w_out[0, 0]
    slot_count = saved_rows.shape[0]
    row_count = saved_rows.shape[1]
    model_width = saved_rows.shape[2]
    inner_width = proj_in.shape[2]
    unit_rows, scales = normalize(saved_rows)
    unit_low = unit_rows.astype(jnp.bfloat16)
    value_low = jnp.einsum(
        "kre,kea->kra", unit_low, proj_in, preferred_element_type=jnp.float32
    ).astype(jnp.bfloat16)
    positions = jnp.arange(sections, dtype=jnp.int32)
    slot_ids = jnp.arange(slot_count, dtype=jnp.int32)
    occupied = slot_ids[None, :] < counts[:, None]
    layer_of = boundary[:-1, None] + slot_ids[None, :]
    offset = (layer_of + 1 - positions[:, None]) % sections
    levels = min((sections - 3 * sections // 4 + 1).bit_length(), (sections - 1).bit_length())
    top_rows = lax.dynamic_index_in_dim(top_grad[0], token_half, 0, keepdims=False)

    def run_section(incoming):

        def upper_layer(grad_top):
            return layer_back(grad_top, unit_rows[1], scales[1], proj_in[1], proj_out[1])

        def lower_layer(grad_top):
            return layer_back(grad_top, unit_rows[0], scales[0], proj_in[0], proj_out[0])

        def no_layer(grad_top):
            return (grad_top, jnp.zeros((row_count, inner_width), jnp.bfloat16))

        lower_start, upper_err = lax.cond(layers_here == 2, upper_layer, no_layer, incoming)
        result, lower_err = lax.cond(layers_here >= 1, lower_layer, no_layer, lower_start)
        return (result, jnp.stack([lower_start, incoming]), jnp.stack([lower_err, upper_err]))

    def loop_turn(turn_index, carried):
        incoming = shifted(carried[0], "section", -2)
        return lax.cond(
            position == sections - 1 - turn_index,
            lambda arriving, kept: run_section(arriving),
            lambda arriving, kept: kept,
            incoming,
            carried,
        )

    start_rows = jnp.where(position == 0, top_rows, jnp.zeros_like(top_rows))
    carried = (
        start_rows,
        jnp.zeros((slot_count, row_count, model_width), jnp.bfloat16),
        jnp.zeros((slot_count, row_count, inner_width), jnp.bfloat16),
    )
    carried = lax.fori_loop(0, sections, loop_turn, carried)
    grads_slots = carried[1]
    errors = carried[2]
    unit_got, value_got, err_got, grad_got = route_items(
        (unit_low, value_low, errors, grads_slots),
        lambda members, stride: jax.tree.map(
            lambda part, own: part.astype(own.dtype),
            shifted(for_sending(members), "section", 2 * stride),
            members,
        ),
        offset,
        occupied,
        positions,
        position,
        levels,
        sections,
    )
    owner_slot = jnp.sum(
        jnp.where(occupied & ((layer_of + 1) % sections == position), slot_ids[None, :], 0)
    )
    unit_own = lax.dynamic_index_in_dim(unit_got, owner_slot, 0, keepdims=False)
    value_own = lax.dynamic_index_in_dim(value_got, owner_slot, 0, keepdims=False)
    err_own = lax.dynamic_index_in_dim(err_got, owner_slot, 0, keepdims=False)
    grad_own = lax.dynamic_index_in_dim(grad_got, owner_slot, 0, keepdims=False)
    in_cols = inner_width // tensors
    out_cols = model_width // tensors
    unit_piece = lax.all_gather(unit_own, "tensor", axis=0, tiled=True)
    value_piece = lax.all_gather(value_own, "tensor", axis=0, tiled=True)
    err_piece = lax.all_gather(err_own, "tensor", axis=0, tiled=True)
    grad_piece = lax.all_gather(grad_own, "tensor", axis=0, tiled=True)
    err_cols = lax.dynamic_slice_in_dim(err_piece, tensor_index * in_cols, in_cols, 1)
    grad_cols = lax.dynamic_slice_in_dim(grad_piece, tensor_index * out_cols, out_cols, 1)
    totals = (
        jnp.dot(unit_piece.T, err_cols, preferred_element_type=jnp.float32),
        jnp.dot(value_piece.T, grad_cols, preferred_element_type=jnp.float32),
    )
    half_model = model_width // 2
    half_inner = inner_width // 2
    mine_in = lax.dynamic_slice_in_dim(totals[0], token_half * half_model, half_model, 0)
    other_in = lax.dynamic_slice_in_dim(totals[0], (1 - token_half) * half_model, half_model, 0)
    mine_out = lax.dynamic_slice_in_dim(totals[1], token_half * half_inner, half_inner, 0)
    other_out = lax.dynamic_slice_in_dim(totals[1], (1 - token_half) * half_inner, half_inner, 0)
    landed_in, landed_out = partner((other_in, other_out), "section", 0)
    grad_in_part, grad_out_part = (
        lax.psum_scatter(mine_in + landed_in, "pipe", scatter_dimension=0, tiled=True),
        lax.psum_scatter(mine_out + landed_out, "pipe", scatter_dimension=0, tiled=True),
    )
    return (grad_in_part[None], grad_out_part[None])


def norm_rows(saved):
    floats = saved.astype(jnp.float32)
    row_scale = jnp.sqrt(jnp.mean(floats * floats, axis=-1, keepdims=True) + EPS)
    return floats / row_scale, row_scale


def nt_dot(left, right):
    return lax.dot_general(left, right, (((1,), (1,)), ((), ())), preferred_element_type=jnp.float32)


def tn_dot(left, right):
    return lax.dot_general(left, right, (((0,), (0,)), ((), ())), preferred_element_type=jnp.float32)


def chain_kernel(pick, top_ref, saved_ref, w_in_ref, w_out_ref, grad_ref, q_buf, p_buf, err, pulled, sems):
    slot = pick[6]
    chunks = q_buf.shape[0]
    step = q_buf.shape[1]
    width = p_buf.shape[1]

    def q_copy(j):
        return pltpu.make_async_copy(w_out_ref.at[slot, pl.ds(j * step, step)], q_buf.at[j], sems.at[j])

    def p_copy(j):
        return pltpu.make_async_copy(w_in_ref.at[slot, pl.ds(j * width, width)], p_buf.at[j], sems.at[chunks + j])

    for j in range(chunks):
        q_copy(j).start()
    for j in range(chunks):
        p_copy(j).start()
    grad_next = top_ref[0]
    for j in range(chunks):
        q_copy(j).wait()
        err[:, j * step : (j + 1) * step] = nt_dot(grad_next, q_buf[j]).astype(jnp.bfloat16)
    unit, row_scale = norm_rows(saved_ref[0])
    for j in range(chunks):
        p_copy(j).wait()
        pulled[:, j * width : (j + 1) * width] = nt_dot(err[...], p_buf[j])
    back = pulled[...]
    inner_mean = jnp.mean(back * unit, axis=-1, keepdims=True)
    grad_ref[...] = (grad_next.astype(jnp.float32) + (back - unit * inner_mean) / row_scale).astype(jnp.bfloat16)


def chain(pick, tops, saved, w_in, w_out):
    rows, model = saved.shape[1:]
    inner = w_in.shape[2]
    chunks = 4
    return pl.pallas_call(
        chain_kernel,
        out_shape=jax.ShapeDtypeStruct((rows, model), jnp.bfloat16),
        grid_spec=pltpu.PrefetchScalarGridSpec(
            num_scalar_prefetch=1,
            grid=(1,),
            in_specs=[
                pl.BlockSpec((1, rows, model), lambda i, pick: (pick[3], 0, 0)),
                pl.BlockSpec((1, rows, model), lambda i, pick: (pick[6], 0, 0)),
                pl.BlockSpec(memory_space=pltpu.HBM),
                pl.BlockSpec(memory_space=pltpu.HBM),
            ],
            out_specs=pl.BlockSpec((rows, model), lambda i, pick: (0, 0)),
            scratch_shapes=[
                pltpu.VMEM((chunks, inner // chunks, model), jnp.bfloat16),
                pltpu.VMEM((chunks, model // chunks, inner), jnp.bfloat16),
                pltpu.VMEM((rows, inner), jnp.bfloat16),
                pltpu.VMEM((rows, model), jnp.float32),
                pltpu.SemaphoreType.DMA((2 * chunks,)),
            ],
        ),
        cost_estimate=pl.CostEstimate(
            flops=4 * rows * model * inner, bytes_accessed=4 * model * inner, transcendentals=0
        ),
        name="chain",
    )(pick, tops, saved, w_in, w_out)


def early_kernel(
    pick, e1, e2, e3, f1, f2, f3, w_in_ref, w_out_ref,
    in_acc, out_acc, q_buf, p_buf, early_part,
    unit, unit_part, grads, err, value, sems,
):
    slot, short, core = pick[0], pick[1], pick[2]
    rows = e1.shape[0]
    part = p_buf.shape[1]
    blocks = 4
    lanes = part // blocks

    def first_of(j):
        return pl.multiple_of((2 * j + core) * lanes, lanes)

    def gather_lanes(target, column):
        for j in range(blocks):
            target[:, column + j * lanes : column + (j + 1) * lanes] = unit[:, pl.ds(first_of(j), lanes)]

    copies = [pltpu.make_async_copy(w_out_ref.at[slot], q_buf, sems.at[0])]
    for j in range(blocks):
        copies.append(
            pltpu.make_async_copy(
                w_in_ref.at[slot, :, pl.ds(first_of(j), lanes)],
                p_buf.at[:, pl.ds(j * lanes, lanes)],
                sems.at[1 + j],
            )
        )
    for copy in copies:
        copy.start()

    def put_unit(first, second):
        unit[:rows, :] = norm_rows(first[...])[0].astype(jnp.bfloat16)
        unit[rows:, :] = norm_rows(second[...])[0].astype(jnp.bfloat16)

    @pl.when(short == 0)
    def _():
        put_unit(e2, f2)

    @pl.when(short != 0)
    def _():
        put_unit(e1, f1)

    gather_lanes(unit_part, 0)
    grads[:rows, :] = e3[...]
    grads[rows:, :] = f3[...]
    copies[0].wait()
    err[...] = nt_dot(grads[...], q_buf[...]).astype(jnp.bfloat16)
    in_acc[...] = tn_dot(unit_part[...], err[...])
    for copy in copies[1:]:
        copy.wait()
    value[...] = jnp.dot(unit[...], p_buf[...], preferred_element_type=jnp.float32).astype(jnp.bfloat16)
    out_acc[...] = tn_dot(value[...], grads[...])

    @pl.when(short == 0)
    def _():
        put_unit(e1, f1)
        gather_lanes(early_part, 0)
        early_part[:, part:] = jnp.dot(
            unit[...], p_buf[...], preferred_element_type=jnp.float32
        ).astype(jnp.bfloat16)

    @pl.when(short != 0)
    def _():
        grads[:rows, :] = e2[...]
        grads[rows:, :] = f2[...]
        early_part[...] = nt_dot(grads[...], q_buf[...]).astype(jnp.bfloat16)


def late_kernel(
    pick, late, flate, e2, f2, early_part, q_buf, p_buf, in_acc, out_acc,
    in_send, in_keep, out_send, out_keep,
    unit, unit_part, value, grads, err,
):
    short, core, half, column = pick[1], pick[2], pick[3], pick[4]
    rows = late.shape[0]
    part = p_buf.shape[1]
    blocks = 4
    lanes = part // blocks

    @pl.when(short == 0)
    def _():
        grads[:rows, :] = late[...]
        grads[rows:, :] = flate[...]
        err[...] = nt_dot(grads[...], q_buf[...]).astype(jnp.bfloat16)
        unit_part[...] = early_part[:, :part]
        value[...] = early_part[:, part:]

    @pl.when(short != 0)
    def _():
        unit[:rows, :] = norm_rows(late[...])[0].astype(jnp.bfloat16)
        unit[rows:, :] = norm_rows(flate[...])[0].astype(jnp.bfloat16)
        for j in range(blocks):
            first = pl.multiple_of((2 * j + core) * lanes, lanes)
            unit_part[:, j * lanes : (j + 1) * lanes] = unit[:, pl.ds(first, lanes)]
        value[...] = jnp.dot(unit[...], p_buf[...], preferred_element_type=jnp.float32).astype(jnp.bfloat16)
        grads[:rows, :] = e2[...]
        grads[rows:, :] = f2[...]
        err[...] = early_part[...]

    half_cols = err.shape[1] // 2
    mine = pl.ds(pl.multiple_of(column * half_cols, half_cols), half_cols)
    other = pl.ds(pl.multiple_of((1 - column) * half_cols, half_cols), half_cols)
    in_send[...] = (in_acc[:, other] + tn_dot(unit_part[...], err[:, other])).astype(jnp.bfloat16)
    in_keep[...] = in_acc[:, mine] + tn_dot(unit_part[...], err[:, mine])
    half_rows = part // 2
    upper = pl.ds(pl.multiple_of(half * half_rows, half_rows), half_rows)
    lower = pl.ds(pl.multiple_of((1 - half) * half_rows, half_rows), half_rows)
    out_send[...] = (out_acc[lower, :] + tn_dot(value[:, lower], grads[...])).astype(jnp.bfloat16)
    out_keep[...] = out_acc[upper, :] + tn_dot(value[:, upper], grads[...])


VMEM = pl.BlockSpec(memory_space=pltpu.VMEM)
SMEM = pl.BlockSpec(memory_space=pltpu.SMEM)
HBM = pl.BlockSpec(memory_space=pltpu.HBM)


def staged_kernel(pick, saved_ref, tops_ref, own_saved, own_top, given, sems):
    slot, half, give_top = pick[0], pick[3], pick[5]
    copies = (
        pltpu.make_async_copy(saved_ref.at[slot], own_saved, sems.at[1]),
        pltpu.make_async_copy(tops_ref.at[half], own_top, sems.at[2]),
    )

    @pl.when(give_top != 0)
    def _():
        pltpu.make_async_copy(tops_ref.at[half], given, sems.at[0]).start()

    @pl.when(give_top == 0)
    def _():
        pltpu.make_async_copy(saved_ref.at[0], given, sems.at[0]).start()

    for copy in copies:
        copy.start()
    pltpu.make_async_copy(saved_ref.at[0], given, sems.at[0]).wait()
    for copy in copies:
        copy.wait()


def staged(pick, saved, tops):
    block = jax.ShapeDtypeStruct(saved.shape[1:], saved.dtype)
    return pl.pallas_call(
        staged_kernel,
        out_shape=(block,) * 3,
        in_specs=[SMEM, HBM, HBM],
        out_specs=(VMEM,) * 3,
        scratch_shapes=[pltpu.SemaphoreType.DMA((3,))],
        compiler_params=pltpu.CompilerParams(vmem_limit_bytes=4 * 2**20),
        name="staged",
    )(pick, saved, tops)


def early_partials(pick, own, partner, w_in, w_out):
    rows, model = own[0].shape
    inner = w_in.shape[2]
    part = model // 2
    return pl.pallas_call(
        early_kernel,
        out_shape=(
            jax.ShapeDtypeStruct((part, inner), jnp.float32),
            jax.ShapeDtypeStruct((part, model), jnp.float32),
            jax.ShapeDtypeStruct((inner, model), jnp.bfloat16),
            jax.ShapeDtypeStruct((model, part), jnp.bfloat16),
            jax.ShapeDtypeStruct((2 * rows, model), jnp.bfloat16),
        ),
        in_specs=[SMEM] + [VMEM] * 6 + [HBM] * 2,
        out_specs=(VMEM,) * 5,
        scratch_shapes=[
            pltpu.VMEM((2 * rows, model), jnp.bfloat16),
            pltpu.VMEM((2 * rows, part), jnp.bfloat16),
            pltpu.VMEM((2 * rows, model), jnp.bfloat16),
            pltpu.VMEM((2 * rows, inner), jnp.bfloat16),
            pltpu.VMEM((2 * rows, part), jnp.bfloat16),
            pltpu.SemaphoreType.DMA((5,)),
        ],
        compiler_params=pltpu.CompilerParams(vmem_limit_bytes=24 * 2**20),
        cost_estimate=pl.CostEstimate(
            flops=10 * rows * model * inner, bytes_accessed=3 * model * inner, transcendentals=0
        ),
        name="early",
    )(pick, *own, *partner, w_in, w_out)


def late_partials(pick, late, other_late, own_top, other_top, early):
    in_acc, out_acc, q_buf, p_buf, early_part = early
    rows, model = late.shape
    inner = q_buf.shape[0]
    part = p_buf.shape[1]
    return pl.pallas_call(
        late_kernel,
        out_shape=(
            jax.ShapeDtypeStruct((part, inner // 2), jnp.bfloat16),
            jax.ShapeDtypeStruct((part, inner // 2), jnp.float32),
            jax.ShapeDtypeStruct((part // 2, model), jnp.bfloat16),
            jax.ShapeDtypeStruct((part // 2, model), jnp.float32),
        ),
        in_specs=[SMEM] + [VMEM] * 9,
        out_specs=(VMEM,) * 4,
        scratch_shapes=[
            pltpu.VMEM((2 * rows, model), jnp.bfloat16),
            pltpu.VMEM((2 * rows, part), jnp.bfloat16),
            pltpu.VMEM((2 * rows, part), jnp.bfloat16),
            pltpu.VMEM((2 * rows, model), jnp.bfloat16),
            pltpu.VMEM((2 * rows, inner), jnp.bfloat16),
        ],
        compiler_params=pltpu.CompilerParams(vmem_limit_bytes=28 * 2**20),
        cost_estimate=pl.CostEstimate(
            flops=8 * rows * model * inner, bytes_accessed=3 * model * inner, transcendentals=0
        ),
        name="late",
    )(pick, late, other_late, own_top, other_top, early_part, q_buf, p_buf, in_acc, out_acc)


def moved(value, route):
    sections = lax.axis_size("section")
    pairs = []
    for source in range(lax.axis_size("pipe") * sections):
        target = route(source // sections, source % sections)
        if target is not None:
            pairs.append((source, target[0] * sections + target[1]))
    return lax.ppermute(value, ("pipe", "section"), pairs)


def two_section_body(bounds, saved_inputs, w_in, w_out, top_grad):
    pipe_index = lax.axis_index("pipe")
    section_index = lax.axis_index("section")
    column = lax.axis_index("tensor")
    relay = pipe_index // 2
    core = pipe_index % 2
    half = section_index % 2
    left = section_index // 2 == 0
    boundary = lax.dynamic_index_in_dim(bounds, relay, 0, keepdims=False)
    short = boundary[1] - boundary[0] == 2
    saved = saved_inputs[0, 0]
    proj_in = w_in[0, 0]
    proj_out = w_out[0, 0]
    tops = top_grad[0]
    model = saved.shape[2]
    inner = proj_in.shape[2]

    def across(value):
        return moved(value, lambda p, s: (p ^ 2, s))

    def across_left(value):
        return moved(value, lambda p, s: (p ^ 2, s) if s < 2 else None)

    def core_swap(value):
        return moved(value, lambda p, s: (p ^ 1, s) if s < 2 else None)

    def half_swap(value):
        return moved(value, lambda p, s: (p, s ^ 1) if s < 2 else None)

    def column_swap(value):
        return lax.ppermute(value, "tensor", [(0, 1), (1, 0)])

    give_top = left & jnp.logical_not(short)
    pick = jnp.stack(
        [part.astype(jnp.int32) for part in (short, short, core, half, column, give_top, left)]
    )
    own_saved, own_top, given = staged(pick, saved, tops)
    swapped = across(given)
    grad_low = chain(pick, tops, saved, proj_in, proj_out)
    late = moved(jnp.where(short, swapped, grad_low), lambda p, s: (p, s - 2) if s >= 2 else None)
    grad_other = across_left(grad_low)
    own = (own_saved, swapped, jnp.where(short, own_top, grad_other))
    partner = tuple(core_swap(part) for part in own)
    early = early_partials(pick, own, partner, proj_in, proj_out)
    other_late = core_swap(late)
    in_send, in_keep, out_send, out_keep = late_partials(pick, late, other_late, own[1], partner[1], early)
    in_landed = column_swap(in_send)
    out_landed = half_swap(out_send)
    in_sum = (in_keep + in_landed.astype(jnp.float32)).reshape(2, -1, inner // 2)
    out_sum = out_keep + out_landed.astype(jnp.float32)
    in_mine = lax.dynamic_index_in_dim(in_sum, half, 0, keepdims=False)
    in_next = lax.dynamic_index_in_dim(in_sum, 1 - half, 0, keepdims=False)
    out_mine = lax.dynamic_slice_in_dim(out_sum, column * (model // 2), model // 2, 1)
    out_next = lax.dynamic_slice_in_dim(out_sum, (1 - column) * (model // 2), model // 2, 1)
    in_landed = half_swap(in_next.astype(jnp.bfloat16))
    out_landed = column_swap(out_next.astype(jnp.bfloat16))
    results = []
    for mine, landed in ((in_mine, in_landed), (out_mine, out_landed)):
        total = (mine + landed.astype(jnp.float32)).reshape(2, -1, mine.shape[1])
        own = lax.dynamic_index_in_dim(total, relay, 0, keepdims=False)
        sent = lax.dynamic_index_in_dim(total, 1 - relay, 0, keepdims=False).astype(jnp.bfloat16)
        got = across_left(sent)
        onward = moved(
            jnp.where(short, got, own.astype(jnp.bfloat16)),
            lambda p, s: (p, s + 2) if s < 2 else None,
        )
        lower = jnp.where(short, own, got.astype(jnp.float32))
        results.append(jnp.where(left, lower, onward.astype(jnp.float32))[None])
    return tuple(results)


def body(bounds, saved_inputs, w_in, w_out, top_grad):
    two_sections = lax.axis_size("section") == 4 and lax.axis_size("pipe") == 4
    if two_sections and lax.axis_size("tensor") == 2:
        return two_section_body(bounds, saved_inputs, w_in, w_out, top_grad)
    return general_body(bounds, saved_inputs, w_in, w_out, top_grad)


def solution(mesh):
    placed = (
        P(),
        P("pipe", "section", None, "tensor", None),
        P("pipe", "section", None, None, None),
        P("pipe", "section", None, None, None),
        P("pipe", None, "tensor", None),
    )
    return jax.shard_map(
        body,
        mesh=mesh,
        in_specs=placed,
        out_specs=(P("section", "pipe", "tensor"), P("section", "pipe", "tensor")),
        check_vma=False,
    )
```

```python
import jax
import jax.numpy as jnp
from jax import lax
from jax.experimental import pallas as pl
from jax.experimental.pallas import tpu as pltpu
from jax.sharding import PartitionSpec as P

EPS = 1e-05


def shifted(value, axis, steps):
    count = lax.axis_size(axis)
    pairs = [(source, (source + steps) % count) for source in range(count)]
    return lax.ppermute(value, axis, pairs)


def for_sending(shard):

    def short(part):
        return part.astype(jnp.bfloat16) if part.dtype == jnp.float32 else part

    return jax.tree.map(short, shard)


def partner(block, axis, bit):
    count = lax.axis_size(axis)
    route = []
    for low in range(count):
        high = low | 1 << bit
        if high != low and high < count:
            route += [(low, high), (high, low)]
    return lax.ppermute(block, axis, route)


def normalize(saved_rows):
    floats = saved_rows.astype(jnp.float32)
    row_scale = jnp.sqrt(jnp.mean(floats * floats, axis=-1, keepdims=True) + EPS)
    return (floats / row_scale, row_scale)


def layer_back(grad_next, unit_rows, row_scale, proj_in, proj_out):
    err_low = jnp.dot(grad_next, proj_out.T, preferred_element_type=jnp.float32).astype(
        jnp.bfloat16
    )
    pulled = jnp.dot(err_low, proj_in.T, preferred_element_type=jnp.float32)
    inner_mean = jnp.mean(pulled * unit_rows, axis=-1, keepdims=True)
    grad_here = (
        grad_next.astype(jnp.float32) + (pulled - unit_rows * inner_mean) / row_scale
    ).astype(jnp.bfloat16)
    return (grad_here, err_low)


def route_items(members, shifter, offset, occupied, positions, here_section, levels, sections):
    for bit_level in reversed(range(levels)):
        stride = 2**bit_level
        passed = offset // (2 * stride) * (2 * stride)
        present = occupied & ((positions[:, None] + passed) % sections == here_section)
        rising = offset // stride % 2 == 1
        send_mask = jnp.any(present & rising, axis=0)
        keep_mask = jnp.any(present & jnp.logical_not(rising), axis=0)
        outgoing = tuple(
            (
                jnp.where(send_mask[:, None, None], member, jnp.zeros_like(member))
                for member in members
            )
        )
        arrived = shifter(outgoing, stride)
        members = tuple(
            (
                jnp.where(keep_mask[:, None, None], member, jnp.zeros_like(member)) + landed
                for member, landed in zip(members, arrived)
            )
        )
    return members


def general_body(bounds, saved_inputs, w_in, w_out, top_grad):
    sections = lax.axis_size("section") // 2
    tensors = lax.axis_size("tensor")
    pipe_index = lax.axis_index("pipe")
    section_index = lax.axis_index("section")
    tensor_index = lax.axis_index("tensor")
    position = section_index // 2
    token_half = section_index % 2
    boundary = lax.dynamic_index_in_dim(bounds, pipe_index // 2, 0, keepdims=False)
    counts = boundary[1:] - boundary[:-1]
    layers_here = lax.dynamic_index_in_dim(counts, position, 0, keepdims=False)
    saved_rows = saved_inputs[0, 0]
    proj_in = w_in[0, 0]
    proj_out = w_out[0, 0]
    slot_count = saved_rows.shape[0]
    row_count = saved_rows.shape[1]
    model_width = saved_rows.shape[2]
    inner_width = proj_in.shape[2]
    unit_rows, scales = normalize(saved_rows)
    unit_low = unit_rows.astype(jnp.bfloat16)
    value_low = jnp.einsum(
        "kre,kea->kra", unit_low, proj_in, preferred_element_type=jnp.float32
    ).astype(jnp.bfloat16)
    positions = jnp.arange(sections, dtype=jnp.int32)
    slot_ids = jnp.arange(slot_count, dtype=jnp.int32)
    occupied = slot_ids[None, :] < counts[:, None]
    layer_of = boundary[:-1, None] + slot_ids[None, :]
    offset = (layer_of + 1 - positions[:, None]) % sections
    levels = min((sections - 3 * sections // 4 + 1).bit_length(), (sections - 1).bit_length())
    top_rows = lax.dynamic_index_in_dim(top_grad[0], token_half, 0, keepdims=False)

    def run_section(incoming):

        def upper_layer(grad_top):
            return layer_back(grad_top, unit_rows[1], scales[1], proj_in[1], proj_out[1])

        def lower_layer(grad_top):
            return layer_back(grad_top, unit_rows[0], scales[0], proj_in[0], proj_out[0])

        def no_layer(grad_top):
            return (grad_top, jnp.zeros((row_count, inner_width), jnp.bfloat16))

        lower_start, upper_err = lax.cond(layers_here == 2, upper_layer, no_layer, incoming)
        result, lower_err = lax.cond(layers_here >= 1, lower_layer, no_layer, lower_start)
        return (result, jnp.stack([lower_start, incoming]), jnp.stack([lower_err, upper_err]))

    def loop_turn(turn_index, carried):
        incoming = shifted(carried[0], "section", -2)
        return lax.cond(
            position == sections - 1 - turn_index,
            lambda arriving, kept: run_section(arriving),
            lambda arriving, kept: kept,
            incoming,
            carried,
        )

    start_rows = jnp.where(position == 0, top_rows, jnp.zeros_like(top_rows))
    carried = (
        start_rows,
        jnp.zeros((slot_count, row_count, model_width), jnp.bfloat16),
        jnp.zeros((slot_count, row_count, inner_width), jnp.bfloat16),
    )
    carried = lax.fori_loop(0, sections, loop_turn, carried)
    grads_slots = carried[1]
    errors = carried[2]
    unit_got, value_got, err_got, grad_got = route_items(
        (unit_low, value_low, errors, grads_slots),
        lambda members, stride: jax.tree.map(
            lambda part, own: part.astype(own.dtype),
            shifted(for_sending(members), "section", 2 * stride),
            members,
        ),
        offset,
        occupied,
        positions,
        position,
        levels,
        sections,
    )
    owner_slot = jnp.sum(
        jnp.where(occupied & ((layer_of + 1) % sections == position), slot_ids[None, :], 0)
    )
    unit_own = lax.dynamic_index_in_dim(unit_got, owner_slot, 0, keepdims=False)
    value_own = lax.dynamic_index_in_dim(value_got, owner_slot, 0, keepdims=False)
    err_own = lax.dynamic_index_in_dim(err_got, owner_slot, 0, keepdims=False)
    grad_own = lax.dynamic_index_in_dim(grad_got, owner_slot, 0, keepdims=False)
    in_cols = inner_width // tensors
    out_cols = model_width // tensors
    unit_piece = lax.all_gather(unit_own, "tensor", axis=0, tiled=True)
    value_piece = lax.all_gather(value_own, "tensor", axis=0, tiled=True)
    err_piece = lax.all_gather(err_own, "tensor", axis=0, tiled=True)
    grad_piece = lax.all_gather(grad_own, "tensor", axis=0, tiled=True)
    err_cols = lax.dynamic_slice_in_dim(err_piece, tensor_index * in_cols, in_cols, 1)
    grad_cols = lax.dynamic_slice_in_dim(grad_piece, tensor_index * out_cols, out_cols, 1)
    totals = (
        jnp.dot(unit_piece.T, err_cols, preferred_element_type=jnp.float32),
        jnp.dot(value_piece.T, grad_cols, preferred_element_type=jnp.float32),
    )
    half_model = model_width // 2
    half_inner = inner_width // 2
    mine_in = lax.dynamic_slice_in_dim(totals[0], token_half * half_model, half_model, 0)
    other_in = lax.dynamic_slice_in_dim(totals[0], (1 - token_half) * half_model, half_model, 0)
    mine_out = lax.dynamic_slice_in_dim(totals[1], token_half * half_inner, half_inner, 0)
    other_out = lax.dynamic_slice_in_dim(totals[1], (1 - token_half) * half_inner, half_inner, 0)
    landed_in, landed_out = partner((other_in, other_out), "section", 0)
    grad_in_part, grad_out_part = (
        lax.psum_scatter(mine_in + landed_in, "pipe", scatter_dimension=0, tiled=True),
        lax.psum_scatter(mine_out + landed_out, "pipe", scatter_dimension=0, tiled=True),
    )
    return (grad_in_part[None], grad_out_part[None])


VMEM = pl.BlockSpec(memory_space=pltpu.VMEM)
SMEM = pl.BlockSpec(memory_space=pltpu.SMEM)
HBM = pl.BlockSpec(memory_space=pltpu.HBM)


class Place:
    def __init__(self, bounds):
        pipe = lax.axis_index("pipe")
        section = lax.axis_index("section")
        self.column = lax.axis_index("tensor")
        self.relay = pipe // 2
        self.core = pipe % 2
        self.half = section % 2
        self.left = section < 2
        self.short = (bounds[self.relay, 1] - bounds[self.relay, 0]) == 2
        self.slot = jnp.where(self.short, 1, 0)
        self.upper_slot = jnp.where(self.left, 1, 0)


def norm_rows(saved):
    floats = saved.astype(jnp.float32)
    row_scale = jnp.sqrt(jnp.mean(floats * floats, axis=-1, keepdims=True) + EPS)
    return floats / row_scale, row_scale


def nt_dot(left, right):
    return lax.dot_general(left, right, (((1,), (1,)), ((), ())), preferred_element_type=jnp.float32)


def tn_dot(left, right):
    return lax.dot_general(left, right, (((0,), (0,)), ((), ())), preferred_element_type=jnp.float32)


def chain_kernel(
    bounds, top_ref, saved_ref, w_in_ref, w_out_ref, grad_ref, top, saved, q_buf, p_buf, err, pulled, sems
):
    place = Place(bounds)
    slot = place.upper_slot
    chunks = q_buf.shape[0]
    step = q_buf.shape[1]
    width = p_buf.shape[1]

    def q_copy(j):
        return pltpu.make_async_copy(w_out_ref.at[slot, pl.ds(j * step, step)], q_buf.at[j], sems.at[j])

    def p_copy(j):
        return pltpu.make_async_copy(w_in_ref.at[slot, pl.ds(j * width, width)], p_buf.at[j], sems.at[chunks + j])

    top_copy = pltpu.make_async_copy(top_ref.at[place.half], top, sems.at[2 * chunks])
    saved_copy = pltpu.make_async_copy(saved_ref.at[slot], saved, sems.at[2 * chunks + 1])
    top_copy.start()
    for j in range(chunks):
        q_copy(j).start()
    saved_copy.start()
    for j in range(chunks):
        p_copy(j).start()
    top_copy.wait()
    grad_next = top[...]
    for j in range(chunks):
        q_copy(j).wait()
        err[:, j * step : (j + 1) * step] = nt_dot(grad_next, q_buf[j]).astype(jnp.bfloat16)
    saved_copy.wait()
    unit, row_scale = norm_rows(saved[...])
    for j in range(chunks):
        p_copy(j).wait()
        pulled[:, j * width : (j + 1) * width] = nt_dot(err[...], p_buf[j])
    back = pulled[...]
    inner_mean = jnp.mean(back * unit, axis=-1, keepdims=True)
    grad_ref[...] = (grad_next.astype(jnp.float32) + (back - unit * inner_mean) / row_scale).astype(jnp.bfloat16)


def chain(bounds, tops, saved, w_in, w_out):
    rows, model = saved.shape[1:]
    inner = w_in.shape[2]
    chunks = 4
    return pl.pallas_call(
        chain_kernel,
        out_shape=jax.ShapeDtypeStruct((rows, model), jnp.bfloat16),
        in_specs=[SMEM] + [HBM] * 4,
        out_specs=VMEM,
        scratch_shapes=[
            pltpu.VMEM((rows, model), jnp.bfloat16),
            pltpu.VMEM((rows, model), jnp.bfloat16),
            pltpu.VMEM((chunks, inner // chunks, model), jnp.bfloat16),
            pltpu.VMEM((chunks, model // chunks, inner), jnp.bfloat16),
            pltpu.VMEM((rows, inner), jnp.bfloat16),
            pltpu.VMEM((rows, model), jnp.float32),
            pltpu.SemaphoreType.DMA((2 * chunks + 2,)),
        ],
        compiler_params=pltpu.CompilerParams(vmem_limit_bytes=60 * 2**20),
        cost_estimate=pl.CostEstimate(
            flops=4 * rows * model * inner, bytes_accessed=4 * model * inner, transcendentals=0
        ),
        name="chain",
    )(bounds, tops, saved, w_in, w_out)


def early_kernel(
    bounds, e1, e2, e3, f1, f2, f3, w_in_ref, w_out_ref,
    in_acc, out_acc, q_buf, p_buf, early_part,
    unit, unit_part, grads, err, value, sems,
):
    place = Place(bounds)
    slot, short, core = place.slot, place.short, place.core
    rows = e1.shape[0]
    part = p_buf.shape[1]
    blocks = 4
    lanes = part // blocks

    def first_of(j):
        return pl.multiple_of((2 * j + core) * lanes, lanes)

    def gather_lanes(target, column):
        for j in range(blocks):
            target[:, column + j * lanes : column + (j + 1) * lanes] = unit[:, pl.ds(first_of(j), lanes)]

    copies = [pltpu.make_async_copy(w_out_ref.at[slot], q_buf, sems.at[0])]
    for j in range(blocks):
        copies.append(
            pltpu.make_async_copy(
                w_in_ref.at[slot, :, pl.ds(first_of(j), lanes)],
                p_buf.at[:, pl.ds(j * lanes, lanes)],
                sems.at[1 + j],
            )
        )
    for copy in copies:
        copy.start()

    def put_unit(first, second):
        unit[:rows, :] = norm_rows(first[...])[0].astype(jnp.bfloat16)
        unit[rows:, :] = norm_rows(second[...])[0].astype(jnp.bfloat16)

    @pl.when(jnp.logical_not(short))
    def _():
        put_unit(e2, f2)

    @pl.when(short)
    def _():
        put_unit(e1, f1)

    gather_lanes(unit_part, 0)
    grads[:rows, :] = e3[...]
    grads[rows:, :] = f3[...]
    copies[0].wait()
    err[...] = nt_dot(grads[...], q_buf[...]).astype(jnp.bfloat16)
    in_acc[...] = tn_dot(unit_part[...], err[...])
    for copy in copies[1:]:
        copy.wait()
    value[...] = jnp.dot(unit[...], p_buf[...], preferred_element_type=jnp.float32).astype(jnp.bfloat16)
    out_acc[...] = tn_dot(value[...], grads[...])

    @pl.when(jnp.logical_not(short))
    def _():
        put_unit(e1, f1)
        gather_lanes(early_part, 0)
        early_part[:, part:] = jnp.dot(
            unit[...], p_buf[...], preferred_element_type=jnp.float32
        ).astype(jnp.bfloat16)

    @pl.when(short)
    def _():
        grads[:rows, :] = e2[...]
        grads[rows:, :] = f2[...]
        early_part[...] = nt_dot(grads[...], q_buf[...]).astype(jnp.bfloat16)


def late_kernel(
    bounds, late, flate, e2, f2, early_part, q_buf, p_buf, in_acc, out_acc,
    in_send, in_keep, out_send, out_keep,
    unit, unit_part, value, grads, err,
):
    place = Place(bounds)
    short, core, half, column = place.short, place.core, place.half, place.column
    rows = late.shape[0]
    part = p_buf.shape[1]
    blocks = 4
    lanes = part // blocks

    @pl.when(jnp.logical_not(short))
    def _():
        grads[:rows, :] = late[...]
        grads[rows:, :] = flate[...]
        err[...] = nt_dot(grads[...], q_buf[...]).astype(jnp.bfloat16)
        unit_part[...] = early_part[:, :part]
        value[...] = early_part[:, part:]

    @pl.when(short)
    def _():
        unit[:rows, :] = norm_rows(late[...])[0].astype(jnp.bfloat16)
        unit[rows:, :] = norm_rows(flate[...])[0].astype(jnp.bfloat16)
        for j in range(blocks):
            first = pl.multiple_of((2 * j + core) * lanes, lanes)
            unit_part[:, j * lanes : (j + 1) * lanes] = unit[:, pl.ds(first, lanes)]
        value[...] = jnp.dot(unit[...], p_buf[...], preferred_element_type=jnp.float32).astype(jnp.bfloat16)
        grads[:rows, :] = e2[...]
        grads[rows:, :] = f2[...]
        err[...] = early_part[...]

    half_cols = err.shape[1] // 2
    mine = pl.ds(pl.multiple_of(column * half_cols, half_cols), half_cols)
    other = pl.ds(pl.multiple_of((1 - column) * half_cols, half_cols), half_cols)
    in_send[...] = (in_acc[:, other] + tn_dot(unit_part[...], err[:, other])).astype(jnp.bfloat16)
    in_keep[...] = in_acc[:, mine] + tn_dot(unit_part[...], err[:, mine])
    half_rows = part // 2
    upper = pl.ds(pl.multiple_of(half * half_rows, half_rows), half_rows)
    lower = pl.ds(pl.multiple_of((1 - half) * half_rows, half_rows), half_rows)
    out_send[...] = (out_acc[lower, :] + tn_dot(value[:, lower], grads[...])).astype(jnp.bfloat16)
    out_keep[...] = out_acc[upper, :] + tn_dot(value[:, upper], grads[...])


def staged_kernel(bounds, saved_ref, tops_ref, own_saved, own_top, given, sems):
    place = Place(bounds)
    give_top = place.left & jnp.logical_not(place.short)
    copies = (
        pltpu.make_async_copy(saved_ref.at[place.slot], own_saved, sems.at[1]),
        pltpu.make_async_copy(tops_ref.at[place.half], own_top, sems.at[2]),
    )

    @pl.when(give_top)
    def _():
        pltpu.make_async_copy(tops_ref.at[place.half], given, sems.at[0]).start()

    @pl.when(jnp.logical_not(give_top))
    def _():
        pltpu.make_async_copy(saved_ref.at[0], given, sems.at[0]).start()

    for copy in copies:
        copy.start()
    pltpu.make_async_copy(saved_ref.at[0], given, sems.at[0]).wait()
    for copy in copies:
        copy.wait()


def staged(bounds, saved, tops):
    block = jax.ShapeDtypeStruct(saved.shape[1:], saved.dtype)
    return pl.pallas_call(
        staged_kernel,
        out_shape=(block,) * 3,
        in_specs=[SMEM, HBM, HBM],
        out_specs=(VMEM,) * 3,
        scratch_shapes=[pltpu.SemaphoreType.DMA((3,))],
        compiler_params=pltpu.CompilerParams(vmem_limit_bytes=60 * 2**20),
        name="staged",
    )(bounds, saved, tops)


def early_partials(bounds, own, partner, w_in, w_out):
    rows, model = own[0].shape
    inner = w_in.shape[2]
    part = model // 2
    return pl.pallas_call(
        early_kernel,
        out_shape=(
            jax.ShapeDtypeStruct((part, inner), jnp.float32),
            jax.ShapeDtypeStruct((part, model), jnp.float32),
            jax.ShapeDtypeStruct((inner, model), jnp.bfloat16),
            jax.ShapeDtypeStruct((model, part), jnp.bfloat16),
            jax.ShapeDtypeStruct((2 * rows, model), jnp.bfloat16),
        ),
        in_specs=[SMEM] + [VMEM] * 6 + [HBM] * 2,
        out_specs=(VMEM,) * 5,
        scratch_shapes=[
            pltpu.VMEM((2 * rows, model), jnp.bfloat16),
            pltpu.VMEM((2 * rows, part), jnp.bfloat16),
            pltpu.VMEM((2 * rows, model), jnp.bfloat16),
            pltpu.VMEM((2 * rows, inner), jnp.bfloat16),
            pltpu.VMEM((2 * rows, part), jnp.bfloat16),
            pltpu.SemaphoreType.DMA((5,)),
        ],
        compiler_params=pltpu.CompilerParams(vmem_limit_bytes=43 * 2**20),
        cost_estimate=pl.CostEstimate(
            flops=10 * rows * model * inner, bytes_accessed=3 * model * inner, transcendentals=0
        ),
        name="early",
    )(bounds, *own, *partner, w_in, w_out)


def late_partials(bounds, late, other_late, own_top, other_top, early):
    in_acc, out_acc, q_buf, p_buf, early_part = early
    rows, model = late.shape
    inner = q_buf.shape[0]
    part = p_buf.shape[1]
    return pl.pallas_call(
        late_kernel,
        out_shape=(
            jax.ShapeDtypeStruct((part, inner // 2), jnp.bfloat16),
            jax.ShapeDtypeStruct((part, inner // 2), jnp.float32),
            jax.ShapeDtypeStruct((part // 2, model), jnp.bfloat16),
            jax.ShapeDtypeStruct((part // 2, model), jnp.float32),
        ),
        in_specs=[SMEM] + [VMEM] * 9,
        out_specs=(VMEM,) * 4,
        scratch_shapes=[
            pltpu.VMEM((2 * rows, model), jnp.bfloat16),
            pltpu.VMEM((2 * rows, part), jnp.bfloat16),
            pltpu.VMEM((2 * rows, part), jnp.bfloat16),
            pltpu.VMEM((2 * rows, model), jnp.bfloat16),
            pltpu.VMEM((2 * rows, inner), jnp.bfloat16),
        ],
        compiler_params=pltpu.CompilerParams(vmem_limit_bytes=28 * 2**20),
        cost_estimate=pl.CostEstimate(
            flops=8 * rows * model * inner, bytes_accessed=3 * model * inner, transcendentals=0
        ),
        name="late",
    )(bounds, late, other_late, own_top, other_top, early_part, q_buf, p_buf, in_acc, out_acc)


def flipped(value, axis, bit):
    return lax.ppermute(value, axis, [(i, i ^ bit) for i in range(lax.axis_size(axis))])


def two_section_body(bounds, saved_inputs, w_in, w_out, top_grad):
    pipe_index = lax.axis_index("pipe")
    section_index = lax.axis_index("section")
    column = lax.axis_index("tensor")
    relay = pipe_index // 2
    half = section_index % 2
    left = section_index // 2 == 0
    boundary = lax.dynamic_index_in_dim(bounds, relay, 0, keepdims=False)
    short = boundary[1] - boundary[0] == 2
    saved = saved_inputs[0, 0]
    proj_in = w_in[0, 0]
    proj_out = w_out[0, 0]
    tops = top_grad[0]
    model = saved.shape[2]
    inner = proj_in.shape[2]

    def across(value):
        return flipped(value, "pipe", 2)

    def core_swap(value):
        return flipped(value, "pipe", 1)

    def half_swap(value):
        return flipped(value, "section", 1)

    def column_swap(value):
        return flipped(value, "tensor", 1)

    def section_swap(value):
        return flipped(value, "section", 2)

    own_saved, own_top, given = staged(bounds, saved, tops)
    swapped = across(given)
    grad_low = chain(bounds, tops, saved, proj_in, proj_out)
    late = section_swap(jnp.where(short, swapped, grad_low))
    grad_other = across(grad_low)
    own = (own_saved, swapped, jnp.where(short, own_top, grad_other))
    partner = tuple(core_swap(part) for part in own)
    early = early_partials(bounds, own, partner, proj_in, proj_out)
    other_late = core_swap(late)
    in_send, in_keep, out_send, out_keep = late_partials(bounds, late, other_late, own[1], partner[1], early)
    in_landed = column_swap(in_send)
    out_landed = half_swap(out_send)
    in_sum = (in_keep + in_landed.astype(jnp.float32)).reshape(2, -1, inner // 2)
    out_sum = out_keep + out_landed.astype(jnp.float32)
    in_mine = lax.dynamic_index_in_dim(in_sum, half, 0, keepdims=False)
    in_next = lax.dynamic_index_in_dim(in_sum, 1 - half, 0, keepdims=False)
    out_mine = lax.dynamic_slice_in_dim(out_sum, column * (model // 2), model // 2, 1)
    out_next = lax.dynamic_slice_in_dim(out_sum, (1 - column) * (model // 2), model // 2, 1)
    in_landed = half_swap(in_next.astype(jnp.bfloat16))
    out_landed = column_swap(out_next.astype(jnp.bfloat16))
    results = []
    for mine, landed in ((in_mine, in_landed), (out_mine, out_landed)):
        total = (mine + landed.astype(jnp.float32)).reshape(2, -1, mine.shape[1])
        own = lax.dynamic_index_in_dim(total, relay, 0, keepdims=False)
        sent = lax.dynamic_index_in_dim(total, 1 - relay, 0, keepdims=False).astype(jnp.bfloat16)
        got = across(sent)
        onward = section_swap(jnp.where(short, got, own.astype(jnp.bfloat16)))
        lower = jnp.where(short, own, got.astype(jnp.float32))
        results.append(jnp.where(left, lower, onward.astype(jnp.float32))[None])
    return tuple(results)


def body(bounds, saved_inputs, w_in, w_out, top_grad):
    two_sections = lax.axis_size("section") == 4 and lax.axis_size("pipe") == 4
    if two_sections and lax.axis_size("tensor") == 2:
        return two_section_body(bounds, saved_inputs, w_in, w_out, top_grad)
    return general_body(bounds, saved_inputs, w_in, w_out, top_grad)


def solution(mesh):
    placed = (
        P(),
        P("pipe", "section", None, "tensor", None),
        P("pipe", "section", None, None, None),
        P("pipe", "section", None, None, None),
        P("pipe", None, "tensor", None),
    )
    return jax.shard_map(
        body,
        mesh=mesh,
        in_specs=placed,
        out_specs=(P("section", "pipe", "tensor"), P("section", "pipe", "tensor")),
        check_vma=False,
    )
```

```python
import jax
import jax.numpy as jnp
from jax import lax
from jax.experimental import pallas as pl
from jax.experimental.pallas import tpu as pltpu
from jax.sharding import PartitionSpec as P

EPS = 1e-05


def shifted(value, axis, steps):
    count = lax.axis_size(axis)
    pairs = [(source, (source + steps) % count) for source in range(count)]
    return lax.ppermute(value, axis, pairs)


def for_sending(shard):

    def short(part):
        return part.astype(jnp.bfloat16) if part.dtype == jnp.float32 else part

    return jax.tree.map(short, shard)


def partner(block, axis, bit):
    count = lax.axis_size(axis)
    route = []
    for low in range(count):
        high = low | 1 << bit
        if high != low and high < count:
            route += [(low, high), (high, low)]
    return lax.ppermute(block, axis, route)


def normalize(saved_rows):
    floats = saved_rows.astype(jnp.float32)
    row_scale = jnp.sqrt(jnp.mean(floats * floats, axis=-1, keepdims=True) + EPS)
    return (floats / row_scale, row_scale)


def layer_back(grad_next, unit_rows, row_scale, proj_in, proj_out):
    err_low = jnp.dot(grad_next, proj_out.T, preferred_element_type=jnp.float32).astype(
        jnp.bfloat16
    )
    pulled = jnp.dot(err_low, proj_in.T, preferred_element_type=jnp.float32)
    inner_mean = jnp.mean(pulled * unit_rows, axis=-1, keepdims=True)
    grad_here = (
        grad_next.astype(jnp.float32) + (pulled - unit_rows * inner_mean) / row_scale
    ).astype(jnp.bfloat16)
    return (grad_here, err_low)


def route_items(members, shifter, offset, occupied, positions, here_section, levels, sections):
    for bit_level in reversed(range(levels)):
        stride = 2**bit_level
        passed = offset // (2 * stride) * (2 * stride)
        present = occupied & ((positions[:, None] + passed) % sections == here_section)
        rising = offset // stride % 2 == 1
        send_mask = jnp.any(present & rising, axis=0)
        keep_mask = jnp.any(present & jnp.logical_not(rising), axis=0)
        outgoing = tuple(
            (
                jnp.where(send_mask[:, None, None], member, jnp.zeros_like(member))
                for member in members
            )
        )
        arrived = shifter(outgoing, stride)
        members = tuple(
            (
                jnp.where(keep_mask[:, None, None], member, jnp.zeros_like(member)) + landed
                for member, landed in zip(members, arrived)
            )
        )
    return members


def general_body(bounds, saved_inputs, w_in, w_out, top_grad):
    sections = lax.axis_size("section") // 2
    tensors = lax.axis_size("tensor")
    pipe_index = lax.axis_index("pipe")
    section_index = lax.axis_index("section")
    tensor_index = lax.axis_index("tensor")
    position = section_index // 2
    token_half = section_index % 2
    boundary = lax.dynamic_index_in_dim(bounds, pipe_index // 2, 0, keepdims=False)
    counts = boundary[1:] - boundary[:-1]
    layers_here = lax.dynamic_index_in_dim(counts, position, 0, keepdims=False)
    saved_rows = saved_inputs[0, 0]
    proj_in = w_in[0, 0]
    proj_out = w_out[0, 0]
    slot_count = saved_rows.shape[0]
    row_count = saved_rows.shape[1]
    model_width = saved_rows.shape[2]
    inner_width = proj_in.shape[2]
    unit_rows, scales = normalize(saved_rows)
    unit_low = unit_rows.astype(jnp.bfloat16)
    value_low = jnp.einsum(
        "kre,kea->kra", unit_low, proj_in, preferred_element_type=jnp.float32
    ).astype(jnp.bfloat16)
    positions = jnp.arange(sections, dtype=jnp.int32)
    slot_ids = jnp.arange(slot_count, dtype=jnp.int32)
    occupied = slot_ids[None, :] < counts[:, None]
    layer_of = boundary[:-1, None] + slot_ids[None, :]
    offset = (layer_of + 1 - positions[:, None]) % sections
    levels = min((sections - 3 * sections // 4 + 1).bit_length(), (sections - 1).bit_length())
    top_rows = lax.dynamic_index_in_dim(top_grad[0], token_half, 0, keepdims=False)

    def run_section(incoming):

        def upper_layer(grad_top):
            return layer_back(grad_top, unit_rows[1], scales[1], proj_in[1], proj_out[1])

        def lower_layer(grad_top):
            return layer_back(grad_top, unit_rows[0], scales[0], proj_in[0], proj_out[0])

        def no_layer(grad_top):
            return (grad_top, jnp.zeros((row_count, inner_width), jnp.bfloat16))

        lower_start, upper_err = lax.cond(layers_here == 2, upper_layer, no_layer, incoming)
        result, lower_err = lax.cond(layers_here >= 1, lower_layer, no_layer, lower_start)
        return (result, jnp.stack([lower_start, incoming]), jnp.stack([lower_err, upper_err]))

    def loop_turn(turn_index, carried):
        incoming = shifted(carried[0], "section", -2)
        return lax.cond(
            position == sections - 1 - turn_index,
            lambda arriving, kept: run_section(arriving),
            lambda arriving, kept: kept,
            incoming,
            carried,
        )

    start_rows = jnp.where(position == 0, top_rows, jnp.zeros_like(top_rows))
    carried = (
        start_rows,
        jnp.zeros((slot_count, row_count, model_width), jnp.bfloat16),
        jnp.zeros((slot_count, row_count, inner_width), jnp.bfloat16),
    )
    carried = lax.fori_loop(0, sections, loop_turn, carried)
    grads_slots = carried[1]
    errors = carried[2]
    unit_got, value_got, err_got, grad_got = route_items(
        (unit_low, value_low, errors, grads_slots),
        lambda members, stride: jax.tree.map(
            lambda part, own: part.astype(own.dtype),
            shifted(for_sending(members), "section", 2 * stride),
            members,
        ),
        offset,
        occupied,
        positions,
        position,
        levels,
        sections,
    )
    owner_slot = jnp.sum(
        jnp.where(occupied & ((layer_of + 1) % sections == position), slot_ids[None, :], 0)
    )
    unit_own = lax.dynamic_index_in_dim(unit_got, owner_slot, 0, keepdims=False)
    value_own = lax.dynamic_index_in_dim(value_got, owner_slot, 0, keepdims=False)
    err_own = lax.dynamic_index_in_dim(err_got, owner_slot, 0, keepdims=False)
    grad_own = lax.dynamic_index_in_dim(grad_got, owner_slot, 0, keepdims=False)
    in_cols = inner_width // tensors
    out_cols = model_width // tensors
    unit_piece = lax.all_gather(unit_own, "tensor", axis=0, tiled=True)
    value_piece = lax.all_gather(value_own, "tensor", axis=0, tiled=True)
    err_piece = lax.all_gather(err_own, "tensor", axis=0, tiled=True)
    grad_piece = lax.all_gather(grad_own, "tensor", axis=0, tiled=True)
    err_cols = lax.dynamic_slice_in_dim(err_piece, tensor_index * in_cols, in_cols, 1)
    grad_cols = lax.dynamic_slice_in_dim(grad_piece, tensor_index * out_cols, out_cols, 1)
    totals = (
        jnp.dot(unit_piece.T, err_cols, preferred_element_type=jnp.float32),
        jnp.dot(value_piece.T, grad_cols, preferred_element_type=jnp.float32),
    )
    half_model = model_width // 2
    half_inner = inner_width // 2
    mine_in = lax.dynamic_slice_in_dim(totals[0], token_half * half_model, half_model, 0)
    other_in = lax.dynamic_slice_in_dim(totals[0], (1 - token_half) * half_model, half_model, 0)
    mine_out = lax.dynamic_slice_in_dim(totals[1], token_half * half_inner, half_inner, 0)
    other_out = lax.dynamic_slice_in_dim(totals[1], (1 - token_half) * half_inner, half_inner, 0)
    landed_in, landed_out = partner((other_in, other_out), "section", 0)
    grad_in_part, grad_out_part = (
        lax.psum_scatter(mine_in + landed_in, "pipe", scatter_dimension=0, tiled=True),
        lax.psum_scatter(mine_out + landed_out, "pipe", scatter_dimension=0, tiled=True),
    )
    return (grad_in_part[None], grad_out_part[None])


VMEM = pl.BlockSpec(memory_space=pltpu.VMEM)
SMEM = pl.BlockSpec(memory_space=pltpu.SMEM)
KERNEL_BYTES = 14 * 2**20
STAGE_FLOPS = 8 * 10**9


class Place:
    def __init__(self, bounds):
        pipe = lax.axis_index("pipe")
        section = lax.axis_index("section")
        self.column = lax.axis_index("tensor")
        self.relay = pipe // 2
        self.core = pipe % 2
        self.half = section % 2
        self.left = section < 2
        self.short = (bounds[self.relay, 1] - bounds[self.relay, 0]) == 2
        self.slot = jnp.where(self.short, 1, 0)
        self.upper_slot = jnp.where(self.left, 1, 0)


def norm_rows(saved):
    floats = saved.astype(jnp.float32)
    row_scale = jnp.sqrt(jnp.mean(floats * floats, axis=-1, keepdims=True) + EPS)
    return floats / row_scale, row_scale


def nt_dot(left, right):
    return lax.dot_general(left, right, (((1,), (1,)), ((), ())), preferred_element_type=jnp.float32)


def tn_dot(left, right):
    return lax.dot_general(left, right, (((0,), (0,)), ((), ())), preferred_element_type=jnp.float32)


def chain_kernel(bounds, tops, saved, w_in, w_out, grad_out):
    place = Place(bounds)
    slot = place.upper_slot
    grad_next = tops[place.half]
    err = nt_dot(grad_next, w_out[slot]).astype(jnp.bfloat16)
    unit, row_scale = norm_rows(saved[slot])
    pulled = nt_dot(err, w_in[slot])
    inner_mean = jnp.mean(pulled * unit, axis=-1, keepdims=True)
    back = grad_next.astype(jnp.float32) + (pulled - unit * inner_mean) / row_scale
    grad_out[...] = back.astype(jnp.bfloat16)


def chain(bounds, tops, saved, w_in, w_out):
    rows, model = saved.shape[1:]
    inner = w_in.shape[2]
    return pl.pallas_call(
        chain_kernel,
        out_shape=jax.ShapeDtypeStruct((rows, model), jnp.bfloat16),
        in_specs=[SMEM] + [VMEM] * 4,
        out_specs=VMEM,
        compiler_params=pltpu.CompilerParams(vmem_limit_bytes=KERNEL_BYTES),
        cost_estimate=pl.CostEstimate(
            flops=4 * rows * model * inner, bytes_accessed=4 * model * inner, transcendentals=0
        ),
        name="chain",
    )(bounds, tops, saved, w_in, w_out)


def opening_kernel(mark):
    mark[...] = jnp.zeros_like(mark)


def opening():
    return pl.pallas_call(
        opening_kernel,
        out_shape=jax.ShapeDtypeStruct((8, 128), jnp.float32),
        out_specs=VMEM,
        compiler_params=pltpu.CompilerParams(vmem_limit_bytes=KERNEL_BYTES),
        cost_estimate=pl.CostEstimate(flops=STAGE_FLOPS, bytes_accessed=4096, transcendentals=0),
        name="opening",
    )()


def staged_kernel(bounds, mark, saved, tops, own_saved, own_top, given):
    place = Place(bounds)
    give_top = place.left & jnp.logical_not(place.short)
    own_saved[...] = saved[place.slot]
    own_top[...] = tops[place.half]

    @pl.when(give_top)
    def _():
        given[...] = tops[place.half]

    @pl.when(jnp.logical_not(give_top))
    def _():
        given[...] = saved[0]


def staged(bounds, saved, tops):
    block = jax.ShapeDtypeStruct(saved.shape[1:], saved.dtype)
    return pl.pallas_call(
        staged_kernel,
        out_shape=(block,) * 3,
        in_specs=[SMEM, VMEM, VMEM, VMEM],
        out_specs=(VMEM,) * 3,
        compiler_params=pltpu.CompilerParams(vmem_limit_bytes=KERNEL_BYTES),
        cost_estimate=pl.CostEstimate(flops=STAGE_FLOPS, bytes_accessed=8 * saved.size, transcendentals=0),
        name="staged",
    )(bounds, opening(), saved, tops)


def by_role_kernel(bounds, full_part, short_part, chosen):
    place = Place(bounds)

    @pl.when(place.short)
    def _():
        chosen[...] = short_part[...]

    @pl.when(jnp.logical_not(place.short))
    def _():
        chosen[...] = full_part[...]


def by_role(bounds, full_part, short_part):
    return pl.pallas_call(
        by_role_kernel,
        out_shape=jax.ShapeDtypeStruct(full_part.shape, full_part.dtype),
        in_specs=[SMEM, VMEM, VMEM],
        out_specs=VMEM,
        compiler_params=pltpu.CompilerParams(vmem_limit_bytes=KERNEL_BYTES),
        name="by_role",
    )(bounds, full_part, short_part)


BLOCKS = 4


def put_unit(unit, first, second):
    rows = first.shape[0]
    unit[:rows, :] = norm_rows(first[...])[0].astype(jnp.bfloat16)
    unit[rows:, :] = norm_rows(second[...])[0].astype(jnp.bfloat16)


def lane_block(j, core, lanes):
    return pl.ds(pl.multiple_of((2 * j + core) * lanes, lanes), lanes)


def core_columns(place, unit, w_in, unit_part, value):
    lanes = unit.shape[1] // (2 * BLOCKS)
    for j in range(BLOCKS):
        block = lane_block(j, place.core, lanes)
        where = pl.ds(j * lanes, lanes)
        unit_part[:, where] = unit[:, block]
        value[:, where] = jnp.dot(
            unit[...], w_in[place.slot, :, block], preferred_element_type=jnp.float32
        ).astype(jnp.bfloat16)


def early_kernel(bounds, e1, e2, f1, f2, w_in, w_out, early_part, unit_part, value, unit):
    place = Place(bounds)
    part = unit_part.shape[1]

    @pl.when(jnp.logical_not(place.short))
    def _():
        put_unit(unit, e2, f2)
        core_columns(place, unit, w_in, unit_part, value)
        put_unit(unit, e1, f1)
        core_columns(place, unit, w_in, early_part.at[:, :part], early_part.at[:, part:])

    @pl.when(place.short)
    def _():
        put_unit(unit, e1, f1)
        core_columns(place, unit, w_in, unit_part, value)
        both = jnp.concatenate([e2[...], f2[...]], axis=0)
        early_part[...] = nt_dot(both, w_out[place.slot]).astype(jnp.bfloat16)


def early_factors(bounds, own, partner, w_in, w_out):
    rows, model = own[0].shape
    inner = w_in.shape[2]
    part = model // 2
    return pl.pallas_call(
        early_kernel,
        out_shape=(
            jax.ShapeDtypeStruct((2 * rows, model), jnp.bfloat16),
            jax.ShapeDtypeStruct((2 * rows, part), jnp.bfloat16),
            jax.ShapeDtypeStruct((2 * rows, part), jnp.bfloat16),
        ),
        in_specs=[SMEM] + [VMEM] * 6,
        out_specs=(VMEM,) * 3,
        scratch_shapes=[pltpu.VMEM((2 * rows, model), jnp.bfloat16)],
        compiler_params=pltpu.CompilerParams(vmem_limit_bytes=KERNEL_BYTES),
        cost_estimate=pl.CostEstimate(
            flops=4 * rows * model * inner, bytes_accessed=3 * model * inner, transcendentals=0
        ),
        name="early",
    )(bounds, *own, *partner, w_in, w_out)


def middle_kernel(bounds, e3, f3, unit_part, value, w_out, in_acc, out_acc):
    place = Place(bounds)
    grads = jnp.concatenate([e3[...], f3[...]], axis=0)
    err = nt_dot(grads, w_out[place.slot]).astype(jnp.bfloat16)
    in_acc[...] = tn_dot(unit_part[...], err)
    out_acc[...] = tn_dot(value[...], grads)


def middle_partials(bounds, e3, f3, unit_part, value, w_out):
    rows, model = e3.shape
    inner = w_out.shape[1]
    part = unit_part.shape[1]
    return pl.pallas_call(
        middle_kernel,
        out_shape=(
            jax.ShapeDtypeStruct((part, inner), jnp.float32),
            jax.ShapeDtypeStruct((part, model), jnp.float32),
        ),
        in_specs=[SMEM] + [VMEM] * 5,
        out_specs=(VMEM,) * 2,
        compiler_params=pltpu.CompilerParams(vmem_limit_bytes=KERNEL_BYTES),
        cost_estimate=pl.CostEstimate(
            flops=8 * rows * model * inner, bytes_accessed=3 * model * inner, transcendentals=0
        ),
        name="middle",
    )(bounds, e3, f3, unit_part, value, w_out)


def late_kernel(
    bounds, late, flate, e2, f2, early_part, in_acc, out_acc, w_in, w_out,
    in_send, in_keep, out_send, out_keep,
    unit, unit_part, value, grads, err,
):
    place = Place(bounds)
    half, column = place.half, place.column
    rows = late.shape[0]
    part = unit_part.shape[1]

    @pl.when(jnp.logical_not(place.short))
    def _():
        grads[:rows, :] = late[...]
        grads[rows:, :] = flate[...]
        err[...] = nt_dot(grads[...], w_out[place.slot]).astype(jnp.bfloat16)
        unit_part[...] = early_part[:, :part]
        value[...] = early_part[:, part:]

    @pl.when(place.short)
    def _():
        put_unit(unit, late, flate)
        core_columns(place, unit, w_in, unit_part, value)
        grads[:rows, :] = e2[...]
        grads[rows:, :] = f2[...]
        err[...] = early_part[...]

    half_cols = err.shape[1] // 2
    mine = pl.ds(pl.multiple_of(column * half_cols, half_cols), half_cols)
    other = pl.ds(pl.multiple_of((1 - column) * half_cols, half_cols), half_cols)
    in_send[...] = (in_acc[:, other] + tn_dot(unit_part[...], err[:, other])).astype(jnp.bfloat16)
    in_keep[...] = in_acc[:, mine] + tn_dot(unit_part[...], err[:, mine])
    half_rows = part // 2
    upper = pl.ds(pl.multiple_of(half * half_rows, half_rows), half_rows)
    lower = pl.ds(pl.multiple_of((1 - half) * half_rows, half_rows), half_rows)
    out_send[...] = (out_acc[lower, :] + tn_dot(value[:, lower], grads[...])).astype(jnp.bfloat16)
    out_keep[...] = out_acc[upper, :] + tn_dot(value[:, upper], grads[...])


def late_partials(bounds, late, other_late, own_top, other_top, early_part, accs, w_in, w_out):
    rows, model = late.shape
    inner = w_out.shape[1]
    part = model // 2
    return pl.pallas_call(
        late_kernel,
        out_shape=(
            jax.ShapeDtypeStruct((part, inner // 2), jnp.bfloat16),
            jax.ShapeDtypeStruct((part, inner // 2), jnp.float32),
            jax.ShapeDtypeStruct((part // 2, model), jnp.bfloat16),
            jax.ShapeDtypeStruct((part // 2, model), jnp.float32),
        ),
        in_specs=[SMEM] + [VMEM] * 9,
        out_specs=(VMEM,) * 4,
        scratch_shapes=[
            pltpu.VMEM((2 * rows, model), jnp.bfloat16),
            pltpu.VMEM((2 * rows, part), jnp.bfloat16),
            pltpu.VMEM((2 * rows, part), jnp.bfloat16),
            pltpu.VMEM((2 * rows, model), jnp.bfloat16),
            pltpu.VMEM((2 * rows, inner), jnp.bfloat16),
        ],
        compiler_params=pltpu.CompilerParams(vmem_limit_bytes=KERNEL_BYTES),
        cost_estimate=pl.CostEstimate(
            flops=8 * rows * model * inner, bytes_accessed=3 * model * inner, transcendentals=0
        ),
        name="late",
    )(bounds, late, other_late, own_top, other_top, early_part, *accs, w_in, w_out)


def flipped(value, axis, bit):
    return lax.ppermute(value, axis, [(i, i ^ bit) for i in range(lax.axis_size(axis))])


def two_section_body(bounds, saved_inputs, w_in, w_out, top_grad):
    pipe_index = lax.axis_index("pipe")
    section_index = lax.axis_index("section")
    column = lax.axis_index("tensor")
    relay = pipe_index // 2
    half = section_index % 2
    left = section_index // 2 == 0
    boundary = lax.dynamic_index_in_dim(bounds, relay, 0, keepdims=False)
    short = boundary[1] - boundary[0] == 2
    saved = saved_inputs[0, 0]
    proj_in = w_in[0, 0]
    proj_out = w_out[0, 0]
    tops = top_grad[0]
    model = saved.shape[2]
    inner = proj_in.shape[2]

    def across(value):
        return flipped(value, "pipe", 2)

    def core_swap(value):
        return flipped(value, "pipe", 1)

    def half_swap(value):
        return flipped(value, "section", 1)

    def column_swap(value):
        return flipped(value, "tensor", 1)

    def section_swap(value):
        return flipped(value, "section", 2)

    own_saved, own_top, given = staged(bounds, saved, tops)
    swapped = across(given)
    grad_low = chain(bounds, tops, saved, proj_in, proj_out)
    hopping = by_role(bounds, grad_low, swapped)
    late = section_swap(hopping)
    grad_other = across(grad_low)
    own = (own_saved, swapped)
    partner = tuple(core_swap(part) for part in own)
    early_part, unit_part, value = early_factors(bounds, own, partner, proj_in, proj_out)
    grad_early = by_role(bounds, grad_other, own_top)
    accs = middle_partials(bounds, grad_early, core_swap(grad_early), unit_part, value, proj_out)
    other_late = core_swap(late)
    in_send, in_keep, out_send, out_keep = late_partials(
        bounds, late, other_late, own[1], partner[1], early_part, accs, proj_in, proj_out
    )
    in_landed = column_swap(in_send)
    out_landed = half_swap(out_send)
    in_sum = (in_keep + in_landed.astype(jnp.float32)).reshape(2, -1, inner // 2)
    out_sum = out_keep + out_landed.astype(jnp.float32)
    in_mine = lax.dynamic_index_in_dim(in_sum, half, 0, keepdims=False)
    in_next = lax.dynamic_index_in_dim(in_sum, 1 - half, 0, keepdims=False)
    out_mine = lax.dynamic_slice_in_dim(out_sum, column * (model // 2), model // 2, 1)
    out_next = lax.dynamic_slice_in_dim(out_sum, (1 - column) * (model // 2), model // 2, 1)
    in_landed = half_swap(in_next.astype(jnp.bfloat16))
    out_landed = column_swap(out_next.astype(jnp.bfloat16))
    results = []
    for mine, landed in ((in_mine, in_landed), (out_mine, out_landed)):
        total = (mine + landed.astype(jnp.float32)).reshape(2, -1, mine.shape[1])
        own = lax.dynamic_index_in_dim(total, relay, 0, keepdims=False)
        sent = lax.dynamic_index_in_dim(total, 1 - relay, 0, keepdims=False).astype(jnp.bfloat16)
        got = across(sent)
        onward = section_swap(jnp.where(short, got, own.astype(jnp.bfloat16)))
        lower = jnp.where(short, own, got.astype(jnp.float32))
        results.append(jnp.where(left, lower, onward.astype(jnp.float32))[None])
    return tuple(results)


def body(bounds, saved_inputs, w_in, w_out, top_grad):
    two_sections = lax.axis_size("section") == 4 and lax.axis_size("pipe") == 4
    if two_sections and lax.axis_size("tensor") == 2:
        return two_section_body(bounds, saved_inputs, w_in, w_out, top_grad)
    return general_body(bounds, saved_inputs, w_in, w_out, top_grad)


def solution(mesh):
    placed = (
        P(),
        P("pipe", "section", None, "tensor", None),
        P("pipe", "section", None, None, None),
        P("pipe", "section", None, None, None),
        P("pipe", None, "tensor", None),
    )
    return jax.shard_map(
        body,
        mesh=mesh,
        in_specs=placed,
        out_specs=(P("section", "pipe", "tensor"), P("section", "pipe", "tensor")),
        check_vma=False,
    )
```

```python
import functools

import jax
import jax.numpy as jnp
from jax import lax
from jax.experimental import pallas as pl
from jax.experimental.pallas import tpu as pltpu
from jax.sharding import PartitionSpec as P

EPS = 1e-05


def shifted(value, axis, steps):
    count = lax.axis_size(axis)
    pairs = [(source, (source + steps) % count) for source in range(count)]
    return lax.ppermute(value, axis, pairs)


def for_sending(shard):

    def short(part):
        return part.astype(jnp.bfloat16) if part.dtype == jnp.float32 else part

    return jax.tree.map(short, shard)


def partner(block, axis, bit):
    count = lax.axis_size(axis)
    route = []
    for low in range(count):
        high = low | 1 << bit
        if high != low and high < count:
            route += [(low, high), (high, low)]
    return lax.ppermute(block, axis, route)


def normalize(saved_rows):
    floats = saved_rows.astype(jnp.float32)
    row_scale = jnp.sqrt(jnp.mean(floats * floats, axis=-1, keepdims=True) + EPS)
    return (floats / row_scale, row_scale)


def layer_back(grad_next, unit_rows, row_scale, proj_in, proj_out):
    err_low = jnp.dot(grad_next, proj_out.T, preferred_element_type=jnp.float32).astype(
        jnp.bfloat16
    )
    pulled = jnp.dot(err_low, proj_in.T, preferred_element_type=jnp.float32)
    inner_mean = jnp.mean(pulled * unit_rows, axis=-1, keepdims=True)
    grad_here = (
        grad_next.astype(jnp.float32) + (pulled - unit_rows * inner_mean) / row_scale
    ).astype(jnp.bfloat16)
    return (grad_here, err_low)


def route_items(members, shifter, offset, occupied, positions, here_section, levels, sections):
    for bit_level in reversed(range(levels)):
        stride = 2**bit_level
        passed = offset // (2 * stride) * (2 * stride)
        present = occupied & ((positions[:, None] + passed) % sections == here_section)
        rising = offset // stride % 2 == 1
        send_mask = jnp.any(present & rising, axis=0)
        keep_mask = jnp.any(present & jnp.logical_not(rising), axis=0)
        outgoing = tuple(
            (
                jnp.where(send_mask[:, None, None], member, jnp.zeros_like(member))
                for member in members
            )
        )
        arrived = shifter(outgoing, stride)
        members = tuple(
            (
                jnp.where(keep_mask[:, None, None], member, jnp.zeros_like(member)) + landed
                for member, landed in zip(members, arrived)
            )
        )
    return members


def general_body(bounds, saved_inputs, w_in, w_out, top_grad):
    sections = lax.axis_size("section") // 2
    tensors = lax.axis_size("tensor")
    pipe_index = lax.axis_index("pipe")
    section_index = lax.axis_index("section")
    tensor_index = lax.axis_index("tensor")
    position = section_index // 2
    token_half = section_index % 2
    boundary = lax.dynamic_index_in_dim(bounds, pipe_index // 2, 0, keepdims=False)
    counts = boundary[1:] - boundary[:-1]
    layers_here = lax.dynamic_index_in_dim(counts, position, 0, keepdims=False)
    saved_rows = saved_inputs[0, 0]
    proj_in = w_in[0, 0]
    proj_out = w_out[0, 0]
    slot_count = saved_rows.shape[0]
    row_count = saved_rows.shape[1]
    model_width = saved_rows.shape[2]
    inner_width = proj_in.shape[2]
    unit_rows, scales = normalize(saved_rows)
    unit_low = unit_rows.astype(jnp.bfloat16)
    value_low = jnp.einsum(
        "kre,kea->kra", unit_low, proj_in, preferred_element_type=jnp.float32
    ).astype(jnp.bfloat16)
    positions = jnp.arange(sections, dtype=jnp.int32)
    slot_ids = jnp.arange(slot_count, dtype=jnp.int32)
    occupied = slot_ids[None, :] < counts[:, None]
    layer_of = boundary[:-1, None] + slot_ids[None, :]
    offset = (layer_of + 1 - positions[:, None]) % sections
    levels = min((sections - 3 * sections // 4 + 1).bit_length(), (sections - 1).bit_length())
    top_rows = lax.dynamic_index_in_dim(top_grad[0], token_half, 0, keepdims=False)

    def run_section(incoming):

        def upper_layer(grad_top):
            return layer_back(grad_top, unit_rows[1], scales[1], proj_in[1], proj_out[1])

        def lower_layer(grad_top):
            return layer_back(grad_top, unit_rows[0], scales[0], proj_in[0], proj_out[0])

        def no_layer(grad_top):
            return (grad_top, jnp.zeros((row_count, inner_width), jnp.bfloat16))

        lower_start, upper_err = lax.cond(layers_here == 2, upper_layer, no_layer, incoming)
        result, lower_err = lax.cond(layers_here >= 1, lower_layer, no_layer, lower_start)
        return (result, jnp.stack([lower_start, incoming]), jnp.stack([lower_err, upper_err]))

    def loop_turn(turn_index, carried):
        incoming = shifted(carried[0], "section", -2)
        return lax.cond(
            position == sections - 1 - turn_index,
            lambda arriving, kept: run_section(arriving),
            lambda arriving, kept: kept,
            incoming,
            carried,
        )

    start_rows = jnp.where(position == 0, top_rows, jnp.zeros_like(top_rows))
    carried = (
        start_rows,
        jnp.zeros((slot_count, row_count, model_width), jnp.bfloat16),
        jnp.zeros((slot_count, row_count, inner_width), jnp.bfloat16),
    )
    carried = lax.fori_loop(0, sections, loop_turn, carried)
    grads_slots = carried[1]
    errors = carried[2]
    unit_got, value_got, err_got, grad_got = route_items(
        (unit_low, value_low, errors, grads_slots),
        lambda members, stride: jax.tree.map(
            lambda part, own: part.astype(own.dtype),
            shifted(for_sending(members), "section", 2 * stride),
            members,
        ),
        offset,
        occupied,
        positions,
        position,
        levels,
        sections,
    )
    owner_slot = jnp.sum(
        jnp.where(occupied & ((layer_of + 1) % sections == position), slot_ids[None, :], 0)
    )
    unit_own = lax.dynamic_index_in_dim(unit_got, owner_slot, 0, keepdims=False)
    value_own = lax.dynamic_index_in_dim(value_got, owner_slot, 0, keepdims=False)
    err_own = lax.dynamic_index_in_dim(err_got, owner_slot, 0, keepdims=False)
    grad_own = lax.dynamic_index_in_dim(grad_got, owner_slot, 0, keepdims=False)
    in_cols = inner_width // tensors
    out_cols = model_width // tensors
    unit_piece = lax.all_gather(unit_own, "tensor", axis=0, tiled=True)
    value_piece = lax.all_gather(value_own, "tensor", axis=0, tiled=True)
    err_piece = lax.all_gather(err_own, "tensor", axis=0, tiled=True)
    grad_piece = lax.all_gather(grad_own, "tensor", axis=0, tiled=True)
    err_cols = lax.dynamic_slice_in_dim(err_piece, tensor_index * in_cols, in_cols, 1)
    grad_cols = lax.dynamic_slice_in_dim(grad_piece, tensor_index * out_cols, out_cols, 1)
    totals = (
        jnp.dot(unit_piece.T, err_cols, preferred_element_type=jnp.float32),
        jnp.dot(value_piece.T, grad_cols, preferred_element_type=jnp.float32),
    )
    half_model = model_width // 2
    half_inner = inner_width // 2
    mine_in = lax.dynamic_slice_in_dim(totals[0], token_half * half_model, half_model, 0)
    other_in = lax.dynamic_slice_in_dim(totals[0], (1 - token_half) * half_model, half_model, 0)
    mine_out = lax.dynamic_slice_in_dim(totals[1], token_half * half_inner, half_inner, 0)
    other_out = lax.dynamic_slice_in_dim(totals[1], (1 - token_half) * half_inner, half_inner, 0)
    landed_in, landed_out = partner((other_in, other_out), "section", 0)
    grad_in_part, grad_out_part = (
        lax.psum_scatter(mine_in + landed_in, "pipe", scatter_dimension=0, tiled=True),
        lax.psum_scatter(mine_out + landed_out, "pipe", scatter_dimension=0, tiled=True),
    )
    return (grad_in_part[None], grad_out_part[None])


VMEM = pl.BlockSpec(memory_space=pltpu.VMEM)
SMEM = pl.BlockSpec(memory_space=pltpu.SMEM)
KERNEL_BYTES = 14 * 2**20
STAGE_FLOPS = 8 * 10**9


class Place:
    def __init__(self, bounds):
        pipe = lax.axis_index("pipe")
        section = lax.axis_index("section")
        self.column = lax.axis_index("tensor")
        self.relay = pipe // 2
        self.core = pipe % 2
        self.half = section % 2
        self.left = section < 2
        self.short = (bounds[self.relay, 1] - bounds[self.relay, 0]) == 2
        self.slot = jnp.where(self.short, 1, 0)
        self.upper_slot = jnp.where(self.left, 1, 0)


def norm_rows(saved):
    floats = saved.astype(jnp.float32)
    row_scale = jnp.sqrt(jnp.mean(floats * floats, axis=-1, keepdims=True) + EPS)
    return floats / row_scale, row_scale


def nt_dot(left, right):
    return lax.dot_general(left, right, (((1,), (1,)), ((), ())), preferred_element_type=jnp.float32)


def tn_dot(left, right):
    return lax.dot_general(left, right, (((0,), (0,)), ((), ())), preferred_element_type=jnp.float32)


def chain_kernel(bounds, tops, saved, w_in, w_out, grad_out):
    place = Place(bounds)
    slot = place.upper_slot
    grad_next = tops[place.half]
    err = nt_dot(grad_next, w_out[slot]).astype(jnp.bfloat16)
    unit, row_scale = norm_rows(saved[slot])
    pulled = nt_dot(err, w_in[slot])
    inner_mean = jnp.mean(pulled * unit, axis=-1, keepdims=True)
    back = grad_next.astype(jnp.float32) + (pulled - unit * inner_mean) / row_scale
    grad_out[...] = back.astype(jnp.bfloat16)


def chain(bounds, tops, saved, w_in, w_out):
    rows, model = saved.shape[1:]
    inner = w_in.shape[2]
    return pl.pallas_call(
        chain_kernel,
        out_shape=jax.ShapeDtypeStruct((rows, model), jnp.bfloat16),
        in_specs=[SMEM] + [VMEM] * 4,
        out_specs=VMEM,
        compiler_params=pltpu.CompilerParams(vmem_limit_bytes=KERNEL_BYTES),
        cost_estimate=pl.CostEstimate(
            flops=4 * rows * model * inner, bytes_accessed=4 * model * inner, transcendentals=0
        ),
        name="chain",
    )(bounds, tops, saved, w_in, w_out)


def opening_kernel(mark):
    mark[...] = jnp.zeros_like(mark)


def opening():
    return pl.pallas_call(
        opening_kernel,
        out_shape=jax.ShapeDtypeStruct((8, 128), jnp.float32),
        out_specs=VMEM,
        compiler_params=pltpu.CompilerParams(vmem_limit_bytes=KERNEL_BYTES),
        cost_estimate=pl.CostEstimate(flops=STAGE_FLOPS, bytes_accessed=4096, transcendentals=0),
        name="opening",
    )()


def staged_kernel(bounds, mark, saved, tops, own_saved, own_top, given):
    place = Place(bounds)
    give_top = place.left & jnp.logical_not(place.short)
    own_saved[...] = saved[place.slot]
    own_top[...] = tops[place.half]

    @pl.when(give_top)
    def _():
        given[...] = tops[place.half]

    @pl.when(jnp.logical_not(give_top))
    def _():
        given[...] = saved[0]


def staged(bounds, saved, tops):
    block = jax.ShapeDtypeStruct(saved.shape[1:], saved.dtype)
    return pl.pallas_call(
        staged_kernel,
        out_shape=(block,) * 3,
        in_specs=[SMEM, VMEM, VMEM, VMEM],
        out_specs=(VMEM,) * 3,
        compiler_params=pltpu.CompilerParams(vmem_limit_bytes=KERNEL_BYTES),
        cost_estimate=pl.CostEstimate(flops=STAGE_FLOPS, bytes_accessed=8 * saved.size, transcendentals=0),
        name="staged",
    )(bounds, opening(), saved, tops)


def by_role_kernel(bounds, full_part, short_part, chosen):
    place = Place(bounds)

    @pl.when(place.short)
    def _():
        chosen[...] = short_part[...]

    @pl.when(jnp.logical_not(place.short))
    def _():
        chosen[...] = full_part[...]


def by_role(bounds, full_part, short_part):
    return pl.pallas_call(
        by_role_kernel,
        out_shape=jax.ShapeDtypeStruct(full_part.shape, full_part.dtype),
        in_specs=[SMEM, VMEM, VMEM],
        out_specs=VMEM,
        compiler_params=pltpu.CompilerParams(vmem_limit_bytes=KERNEL_BYTES),
        name="by_role",
    )(bounds, full_part, short_part)


BLOCKS = 4


def put_unit(unit, first, second):
    rows = first.shape[0]
    unit[:rows, :] = norm_rows(first[...])[0].astype(jnp.bfloat16)
    unit[rows:, :] = norm_rows(second[...])[0].astype(jnp.bfloat16)


def lane_block(j, place, lanes):
    owner = place.relay if j // 2 else 1 - place.relay
    return pl.ds(pl.multiple_of((4 * (j % 2) + 2 * owner + place.core) * lanes, lanes), lanes)


def core_columns(place, unit, w_in, unit_part, value):
    lanes = unit.shape[1] // (2 * BLOCKS)
    for j in range(BLOCKS):
        block = lane_block(j, place, lanes)
        where = pl.ds(j * lanes, lanes)
        unit_part[:, where] = unit[:, block]
        value[:, where] = jnp.dot(
            unit[...], w_in[place.slot, :, block], preferred_element_type=jnp.float32
        ).astype(jnp.bfloat16)


def early_kernel(bounds, e1, e2, f1, f2, w_in, w_out, early_part, unit_part, value, unit):
    place = Place(bounds)
    part = unit_part.shape[1]

    @pl.when(jnp.logical_not(place.short))
    def _():
        put_unit(unit, e2, f2)
        core_columns(place, unit, w_in, unit_part, value)
        put_unit(unit, e1, f1)
        core_columns(place, unit, w_in, early_part.at[:, :part], early_part.at[:, part:])

    @pl.when(place.short)
    def _():
        put_unit(unit, e1, f1)
        core_columns(place, unit, w_in, unit_part, value)
        both = jnp.concatenate([e2[...], f2[...]], axis=0)
        early_part[...] = nt_dot(both, w_out[place.slot]).astype(jnp.bfloat16)


def early_factors(bounds, own, partner, w_in, w_out):
    rows, model = own[0].shape
    inner = w_in.shape[2]
    part = model // 2
    return pl.pallas_call(
        early_kernel,
        out_shape=(
            jax.ShapeDtypeStruct((2 * rows, model), jnp.bfloat16),
            jax.ShapeDtypeStruct((2 * rows, part), jnp.bfloat16),
            jax.ShapeDtypeStruct((2 * rows, part), jnp.bfloat16),
        ),
        in_specs=[SMEM] + [VMEM] * 6,
        out_specs=(VMEM,) * 3,
        scratch_shapes=[pltpu.VMEM((2 * rows, model), jnp.bfloat16)],
        compiler_params=pltpu.CompilerParams(vmem_limit_bytes=KERNEL_BYTES),
        cost_estimate=pl.CostEstimate(
            flops=4 * rows * model * inner, bytes_accessed=3 * model * inner, transcendentals=0
        ),
        name="early",
    )(bounds, *own, *partner, w_in, w_out)


def middle_kernel(bounds, e3, f3, unit_part, value, w_out, in_acc, out_acc):
    place = Place(bounds)
    grads = jnp.concatenate([e3[...], f3[...]], axis=0)
    err = nt_dot(grads, w_out[place.slot]).astype(jnp.bfloat16)
    in_acc[...] = tn_dot(unit_part[...], err)
    out_acc[...] = tn_dot(value[...], grads)


def middle_partials(bounds, e3, f3, unit_part, value, w_out):
    rows, model = e3.shape
    inner = w_out.shape[1]
    part = unit_part.shape[1]
    return pl.pallas_call(
        middle_kernel,
        out_shape=(
            jax.ShapeDtypeStruct((part, inner), jnp.float32),
            jax.ShapeDtypeStruct((part, model), jnp.float32),
        ),
        in_specs=[SMEM] + [VMEM] * 5,
        out_specs=(VMEM,) * 2,
        compiler_params=pltpu.CompilerParams(vmem_limit_bytes=KERNEL_BYTES),
        cost_estimate=pl.CostEstimate(
            flops=8 * rows * model * inner, bytes_accessed=3 * model * inner, transcendentals=0
        ),
        name="middle",
    )(bounds, e3, f3, unit_part, value, w_out)


def late_kernel(
    bounds, late, flate, e2, f2, early_part, in_acc, out_acc, w_in, w_out, *outs
):
    far, near = outs[:4], outs[4:8]
    unit, unit_part, value, grads, err = outs[8:]
    place = Place(bounds)
    half, column = place.half, place.column
    rows = late.shape[0]
    part = unit_part.shape[1]

    @pl.when(jnp.logical_not(place.short))
    def _():
        grads[:rows, :] = late[...]
        grads[rows:, :] = flate[...]
        err[...] = nt_dot(grads[...], w_out[place.slot]).astype(jnp.bfloat16)
        unit_part[...] = early_part[:, :part]
        value[...] = early_part[:, part:]

    @pl.when(place.short)
    def _():
        put_unit(unit, late, flate)
        core_columns(place, unit, w_in, unit_part, value)
        grads[:rows, :] = e2[...]
        grads[rows:, :] = f2[...]
        err[...] = early_part[...]

    half_cols = err.shape[1] // 2
    mine = pl.ds(pl.multiple_of(column * half_cols, half_cols), half_cols)
    other = pl.ds(pl.multiple_of((1 - column) * half_cols, half_cols), half_cols)
    group = part // 2
    block = part // 4
    for k, (in_send, in_keep, out_send, out_keep) in enumerate((far, near)):
        rows_of = slice(k * group, (k + 1) * group)
        in_send[...] = (in_acc[rows_of, other] + tn_dot(unit_part[:, rows_of], err[:, other])).astype(jnp.bfloat16)
        in_keep[...] = in_acc[rows_of, mine] + tn_dot(unit_part[:, rows_of], err[:, mine])
        kept = pl.ds(pl.multiple_of(k * group + half * block, block), block)
        sent = pl.ds(pl.multiple_of(k * group + (1 - half) * block, block), block)
        out_send[...] = (out_acc[sent, :] + tn_dot(value[:, sent], grads[...])).astype(jnp.bfloat16)
        out_keep[...] = out_acc[kept, :] + tn_dot(value[:, kept], grads[...])


def late_partials(bounds, late, other_late, own_top, other_top, early_part, accs, w_in, w_out):
    rows, model = late.shape
    inner = w_out.shape[1]
    part = model // 2
    return pl.pallas_call(
        late_kernel,
        out_shape=(
            jax.ShapeDtypeStruct((part // 2, inner // 2), jnp.bfloat16),
            jax.ShapeDtypeStruct((part // 2, inner // 2), jnp.float32),
            jax.ShapeDtypeStruct((part // 4, model), jnp.bfloat16),
            jax.ShapeDtypeStruct((part // 4, model), jnp.float32),
        )
        * 2,
        in_specs=[SMEM] + [VMEM] * 9,
        out_specs=(VMEM,) * 8,
        scratch_shapes=[
            pltpu.VMEM((2 * rows, model), jnp.bfloat16),
            pltpu.VMEM((2 * rows, part), jnp.bfloat16),
            pltpu.VMEM((2 * rows, part), jnp.bfloat16),
            pltpu.VMEM((2 * rows, model), jnp.bfloat16),
            pltpu.VMEM((2 * rows, inner), jnp.bfloat16),
        ],
        compiler_params=pltpu.CompilerParams(vmem_limit_bytes=KERNEL_BYTES),
        cost_estimate=pl.CostEstimate(
            flops=8 * rows * model * inner, bytes_accessed=3 * model * inner, transcendentals=0
        ),
        name="late",
    )(bounds, late, other_late, own_top, other_top, early_part, *accs, w_in, w_out)


def first_add_kernel(bounds, in_keep, in_land, out_keep, out_land, in_mine, in_next, out_mine, out_next):
    place = Place(bounds)
    rows = in_mine.shape[0]
    cols = out_mine.shape[1]

    def row_block(which):
        return pl.ds(pl.multiple_of(which * rows, rows), rows)

    def col_block(which):
        return pl.ds(pl.multiple_of(which * cols, cols), cols)

    kept, sent = row_block(place.half), row_block(1 - place.half)
    in_mine[...] = in_keep[kept, :] + in_land[kept, :].astype(jnp.float32)
    in_next[...] = (in_keep[sent, :] + in_land[sent, :].astype(jnp.float32)).astype(jnp.bfloat16)
    kept, sent = col_block(place.column), col_block(1 - place.column)
    out_mine[...] = out_keep[:, kept] + out_land[:, kept].astype(jnp.float32)
    out_next[...] = (out_keep[:, sent] + out_land[:, sent].astype(jnp.float32)).astype(jnp.bfloat16)


def second_add_kernel(in_mine, in_land, out_mine, out_land, total):
    total[0] = (in_mine[...] + in_land[...].astype(jnp.float32)).astype(total.dtype)
    total[1] = (out_mine[...] + out_land[...].astype(jnp.float32)).astype(total.dtype)


def hand_on_kernel(bounds, near, got, in_give, out_give, lower):
    place = Place(bounds)

    @pl.when(place.short)
    def _():
        in_give[...] = got[0]
        out_give[...] = got[1]
        lower[...] = near[...]

    @pl.when(jnp.logical_not(place.short))
    def _():
        in_give[...] = near[0].astype(jnp.bfloat16)
        out_give[...] = near[1].astype(jnp.bfloat16)
        lower[...] = got[...].astype(jnp.float32)


def result_kernel(which, lower, landed, result):
    left = lax.axis_index("section") < 2

    @pl.when(left)
    def _():
        result[0] = lower[which]

    @pl.when(jnp.logical_not(left))
    def _():
        result[0] = landed[...].astype(jnp.float32)


def small_call(kernel, operands, shapes, use_bounds=True):
    return pl.pallas_call(
        kernel,
        out_shape=shapes,
        in_specs=([SMEM] if use_bounds else []) + [VMEM] * (len(operands) - use_bounds),
        out_specs=jax.tree.map(lambda _: VMEM, shapes),
        compiler_params=pltpu.CompilerParams(vmem_limit_bytes=KERNEL_BYTES),
    )(*operands)


def low_shape(*dims):
    return jax.ShapeDtypeStruct(dims, jnp.bfloat16)


def full_shape(*dims):
    return jax.ShapeDtypeStruct(dims, jnp.float32)


def flipped(value, axis, bit):
    return lax.ppermute(value, axis, [(i, i ^ bit) for i in range(lax.axis_size(axis))])


def two_section_body(bounds, saved_inputs, w_in, w_out, top_grad):
    saved = saved_inputs[0, 0]
    proj_in = w_in[0, 0]
    proj_out = w_out[0, 0]
    tops = top_grad[0]
    model = saved.shape[2]

    def across(value):
        return flipped(value, "pipe", 2)

    def core_swap(value):
        return flipped(value, "pipe", 1)

    def half_swap(value):
        return flipped(value, "section", 1)

    def column_swap(value):
        return flipped(value, "tensor", 1)

    def section_swap(value):
        return flipped(value, "section", 2)

    own_saved, own_top, given = staged(bounds, saved, tops)
    swapped = across(given)
    grad_low = chain(bounds, tops, saved, proj_in, proj_out)
    hopping = by_role(bounds, grad_low, swapped)
    late = section_swap(hopping)
    grad_other = across(grad_low)
    own = (own_saved, swapped)
    partner = tuple(core_swap(part) for part in own)
    early_part, unit_part, value = early_factors(bounds, own, partner, proj_in, proj_out)
    grad_early = by_role(bounds, grad_other, own_top)
    accs = middle_partials(bounds, grad_early, core_swap(grad_early), unit_part, value, proj_out)
    other_late = core_swap(late)
    outs = late_partials(
        bounds, late, other_late, own[1], partner[1], early_part, accs, proj_in, proj_out
    )
    groups = (outs[:4], outs[4:])
    landed = [(column_swap(in_send), half_swap(out_send)) for in_send, _, out_send, _ in groups]
    rows = model // (2 * BLOCKS)
    block = (rows, model // 2)
    totals = []
    for (_, in_keep, _, out_keep), (in_land, out_land), kind in zip(
        groups, landed, (low_shape, full_shape)
    ):
        in_mine, in_next, out_mine, out_next = small_call(
            first_add_kernel,
            (bounds, in_keep, in_land, out_keep, out_land),
            (full_shape(*block), low_shape(*block)) * 2,
        )
        in_land, out_land = half_swap(in_next), column_swap(out_next)
        totals.append(
            small_call(
                second_add_kernel,
                (in_mine, in_land, out_mine, out_land),
                kind(2, *block),
                use_bounds=False,
            )
        )
    far, near = totals
    got = across(far)
    in_give, out_give, lower = small_call(
        hand_on_kernel,
        (bounds, near, got),
        (low_shape(*block), low_shape(*block), full_shape(2, *block)),
    )
    return tuple(
        small_call(
            functools.partial(result_kernel, which),
            (lower, section_swap(give)),
            full_shape(1, *block),
            use_bounds=False,
        )
        for which, give in enumerate((in_give, out_give))
    )


def body(bounds, saved_inputs, w_in, w_out, top_grad):
    two_sections = lax.axis_size("section") == 4 and lax.axis_size("pipe") == 4
    if two_sections and lax.axis_size("tensor") == 2:
        return two_section_body(bounds, saved_inputs, w_in, w_out, top_grad)
    return general_body(bounds, saved_inputs, w_in, w_out, top_grad)


def solution(mesh):
    placed = (
        P(),
        P("pipe", "section", None, "tensor", None),
        P("pipe", "section", None, None, None),
        P("pipe", "section", None, None, None),
        P("pipe", None, "tensor", None),
    )
    return jax.shard_map(
        body,
        mesh=mesh,
        in_specs=placed,
        out_specs=(P("section", "pipe", "tensor"), P("section", "pipe", "tensor")),
        check_vma=False,
    )
```

```python
import jax
import jax.numpy as jnp
from jax import lax
from jax.experimental import pallas as pl
from jax.experimental.pallas import tpu as pltpu
from jax.sharding import PartitionSpec as P

EPS = 1e-05


def shifted(value, axis, steps):
    count = lax.axis_size(axis)
    pairs = [(source, (source + steps) % count) for source in range(count)]
    return lax.ppermute(value, axis, pairs)


def for_sending(shard):

    def short(part):
        return part.astype(jnp.bfloat16) if part.dtype == jnp.float32 else part

    return jax.tree.map(short, shard)


def partner(block, axis, bit):
    count = lax.axis_size(axis)
    route = []
    for low in range(count):
        high = low | 1 << bit
        if high != low and high < count:
            route += [(low, high), (high, low)]
    return lax.ppermute(block, axis, route)


def normalize(saved_rows):
    floats = saved_rows.astype(jnp.float32)
    row_scale = jnp.sqrt(jnp.mean(floats * floats, axis=-1, keepdims=True) + EPS)
    return (floats / row_scale, row_scale)


def layer_back(grad_next, unit_rows, row_scale, proj_in, proj_out):
    err_low = jnp.dot(grad_next, proj_out.T, preferred_element_type=jnp.float32).astype(
        jnp.bfloat16
    )
    pulled = jnp.dot(err_low, proj_in.T, preferred_element_type=jnp.float32)
    inner_mean = jnp.mean(pulled * unit_rows, axis=-1, keepdims=True)
    grad_here = (
        grad_next.astype(jnp.float32) + (pulled - unit_rows * inner_mean) / row_scale
    ).astype(jnp.bfloat16)
    return (grad_here, err_low)


def route_items(members, shifter, offset, occupied, positions, here_section, levels, sections):
    for bit_level in reversed(range(levels)):
        stride = 2**bit_level
        passed = offset // (2 * stride) * (2 * stride)
        present = occupied & ((positions[:, None] + passed) % sections == here_section)
        rising = offset // stride % 2 == 1
        send_mask = jnp.any(present & rising, axis=0)
        keep_mask = jnp.any(present & jnp.logical_not(rising), axis=0)
        outgoing = tuple(
            (
                jnp.where(send_mask[:, None, None], member, jnp.zeros_like(member))
                for member in members
            )
        )
        arrived = shifter(outgoing, stride)
        members = tuple(
            (
                jnp.where(keep_mask[:, None, None], member, jnp.zeros_like(member)) + landed
                for member, landed in zip(members, arrived)
            )
        )
    return members


def general_body(bounds, saved_inputs, w_in, w_out, top_grad):
    sections = lax.axis_size("section") // 2
    tensors = lax.axis_size("tensor")
    pipe_index = lax.axis_index("pipe")
    section_index = lax.axis_index("section")
    tensor_index = lax.axis_index("tensor")
    position = section_index // 2
    token_half = section_index % 2
    boundary = lax.dynamic_index_in_dim(bounds, pipe_index // 2, 0, keepdims=False)
    counts = boundary[1:] - boundary[:-1]
    layers_here = lax.dynamic_index_in_dim(counts, position, 0, keepdims=False)
    saved_rows = saved_inputs[0, 0]
    proj_in = w_in[0, 0]
    proj_out = w_out[0, 0]
    slot_count = saved_rows.shape[0]
    row_count = saved_rows.shape[1]
    model_width = saved_rows.shape[2]
    inner_width = proj_in.shape[2]
    unit_rows, scales = normalize(saved_rows)
    unit_low = unit_rows.astype(jnp.bfloat16)
    value_low = jnp.einsum(
        "kre,kea->kra", unit_low, proj_in, preferred_element_type=jnp.float32
    ).astype(jnp.bfloat16)
    positions = jnp.arange(sections, dtype=jnp.int32)
    slot_ids = jnp.arange(slot_count, dtype=jnp.int32)
    occupied = slot_ids[None, :] < counts[:, None]
    layer_of = boundary[:-1, None] + slot_ids[None, :]
    offset = (layer_of + 1 - positions[:, None]) % sections
    levels = min((sections - 3 * sections // 4 + 1).bit_length(), (sections - 1).bit_length())
    top_rows = lax.dynamic_index_in_dim(top_grad[0], token_half, 0, keepdims=False)

    def run_section(incoming):

        def upper_layer(grad_top):
            return layer_back(grad_top, unit_rows[1], scales[1], proj_in[1], proj_out[1])

        def lower_layer(grad_top):
            return layer_back(grad_top, unit_rows[0], scales[0], proj_in[0], proj_out[0])

        def no_layer(grad_top):
            return (grad_top, jnp.zeros((row_count, inner_width), jnp.bfloat16))

        lower_start, upper_err = lax.cond(layers_here == 2, upper_layer, no_layer, incoming)
        result, lower_err = lax.cond(layers_here >= 1, lower_layer, no_layer, lower_start)
        return (result, jnp.stack([lower_start, incoming]), jnp.stack([lower_err, upper_err]))

    def loop_turn(turn_index, carried):
        incoming = shifted(carried[0], "section", -2)
        return lax.cond(
            position == sections - 1 - turn_index,
            lambda arriving, kept: run_section(arriving),
            lambda arriving, kept: kept,
            incoming,
            carried,
        )

    start_rows = jnp.where(position == 0, top_rows, jnp.zeros_like(top_rows))
    carried = (
        start_rows,
        jnp.zeros((slot_count, row_count, model_width), jnp.bfloat16),
        jnp.zeros((slot_count, row_count, inner_width), jnp.bfloat16),
    )
    carried = lax.fori_loop(0, sections, loop_turn, carried)
    grads_slots = carried[1]
    errors = carried[2]
    unit_got, value_got, err_got, grad_got = route_items(
        (unit_low, value_low, errors, grads_slots),
        lambda members, stride: jax.tree.map(
            lambda part, own: part.astype(own.dtype),
            shifted(for_sending(members), "section", 2 * stride),
            members,
        ),
        offset,
        occupied,
        positions,
        position,
        levels,
        sections,
    )
    owner_slot = jnp.sum(
        jnp.where(occupied & ((layer_of + 1) % sections == position), slot_ids[None, :], 0)
    )
    unit_own = lax.dynamic_index_in_dim(unit_got, owner_slot, 0, keepdims=False)
    value_own = lax.dynamic_index_in_dim(value_got, owner_slot, 0, keepdims=False)
    err_own = lax.dynamic_index_in_dim(err_got, owner_slot, 0, keepdims=False)
    grad_own = lax.dynamic_index_in_dim(grad_got, owner_slot, 0, keepdims=False)
    in_cols = inner_width // tensors
    out_cols = model_width // tensors
    unit_piece = lax.all_gather(unit_own, "tensor", axis=0, tiled=True)
    value_piece = lax.all_gather(value_own, "tensor", axis=0, tiled=True)
    err_piece = lax.all_gather(err_own, "tensor", axis=0, tiled=True)
    grad_piece = lax.all_gather(grad_own, "tensor", axis=0, tiled=True)
    err_cols = lax.dynamic_slice_in_dim(err_piece, tensor_index * in_cols, in_cols, 1)
    grad_cols = lax.dynamic_slice_in_dim(grad_piece, tensor_index * out_cols, out_cols, 1)
    totals = (
        jnp.dot(unit_piece.T, err_cols, preferred_element_type=jnp.float32),
        jnp.dot(value_piece.T, grad_cols, preferred_element_type=jnp.float32),
    )
    half_model = model_width // 2
    half_inner = inner_width // 2
    mine_in = lax.dynamic_slice_in_dim(totals[0], token_half * half_model, half_model, 0)
    other_in = lax.dynamic_slice_in_dim(totals[0], (1 - token_half) * half_model, half_model, 0)
    mine_out = lax.dynamic_slice_in_dim(totals[1], token_half * half_inner, half_inner, 0)
    other_out = lax.dynamic_slice_in_dim(totals[1], (1 - token_half) * half_inner, half_inner, 0)
    landed_in, landed_out = partner((other_in, other_out), "section", 0)
    grad_in_part, grad_out_part = (
        lax.psum_scatter(mine_in + landed_in, "pipe", scatter_dimension=0, tiled=True),
        lax.psum_scatter(mine_out + landed_out, "pipe", scatter_dimension=0, tiled=True),
    )
    return (grad_in_part[None], grad_out_part[None])


VMEM = pl.BlockSpec(memory_space=pltpu.VMEM)
SMEM = pl.BlockSpec(memory_space=pltpu.SMEM)
KERNEL_BYTES = 14 * 2**20
STAGE_FLOPS = 8 * 10**9


class Place:
    def __init__(self, bounds):
        pipe = lax.axis_index("pipe")
        section = lax.axis_index("section")
        self.column = lax.axis_index("tensor")
        self.relay = pipe // 2
        self.core = pipe % 2
        self.half = section % 2
        self.left = section < 2
        self.short = (bounds[self.relay, 1] - bounds[self.relay, 0]) == 2
        self.slot = jnp.where(self.short, 1, 0)
        self.upper_slot = jnp.where(self.left, 1, 0)


def norm_rows(saved):
    floats = saved.astype(jnp.float32)
    row_scale = jnp.sqrt(jnp.mean(floats * floats, axis=-1, keepdims=True) + EPS)
    return floats / row_scale, row_scale


def nt_dot(left, right):
    return lax.dot_general(left, right, (((1,), (1,)), ((), ())), preferred_element_type=jnp.float32)


def tn_dot(left, right):
    return lax.dot_general(left, right, (((0,), (0,)), ((), ())), preferred_element_type=jnp.float32)


def chain_kernel(bounds, tops, saved, w_in, w_out, grad_out):
    place = Place(bounds)
    slot = place.upper_slot
    grad_next = tops[place.half]
    err = nt_dot(grad_next, w_out[slot]).astype(jnp.bfloat16)
    unit, row_scale = norm_rows(saved[slot])
    pulled = nt_dot(err, w_in[slot])
    inner_mean = jnp.mean(pulled * unit, axis=-1, keepdims=True)
    back = grad_next.astype(jnp.float32) + (pulled - unit * inner_mean) / row_scale
    grad_out[...] = back.astype(jnp.bfloat16)


def chain(bounds, tops, saved, w_in, w_out):
    rows, model = saved.shape[1:]
    inner = w_in.shape[2]
    return pl.pallas_call(
        chain_kernel,
        out_shape=jax.ShapeDtypeStruct((rows, model), jnp.bfloat16),
        in_specs=[SMEM] + [VMEM] * 4,
        out_specs=VMEM,
        compiler_params=pltpu.CompilerParams(vmem_limit_bytes=KERNEL_BYTES),
        cost_estimate=pl.CostEstimate(
            flops=4 * rows * model * inner, bytes_accessed=4 * model * inner, transcendentals=0
        ),
        name="chain",
    )(bounds, tops, saved, w_in, w_out)


def opening_kernel(mark):
    mark[...] = jnp.zeros_like(mark)


def opening():
    return pl.pallas_call(
        opening_kernel,
        out_shape=jax.ShapeDtypeStruct((8, 128), jnp.float32),
        out_specs=VMEM,
        compiler_params=pltpu.CompilerParams(vmem_limit_bytes=KERNEL_BYTES),
        cost_estimate=pl.CostEstimate(flops=STAGE_FLOPS, bytes_accessed=4096, transcendentals=0),
        name="opening",
    )()


def staged_kernel(bounds, mark, saved, tops, own_saved, own_top, given):
    place = Place(bounds)
    give_top = place.left & jnp.logical_not(place.short)
    own_saved[...] = saved[place.slot]
    own_top[...] = tops[place.half]

    @pl.when(give_top)
    def _():
        given[...] = tops[place.half]

    @pl.when(jnp.logical_not(give_top))
    def _():
        given[...] = saved[0]


def staged(bounds, saved, tops):
    block = jax.ShapeDtypeStruct(saved.shape[1:], saved.dtype)
    return pl.pallas_call(
        staged_kernel,
        out_shape=(block,) * 3,
        in_specs=[SMEM, VMEM, VMEM, VMEM],
        out_specs=(VMEM,) * 3,
        compiler_params=pltpu.CompilerParams(vmem_limit_bytes=KERNEL_BYTES),
        cost_estimate=pl.CostEstimate(flops=STAGE_FLOPS, bytes_accessed=8 * saved.size, transcendentals=0),
        name="staged",
    )(bounds, opening(), saved, tops)


def by_role_kernel(bounds, full_part, short_part, chosen):
    place = Place(bounds)

    @pl.when(place.short)
    def _():
        chosen[...] = short_part[...]

    @pl.when(jnp.logical_not(place.short))
    def _():
        chosen[...] = full_part[...]


def by_role(bounds, full_part, short_part):
    return pl.pallas_call(
        by_role_kernel,
        out_shape=jax.ShapeDtypeStruct(full_part.shape, full_part.dtype),
        in_specs=[SMEM, VMEM, VMEM],
        out_specs=VMEM,
        compiler_params=pltpu.CompilerParams(vmem_limit_bytes=KERNEL_BYTES),
        name="by_role",
    )(bounds, full_part, short_part)


def value_kernel(saved, w_in, value):
    unit = norm_rows(saved[0])[0].astype(jnp.bfloat16)
    value[...] = jnp.dot(unit, w_in[0], preferred_element_type=jnp.float32).astype(jnp.bfloat16)


BLOCKS = 4


def put_unit(unit, first, second):
    rows = first.shape[0]
    unit[:rows, :] = norm_rows(first[...])[0].astype(jnp.bfloat16)
    unit[rows:, :] = norm_rows(second[...])[0].astype(jnp.bfloat16)


def lane_block(j, place, lanes):
    owner = place.relay if j // 2 else 1 - place.relay
    return pl.ds(pl.multiple_of((4 * (j % 2) + 2 * owner + place.core) * lanes, lanes), lanes)


def unit_columns(place, unit, unit_part):
    lanes = unit.shape[1] // (2 * BLOCKS)
    for j in range(BLOCKS):
        unit_part[:, j * lanes : (j + 1) * lanes] = unit[:, lane_block(j, place, lanes)]


def core_columns(place, unit, w_in, unit_part, value):
    lanes = unit.shape[1] // (2 * BLOCKS)
    for j in range(BLOCKS):
        block = lane_block(j, place, lanes)
        where = pl.ds(j * lanes, lanes)
        unit_part[:, where] = unit[:, block]
        value[:, where] = jnp.dot(
            unit[...], w_in[place.slot, :, block], preferred_element_type=jnp.float32
        ).astype(jnp.bfloat16)


def early_kernel(bounds, e1, e2, f1, f2, w_in, w_out, early_part, unit_part, value, unit):
    place = Place(bounds)

    @pl.when(jnp.logical_not(place.short))
    def _():
        put_unit(unit, e2, f2)
        unit_columns(place, unit, unit_part)
        value[...] = jnp.zeros_like(value)
        put_unit(unit, e1, f1)
        unit_columns(place, unit, early_part)

    @pl.when(place.short)
    def _():
        put_unit(unit, e1, f1)
        core_columns(place, unit, w_in, unit_part, value)
        both = jnp.concatenate([e2[...], f2[...]], axis=0)
        early_part[...] = nt_dot(both, w_out[place.slot]).astype(jnp.bfloat16)


def early_factors(bounds, own, partner, w_in, w_out):
    rows, model = own[0].shape
    inner = w_in.shape[2]
    part = model // 2
    return pl.pallas_call(
        early_kernel,
        out_shape=(
            jax.ShapeDtypeStruct((2 * rows, model), jnp.bfloat16),
            jax.ShapeDtypeStruct((2 * rows, part), jnp.bfloat16),
            jax.ShapeDtypeStruct((2 * rows, part), jnp.bfloat16),
        ),
        in_specs=[SMEM] + [VMEM] * 6,
        out_specs=(VMEM,) * 3,
        scratch_shapes=[pltpu.VMEM((2 * rows, model), jnp.bfloat16)],
        compiler_params=pltpu.CompilerParams(vmem_limit_bytes=KERNEL_BYTES),
        cost_estimate=pl.CostEstimate(
            flops=4 * rows * model * inner, bytes_accessed=3 * model * inner, transcendentals=0
        ),
        name="early",
    )(bounds, *own, *partner, w_in, w_out)


def middle_kernel(bounds, e3, f3, unit_part, value, w_out, in_acc, out_acc):
    place = Place(bounds)
    grads = jnp.concatenate([e3[...], f3[...]], axis=0)
    err = nt_dot(grads, w_out[place.slot]).astype(jnp.bfloat16)
    in_acc[...] = tn_dot(unit_part[...], err)
    out_acc[...] = tn_dot(value[...], grads)


def middle_partials(bounds, e3, f3, unit_part, value, w_out):
    rows, model = e3.shape
    inner = w_out.shape[1]
    part = unit_part.shape[1]
    return pl.pallas_call(
        middle_kernel,
        out_shape=(
            jax.ShapeDtypeStruct((part, inner), jnp.float32),
            jax.ShapeDtypeStruct((part, model), jnp.float32),
        ),
        in_specs=[SMEM] + [VMEM] * 5,
        out_specs=(VMEM,) * 2,
        compiler_params=pltpu.CompilerParams(vmem_limit_bytes=KERNEL_BYTES),
        cost_estimate=pl.CostEstimate(
            flops=8 * rows * model * inner, bytes_accessed=3 * model * inner, transcendentals=0
        ),
        name="middle",
    )(bounds, e3, f3, unit_part, value, w_out)


def split_sums(place, left_part, right_part, acc, x_send, x_keep, z_send, z_keep):
    group = left_part.shape[1] // 2
    block = group // 2
    cols = right_part.shape[1] // 2

    def sums(rows_of, cols_of):
        new = tn_dot(left_part[:, rows_of], right_part[:, cols_of])
        return new if acc is None else acc[rows_of, cols_of] + new

    far = slice(0, group)
    every = slice(None)
    mine = pl.ds(pl.multiple_of(place.column * cols, cols), cols)
    other = pl.ds(pl.multiple_of((1 - place.column) * cols, cols), cols)
    kept = pl.ds(pl.multiple_of(group + place.half * block, block), block)
    sent = pl.ds(pl.multiple_of(group + (1 - place.half) * block, block), block)
    x_send[...] = sums(far, other).astype(jnp.bfloat16)
    x_keep[...] = sums(far, mine)
    z_send[...] = sums(sent, every).astype(jnp.bfloat16)
    z_keep[...] = sums(kept, every)


def late_in_kernel(
    bounds, late, flate, early_part, in_acc, w_out, x_send, x_keep, z_send, z_keep, unit, unit_part, err,
):
    place = Place(bounds)
    part = unit_part.shape[1]

    @pl.when(jnp.logical_not(place.short))
    def _():
        grads = jnp.concatenate([late[...], flate[...]], axis=0)
        err[...] = nt_dot(grads, w_out[place.slot]).astype(jnp.bfloat16)
        unit_part[...] = early_part[:, :part]

    @pl.when(place.short)
    def _():
        put_unit(unit, late, flate)
        unit_columns(place, unit, unit_part)
        err[...] = early_part[...]

    split_sums(place, unit_part, err, in_acc, x_send, x_keep, z_send, z_keep)


def late_out_kernel(
    bounds, unit, e2, f2, out_acc, w_in, late, flate, low, flow, up, fup,
    x_send, x_keep, z_send, z_keep, value, grads, unit_part,
):
    place = Place(bounds)
    rows = e2.shape[0]
    part = value.shape[1]
    lanes = part // BLOCKS
    outs = (x_send, x_keep, z_send, z_keep)

    def put_grads(first, second):
        grads[:rows, :] = first[...]
        grads[rows:, :] = second[...]

    @pl.when(place.left)
    def _():
        core_columns(place, unit, w_in, unit_part, value)
        put_grads(e2, f2)
        split_sums(place, value, grads, out_acc, *outs)

    @pl.when(jnp.logical_not(place.left))
    def _():
        for j in range(BLOCKS):
            block = lane_block(j, place, lanes)
            where = pl.ds(j * lanes, lanes)
            value[:rows, where] = up[:, block]
            value[rows:, where] = fup[:, block]

        @pl.when(place.short)
        def _():
            put_grads(late, flate)

        @pl.when(jnp.logical_not(place.short))
        def _():
            put_grads(low, flow)

        split_sums(place, value, grads, None, *outs)


def split_shapes(part, width):
    return (
        low_shape(part // 2, width // 2),
        full_shape(part // 2, width // 2),
        low_shape(part // 4, width),
        full_shape(part // 4, width),
    )


def x_add_kernel(keep, land, mine, following):
    half = lax.axis_index("section") % 2
    rows = mine.shape[0]
    kept = pl.ds(pl.multiple_of(half * rows, rows), rows)
    sent = pl.ds(pl.multiple_of((1 - half) * rows, rows), rows)
    mine[...] = keep[kept, :] + land[kept, :].astype(jnp.float32)
    following[...] = (keep[sent, :] + land[sent, :].astype(jnp.float32)).astype(jnp.bfloat16)


def z_add_kernel(keep, land, mine, following):
    column = lax.axis_index("tensor")
    cols = mine.shape[1]
    kept = pl.ds(pl.multiple_of(column * cols, cols), cols)
    sent = pl.ds(pl.multiple_of((1 - column) * cols, cols), cols)
    mine[...] = keep[:, kept] + land[:, kept].astype(jnp.float32)
    following[...] = (keep[:, sent] + land[:, sent].astype(jnp.float32)).astype(jnp.bfloat16)


def last_add_kernel(mine, land, total):
    total[...] = (mine[...] + land[...].astype(jnp.float32)).astype(total.dtype)


def hand_on_kernel(bounds, near, got, give, lower):
    place = Place(bounds)

    @pl.when(place.short)
    def _():
        give[...] = got[...]
        lower[...] = near[...]

    @pl.when(jnp.logical_not(place.short))
    def _():
        give[...] = near[...].astype(jnp.bfloat16)
        lower[...] = got[...].astype(jnp.float32)


def in_result_kernel(lower, landed, result):
    left = lax.axis_index("section") < 2

    @pl.when(left)
    def _():
        result[0] = lower[...]

    @pl.when(jnp.logical_not(left))
    def _():
        result[0] = landed[...].astype(jnp.float32)


def out_result_kernel(bounds, near, got, result):
    place = Place(bounds)
    upper = jnp.logical_not(place.left)

    @pl.when(upper)
    def _():
        result[0] = near[...] + got[...].astype(jnp.float32)

    @pl.when(place.left & place.short)
    def _():
        result[0] = near[...]

    @pl.when(place.left & jnp.logical_not(place.short))
    def _():
        result[0] = got[...].astype(jnp.float32)


def small_call(kernel, operands, shapes, scratch=(), flops=0):
    specs = [SMEM if part.ndim == 2 and part.dtype == jnp.int32 else VMEM for part in operands]
    cost = pl.CostEstimate(flops=flops, bytes_accessed=0, transcendentals=0) if flops else None
    return pl.pallas_call(
        kernel,
        out_shape=shapes,
        in_specs=specs,
        out_specs=jax.tree.map(lambda _: VMEM, shapes),
        scratch_shapes=scratch,
        compiler_params=pltpu.CompilerParams(vmem_limit_bytes=KERNEL_BYTES),
        cost_estimate=cost,
    )(*operands)


def low_shape(*dims):
    return jax.ShapeDtypeStruct(dims, jnp.bfloat16)


def full_shape(*dims):
    return jax.ShapeDtypeStruct(dims, jnp.float32)


def flipped(value, axis, bit):
    return lax.ppermute(value, axis, [(i, i ^ bit) for i in range(lax.axis_size(axis))])


def two_section_body(bounds, saved_inputs, w_in, w_out, top_grad):
    saved = saved_inputs[0, 0]
    proj_in = w_in[0, 0]
    proj_out = w_out[0, 0]
    tops = top_grad[0]
    model = saved.shape[2]
    inner = proj_in.shape[2]

    def across(value):
        return flipped(value, "pipe", 2)

    def core_swap(value):
        return flipped(value, "pipe", 1)

    def half_swap(value):
        return flipped(value, "section", 1)

    def column_swap(value):
        return flipped(value, "tensor", 1)

    half_axis = lax.axis_size("section") // 2

    def upward(value):
        return lax.ppermute(value, "section", [(i, i + half_axis) for i in range(half_axis)])

    def downward(value):
        return lax.ppermute(value, "section", [(i + half_axis, i) for i in range(half_axis)])

    def section_swap(value):
        return flipped(value, "section", 2)

    own_saved, own_top, given = staged(bounds, saved, tops)
    swapped = across(given)
    rows = saved.shape[1]
    row_block = low_shape(rows, model)
    value_low = small_call(value_kernel, (saved, proj_in), row_block, flops=2 * rows * model * inner)
    lifted = upward(value_low)
    grad_low = chain(bounds, tops, saved, proj_in, proj_out)
    hopping = by_role(bounds, grad_low, swapped)
    late = downward(hopping)
    grad_other = across(grad_low)
    raised = upward(grad_low)
    own = (own_saved, swapped)
    partner = tuple(core_swap(part) for part in own)
    early_part, unit_part, value = early_factors(bounds, own, partner, proj_in, proj_out)
    grad_early = by_role(bounds, grad_other, own_top)
    in_acc, out_acc = middle_partials(bounds, grad_early, core_swap(grad_early), unit_part, value, proj_out)
    other_low = core_swap(grad_low)
    other_lifted = core_swap(lifted)
    other_raised = core_swap(raised)
    other_late = core_swap(late)
    part = model // 2
    pair = 2 * rows
    *in_parts, unit_late = small_call(
        late_in_kernel,
        (bounds, late, other_late, early_part, in_acc, proj_out),
        split_shapes(part, inner) + (low_shape(pair, model),),
        scratch=[pltpu.VMEM((pair, part), jnp.bfloat16), pltpu.VMEM((pair, inner), jnp.bfloat16)],
        flops=6 * rows * model * inner,
    )
    out_parts = small_call(
        late_out_kernel,
        (bounds, unit_late, own[1], partner[1], out_acc, proj_in)
        + (raised, other_raised, grad_low, other_low, lifted, other_lifted),
        split_shapes(part, model),
        scratch=[
            pltpu.VMEM((pair, part), jnp.bfloat16),
            pltpu.VMEM((pair, model), jnp.bfloat16),
            pltpu.VMEM((pair, part), jnp.bfloat16),
        ],
        flops=4 * rows * model * inner,
    )
    block = (model // (2 * BLOCKS), model // 2)
    sums = []
    for (x_send, x_keep, z_send, z_keep) in (in_parts, out_parts):
        pair_shapes = (full_shape(*block), low_shape(*block))
        x_land, z_land = column_swap(x_send), half_swap(z_send)
        far, far_next = small_call(x_add_kernel, (x_keep, x_land), pair_shapes)
        near, near_next = small_call(z_add_kernel, (z_keep, z_land), pair_shapes)
        far_land, near_land = half_swap(far_next), column_swap(near_next)
        far = small_call(last_add_kernel, (far, far_land), low_shape(*block))
        got = across(far)
        near = small_call(last_add_kernel, (near, near_land), full_shape(*block))
        sums.append((near, got))
    (in_near, in_got), (out_near, out_got) = sums
    give, lower = small_call(
        hand_on_kernel, (bounds, in_near, in_got), (low_shape(*block), full_shape(*block))
    )
    landed = section_swap(give)
    return (
        small_call(in_result_kernel, (lower, landed), full_shape(1, *block)),
        small_call(out_result_kernel, (bounds, out_near, out_got), full_shape(1, *block)),
    )


def body(bounds, saved_inputs, w_in, w_out, top_grad):
    two_sections = lax.axis_size("section") == 4 and lax.axis_size("pipe") == 4
    if two_sections and lax.axis_size("tensor") == 2:
        return two_section_body(bounds, saved_inputs, w_in, w_out, top_grad)
    return general_body(bounds, saved_inputs, w_in, w_out, top_grad)


def solution(mesh):
    placed = (
        P(),
        P("pipe", "section", None, "tensor", None),
        P("pipe", "section", None, None, None),
        P("pipe", "section", None, None, None),
        P("pipe", None, "tensor", None),
    )
    return jax.shard_map(
        body,
        mesh=mesh,
        in_specs=placed,
        out_specs=(P("section", "pipe", "tensor"), P("section", "pipe", "tensor")),
        check_vma=False,
    )
```

```python
import jax
import jax.numpy as jnp
from jax import lax
from jax.experimental import pallas as pl
from jax.experimental.pallas import tpu as pltpu
from jax.sharding import PartitionSpec as P

EPS = 1e-05


def shifted(value, axis, steps):
    count = lax.axis_size(axis)
    pairs = [(source, (source + steps) % count) for source in range(count)]
    return lax.ppermute(value, axis, pairs)


def for_sending(shard):

    def short(part):
        return part.astype(jnp.bfloat16) if part.dtype == jnp.float32 else part

    return jax.tree.map(short, shard)


def partner(block, axis, bit):
    count = lax.axis_size(axis)
    route = []
    for low in range(count):
        high = low | 1 << bit
        if high != low and high < count:
            route += [(low, high), (high, low)]
    return lax.ppermute(block, axis, route)


def normalize(saved_rows):
    floats = saved_rows.astype(jnp.float32)
    row_scale = jnp.sqrt(jnp.mean(floats * floats, axis=-1, keepdims=True) + EPS)
    return (floats / row_scale, row_scale)


def layer_back(grad_next, unit_rows, row_scale, proj_in, proj_out):
    err_low = jnp.dot(grad_next, proj_out.T, preferred_element_type=jnp.float32).astype(
        jnp.bfloat16
    )
    pulled = jnp.dot(err_low, proj_in.T, preferred_element_type=jnp.float32)
    inner_mean = jnp.mean(pulled * unit_rows, axis=-1, keepdims=True)
    grad_here = (
        grad_next.astype(jnp.float32) + (pulled - unit_rows * inner_mean) / row_scale
    ).astype(jnp.bfloat16)
    return (grad_here, err_low)


def route_items(members, shifter, offset, occupied, positions, here_section, levels, sections):
    for bit_level in reversed(range(levels)):
        stride = 2**bit_level
        passed = offset // (2 * stride) * (2 * stride)
        present = occupied & ((positions[:, None] + passed) % sections == here_section)
        rising = offset // stride % 2 == 1
        send_mask = jnp.any(present & rising, axis=0)
        keep_mask = jnp.any(present & jnp.logical_not(rising), axis=0)
        outgoing = tuple(
            (
                jnp.where(send_mask[:, None, None], member, jnp.zeros_like(member))
                for member in members
            )
        )
        arrived = shifter(outgoing, stride)
        members = tuple(
            (
                jnp.where(keep_mask[:, None, None], member, jnp.zeros_like(member)) + landed
                for member, landed in zip(members, arrived)
            )
        )
    return members


def general_body(bounds, saved_inputs, w_in, w_out, top_grad):
    sections = lax.axis_size("section") // 2
    tensors = lax.axis_size("tensor")
    pipe_index = lax.axis_index("pipe")
    section_index = lax.axis_index("section")
    tensor_index = lax.axis_index("tensor")
    position = section_index // 2
    token_half = section_index % 2
    boundary = lax.dynamic_index_in_dim(bounds, pipe_index // 2, 0, keepdims=False)
    counts = boundary[1:] - boundary[:-1]
    layers_here = lax.dynamic_index_in_dim(counts, position, 0, keepdims=False)
    saved_rows = saved_inputs[0, 0]
    proj_in = w_in[0, 0]
    proj_out = w_out[0, 0]
    slot_count = saved_rows.shape[0]
    row_count = saved_rows.shape[1]
    model_width = saved_rows.shape[2]
    inner_width = proj_in.shape[2]
    unit_rows, scales = normalize(saved_rows)
    unit_low = unit_rows.astype(jnp.bfloat16)
    value_low = jnp.einsum(
        "kre,kea->kra", unit_low, proj_in, preferred_element_type=jnp.float32
    ).astype(jnp.bfloat16)
    positions = jnp.arange(sections, dtype=jnp.int32)
    slot_ids = jnp.arange(slot_count, dtype=jnp.int32)
    occupied = slot_ids[None, :] < counts[:, None]
    layer_of = boundary[:-1, None] + slot_ids[None, :]
    offset = (layer_of + 1 - positions[:, None]) % sections
    levels = min((sections - 3 * sections // 4 + 1).bit_length(), (sections - 1).bit_length())
    top_rows = lax.dynamic_index_in_dim(top_grad[0], token_half, 0, keepdims=False)

    def run_section(incoming):

        def upper_layer(grad_top):
            return layer_back(grad_top, unit_rows[1], scales[1], proj_in[1], proj_out[1])

        def lower_layer(grad_top):
            return layer_back(grad_top, unit_rows[0], scales[0], proj_in[0], proj_out[0])

        def no_layer(grad_top):
            return (grad_top, jnp.zeros((row_count, inner_width), jnp.bfloat16))

        lower_start, upper_err = lax.cond(layers_here == 2, upper_layer, no_layer, incoming)
        result, lower_err = lax.cond(layers_here >= 1, lower_layer, no_layer, lower_start)
        return (result, jnp.stack([lower_start, incoming]), jnp.stack([lower_err, upper_err]))

    def loop_turn(turn_index, carried):
        incoming = shifted(carried[0], "section", -2)
        return lax.cond(
            position == sections - 1 - turn_index,
            lambda arriving, kept: run_section(arriving),
            lambda arriving, kept: kept,
            incoming,
            carried,
        )

    start_rows = jnp.where(position == 0, top_rows, jnp.zeros_like(top_rows))
    carried = (
        start_rows,
        jnp.zeros((slot_count, row_count, model_width), jnp.bfloat16),
        jnp.zeros((slot_count, row_count, inner_width), jnp.bfloat16),
    )
    carried = lax.fori_loop(0, sections, loop_turn, carried)
    grads_slots = carried[1]
    errors = carried[2]
    unit_got, value_got, err_got, grad_got = route_items(
        (unit_low, value_low, errors, grads_slots),
        lambda members, stride: jax.tree.map(
            lambda part, own: part.astype(own.dtype),
            shifted(for_sending(members), "section", 2 * stride),
            members,
        ),
        offset,
        occupied,
        positions,
        position,
        levels,
        sections,
    )
    owner_slot = jnp.sum(
        jnp.where(occupied & ((layer_of + 1) % sections == position), slot_ids[None, :], 0)
    )
    unit_own = lax.dynamic_index_in_dim(unit_got, owner_slot, 0, keepdims=False)
    value_own = lax.dynamic_index_in_dim(value_got, owner_slot, 0, keepdims=False)
    err_own = lax.dynamic_index_in_dim(err_got, owner_slot, 0, keepdims=False)
    grad_own = lax.dynamic_index_in_dim(grad_got, owner_slot, 0, keepdims=False)
    in_cols = inner_width // tensors
    out_cols = model_width // tensors
    unit_piece = lax.all_gather(unit_own, "tensor", axis=0, tiled=True)
    value_piece = lax.all_gather(value_own, "tensor", axis=0, tiled=True)
    err_piece = lax.all_gather(err_own, "tensor", axis=0, tiled=True)
    grad_piece = lax.all_gather(grad_own, "tensor", axis=0, tiled=True)
    err_cols = lax.dynamic_slice_in_dim(err_piece, tensor_index * in_cols, in_cols, 1)
    grad_cols = lax.dynamic_slice_in_dim(grad_piece, tensor_index * out_cols, out_cols, 1)
    totals = (
        jnp.dot(unit_piece.T, err_cols, preferred_element_type=jnp.float32),
        jnp.dot(value_piece.T, grad_cols, preferred_element_type=jnp.float32),
    )
    half_model = model_width // 2
    half_inner = inner_width // 2
    mine_in = lax.dynamic_slice_in_dim(totals[0], token_half * half_model, half_model, 0)
    other_in = lax.dynamic_slice_in_dim(totals[0], (1 - token_half) * half_model, half_model, 0)
    mine_out = lax.dynamic_slice_in_dim(totals[1], token_half * half_inner, half_inner, 0)
    other_out = lax.dynamic_slice_in_dim(totals[1], (1 - token_half) * half_inner, half_inner, 0)
    landed_in, landed_out = partner((other_in, other_out), "section", 0)
    grad_in_part, grad_out_part = (
        lax.psum_scatter(mine_in + landed_in, "pipe", scatter_dimension=0, tiled=True),
        lax.psum_scatter(mine_out + landed_out, "pipe", scatter_dimension=0, tiled=True),
    )
    return (grad_in_part[None], grad_out_part[None])


VMEM = pl.BlockSpec(memory_space=pltpu.VMEM)
SMEM = pl.BlockSpec(memory_space=pltpu.SMEM)
KERNEL_BYTES = 14 * 2**20
STAGE_FLOPS = 8 * 10**9


class Place:
    def __init__(self, bounds):
        pipe = lax.axis_index("pipe")
        section = lax.axis_index("section")
        self.column = lax.axis_index("tensor")
        self.relay = pipe // 2
        self.core = pipe % 2
        self.half = section % 2
        self.left = section < 2
        self.short = (bounds[self.relay, 1] - bounds[self.relay, 0]) == 2
        self.slot = jnp.where(self.short, 1, 0)
        self.upper_slot = jnp.where(self.left, 1, 0)


def norm_rows(saved):
    floats = saved.astype(jnp.float32)
    row_scale = jnp.sqrt(jnp.mean(floats * floats, axis=-1, keepdims=True) + EPS)
    return floats / row_scale, row_scale


def nt_dot(left, right):
    return lax.dot_general(left, right, (((1,), (1,)), ((), ())), preferred_element_type=jnp.float32)


def tn_dot(left, right):
    return lax.dot_general(left, right, (((0,), (0,)), ((), ())), preferred_element_type=jnp.float32)


def chain_kernel(bounds, tops, saved, w_in, w_out, grad_out, upward):
    place = Place(bounds)
    slot = place.upper_slot
    first_unit = norm_rows(saved[0])[0].astype(jnp.bfloat16)
    upward[0] = jnp.dot(first_unit, w_in[0], preferred_element_type=jnp.float32).astype(jnp.bfloat16)
    grad_next = tops[place.half]
    err = nt_dot(grad_next, w_out[slot]).astype(jnp.bfloat16)
    unit, row_scale = norm_rows(saved[slot])
    pulled = nt_dot(err, w_in[slot])
    inner_mean = jnp.mean(pulled * unit, axis=-1, keepdims=True)
    back = grad_next.astype(jnp.float32) + (pulled - unit * inner_mean) / row_scale
    grad_low = back.astype(jnp.bfloat16)
    grad_out[...] = grad_low
    upward[1] = grad_low


def chain(bounds, tops, saved, w_in, w_out):
    rows, model = saved.shape[1:]
    inner = w_in.shape[2]
    return pl.pallas_call(
        chain_kernel,
        out_shape=(low_shape(rows, model), low_shape(2, rows, model)),
        in_specs=[SMEM] + [VMEM] * 4,
        out_specs=(VMEM,) * 2,
        compiler_params=pltpu.CompilerParams(vmem_limit_bytes=KERNEL_BYTES),
        cost_estimate=pl.CostEstimate(
            flops=6 * rows * model * inner, bytes_accessed=4 * model * inner, transcendentals=0
        ),
        name="chain",
    )(bounds, tops, saved, w_in, w_out)


def opening_kernel(mark):
    mark[...] = jnp.zeros_like(mark)


def opening():
    return pl.pallas_call(
        opening_kernel,
        out_shape=jax.ShapeDtypeStruct((8, 128), jnp.float32),
        out_specs=VMEM,
        compiler_params=pltpu.CompilerParams(vmem_limit_bytes=KERNEL_BYTES),
        cost_estimate=pl.CostEstimate(flops=STAGE_FLOPS, bytes_accessed=4096, transcendentals=0),
        name="opening",
    )()


def staged_kernel(bounds, mark, saved, tops, own_saved, own_top, given):
    place = Place(bounds)
    give_top = place.left & jnp.logical_not(place.short)
    own_saved[...] = saved[place.slot]
    own_top[...] = tops[place.half]

    @pl.when(give_top)
    def _():
        given[...] = tops[place.half]

    @pl.when(jnp.logical_not(give_top))
    def _():
        given[...] = saved[0]


def staged(bounds, saved, tops):
    block = jax.ShapeDtypeStruct(saved.shape[1:], saved.dtype)
    return pl.pallas_call(
        staged_kernel,
        out_shape=(block,) * 3,
        in_specs=[SMEM, VMEM, VMEM, VMEM],
        out_specs=(VMEM,) * 3,
        compiler_params=pltpu.CompilerParams(vmem_limit_bytes=KERNEL_BYTES),
        cost_estimate=pl.CostEstimate(flops=STAGE_FLOPS, bytes_accessed=8 * saved.size, transcendentals=0),
        name="staged",
    )(bounds, opening(), saved, tops)


def by_role_kernel(bounds, full_part, short_part, chosen):
    place = Place(bounds)

    @pl.when(place.short)
    def _():
        chosen[...] = short_part[...]

    @pl.when(jnp.logical_not(place.short))
    def _():
        chosen[...] = full_part[...]


def by_role(bounds, full_part, short_part):
    return pl.pallas_call(
        by_role_kernel,
        out_shape=jax.ShapeDtypeStruct(full_part.shape, full_part.dtype),
        in_specs=[SMEM, VMEM, VMEM],
        out_specs=VMEM,
        compiler_params=pltpu.CompilerParams(vmem_limit_bytes=KERNEL_BYTES),
        name="by_role",
    )(bounds, full_part, short_part)


BLOCKS = 4


def put_unit(unit, first, second):
    rows = first.shape[0]
    unit[:rows, :] = norm_rows(first[...])[0].astype(jnp.bfloat16)
    unit[rows:, :] = norm_rows(second[...])[0].astype(jnp.bfloat16)


def lane_block(j, place, lanes):
    owner = place.relay if j // 2 else 1 - place.relay
    return pl.ds(pl.multiple_of((4 * (j % 2) + 2 * owner + place.core) * lanes, lanes), lanes)


def unit_columns(place, unit, unit_part):
    lanes = unit.shape[1] // (2 * BLOCKS)
    for j in range(BLOCKS):
        unit_part[:, j * lanes : (j + 1) * lanes] = unit[:, lane_block(j, place, lanes)]


def core_columns(place, unit, w_in, unit_part, value):
    lanes = unit.shape[1] // (2 * BLOCKS)
    for j in range(BLOCKS):
        block = lane_block(j, place, lanes)
        where = pl.ds(j * lanes, lanes)
        unit_part[:, where] = unit[:, block]
        value[:, where] = jnp.dot(
            unit[...], w_in[place.slot, :, block], preferred_element_type=jnp.float32
        ).astype(jnp.bfloat16)


def early_kernel(bounds, e1, e2, f1, f2, w_in, w_out, early_part, unit_part, value, unit):
    place = Place(bounds)

    @pl.when(jnp.logical_not(place.short))
    def _():
        put_unit(unit, e2, f2)
        unit_columns(place, unit, unit_part)
        value[...] = jnp.zeros_like(value)
        put_unit(unit, e1, f1)
        unit_columns(place, unit, early_part)

    @pl.when(place.short)
    def _():
        put_unit(unit, e1, f1)
        core_columns(place, unit, w_in, unit_part, value)
        both = jnp.concatenate([e2[...], f2[...]], axis=0)
        early_part[...] = nt_dot(both, w_out[place.slot]).astype(jnp.bfloat16)


def early_factors(bounds, own, partner, w_in, w_out):
    rows, model = own[0].shape
    inner = w_in.shape[2]
    part = model // 2
    return pl.pallas_call(
        early_kernel,
        out_shape=(
            jax.ShapeDtypeStruct((2 * rows, model), jnp.bfloat16),
            jax.ShapeDtypeStruct((2 * rows, part), jnp.bfloat16),
            jax.ShapeDtypeStruct((2 * rows, part), jnp.bfloat16),
        ),
        in_specs=[SMEM] + [VMEM] * 6,
        out_specs=(VMEM,) * 3,
        scratch_shapes=[pltpu.VMEM((2 * rows, model), jnp.bfloat16)],
        compiler_params=pltpu.CompilerParams(vmem_limit_bytes=KERNEL_BYTES),
        cost_estimate=pl.CostEstimate(
            flops=4 * rows * model * inner, bytes_accessed=3 * model * inner, transcendentals=0
        ),
        name="early",
    )(bounds, *own, *partner, w_in, w_out)


def middle_kernel(bounds, e3, f3, unit_part, value, w_out, in_acc, out_acc):
    place = Place(bounds)
    grads = jnp.concatenate([e3[...], f3[...]], axis=0)
    err = nt_dot(grads, w_out[place.slot]).astype(jnp.bfloat16)
    in_acc[...] = tn_dot(unit_part[...], err)
    out_acc[...] = tn_dot(value[...], grads)


def middle_partials(bounds, e3, f3, unit_part, value, w_out):
    rows, model = e3.shape
    inner = w_out.shape[1]
    part = unit_part.shape[1]
    return pl.pallas_call(
        middle_kernel,
        out_shape=(
            jax.ShapeDtypeStruct((part, inner), jnp.float32),
            jax.ShapeDtypeStruct((part, model), jnp.float32),
        ),
        in_specs=[SMEM] + [VMEM] * 5,
        out_specs=(VMEM,) * 2,
        compiler_params=pltpu.CompilerParams(vmem_limit_bytes=KERNEL_BYTES),
        cost_estimate=pl.CostEstimate(
            flops=8 * rows * model * inner, bytes_accessed=3 * model * inner, transcendentals=0
        ),
        name="middle",
    )(bounds, e3, f3, unit_part, value, w_out)


def split_sums(place, left_part, right_part, acc, x_send, x_keep, z_send, z_keep):
    group = left_part.shape[1] // 2
    block = group // 2
    cols = right_part.shape[1] // 2

    def sums(rows_of, cols_of):
        new = tn_dot(left_part[:, rows_of], right_part[:, cols_of])
        return new if acc is None else acc[rows_of, cols_of] + new

    far = slice(0, group)
    every = slice(None)
    mine = pl.ds(pl.multiple_of(place.column * cols, cols), cols)
    other = pl.ds(pl.multiple_of((1 - place.column) * cols, cols), cols)
    kept = pl.ds(pl.multiple_of(group + place.half * block, block), block)
    sent = pl.ds(pl.multiple_of(group + (1 - place.half) * block, block), block)
    x_send[...] = sums(far, other).astype(jnp.bfloat16)
    x_keep[...] = sums(far, mine)
    z_send[...] = sums(sent, every).astype(jnp.bfloat16)
    z_keep[...] = sums(kept, every)


def late_in_kernel(
    bounds, late, flate, early_part, in_acc, w_out, x_send, x_keep, z_send, z_keep, unit, unit_part, err,
):
    place = Place(bounds)
    part = unit_part.shape[1]

    @pl.when(jnp.logical_not(place.short))
    def _():
        grads = jnp.concatenate([late[...], flate[...]], axis=0)
        err[...] = nt_dot(grads, w_out[place.slot]).astype(jnp.bfloat16)
        unit_part[...] = early_part[:, :part]

    @pl.when(place.short)
    def _():
        put_unit(unit, late, flate)
        unit_columns(place, unit, unit_part)
        err[...] = early_part[...]

    split_sums(place, unit_part, err, in_acc, x_send, x_keep, z_send, z_keep)


def late_out_kernel(
    bounds, unit, e2, f2, out_acc, w_in, up, fup, low, flow,
    x_send, x_keep, z_send, z_keep, value, grads, unit_part,
):
    place = Place(bounds)
    rows = e2.shape[0]
    part = value.shape[1]
    lanes = part // BLOCKS
    outs = (x_send, x_keep, z_send, z_keep)

    def put_grads(first, second):
        grads[:rows, :] = first[...]
        grads[rows:, :] = second[...]

    @pl.when(place.left)
    def _():
        core_columns(place, unit, w_in, unit_part, value)
        put_grads(e2, f2)
        split_sums(place, value, grads, out_acc, *outs)

    @pl.when(jnp.logical_not(place.left))
    def _():
        for j in range(BLOCKS):
            block = lane_block(j, place, lanes)
            where = pl.ds(j * lanes, lanes)
            value[:rows, where] = up[0, :, block]
            value[rows:, where] = fup[0, :, block]

        @pl.when(place.short)
        def _():
            put_grads(up.at[1], fup.at[1])

        @pl.when(jnp.logical_not(place.short))
        def _():
            put_grads(low, flow)

        split_sums(place, value, grads, None, *outs)


def split_shapes(part, width):
    return (
        low_shape(part // 2, width // 2),
        full_shape(part // 2, width // 2),
        low_shape(part // 4, width),
        full_shape(part // 4, width),
    )


def x_add_kernel(keep, land, mine, following):
    half = lax.axis_index("section") % 2
    rows = mine.shape[0]
    kept = pl.ds(pl.multiple_of(half * rows, rows), rows)
    sent = pl.ds(pl.multiple_of((1 - half) * rows, rows), rows)
    mine[...] = keep[kept, :] + land[kept, :].astype(jnp.float32)
    following[...] = (keep[sent, :] + land[sent, :].astype(jnp.float32)).astype(jnp.bfloat16)


def z_add_kernel(keep, land, mine, following):
    column = lax.axis_index("tensor")
    cols = mine.shape[1]
    kept = pl.ds(pl.multiple_of(column * cols, cols), cols)
    sent = pl.ds(pl.multiple_of((1 - column) * cols, cols), cols)
    mine[...] = keep[:, kept] + land[:, kept].astype(jnp.float32)
    following[...] = (keep[:, sent] + land[:, sent].astype(jnp.float32)).astype(jnp.bfloat16)


def last_add_kernel(mine, land, total):
    total[...] = (mine[...] + land[...].astype(jnp.float32)).astype(total.dtype)


def hand_on_kernel(bounds, near, got, give, lower):
    place = Place(bounds)

    @pl.when(place.short)
    def _():
        give[...] = got[...]
        lower[...] = near[...]

    @pl.when(jnp.logical_not(place.short))
    def _():
        give[...] = near[...].astype(jnp.bfloat16)
        lower[...] = got[...].astype(jnp.float32)


def in_result_kernel(lower, landed, result):
    left = lax.axis_index("section") < 2

    @pl.when(left)
    def _():
        result[0] = lower[...]

    @pl.when(jnp.logical_not(left))
    def _():
        result[0] = landed[...].astype(jnp.float32)


def out_result_kernel(bounds, near, got, result):
    place = Place(bounds)
    upper = jnp.logical_not(place.left)

    @pl.when(upper)
    def _():
        result[0] = near[...] + got[...].astype(jnp.float32)

    @pl.when(place.left & place.short)
    def _():
        result[0] = near[...]

    @pl.when(place.left & jnp.logical_not(place.short))
    def _():
        result[0] = got[...].astype(jnp.float32)


def small_call(kernel, operands, shapes, scratch=(), flops=0):
    specs = [SMEM if part.ndim == 2 and part.dtype == jnp.int32 else VMEM for part in operands]
    cost = pl.CostEstimate(flops=flops, bytes_accessed=0, transcendentals=0) if flops else None
    return pl.pallas_call(
        kernel,
        out_shape=shapes,
        in_specs=specs,
        out_specs=jax.tree.map(lambda _: VMEM, shapes),
        scratch_shapes=scratch,
        compiler_params=pltpu.CompilerParams(vmem_limit_bytes=KERNEL_BYTES),
        cost_estimate=cost,
    )(*operands)


def low_shape(*dims):
    return jax.ShapeDtypeStruct(dims, jnp.bfloat16)


def full_shape(*dims):
    return jax.ShapeDtypeStruct(dims, jnp.float32)


def flipped(value, axis, bit):
    return lax.ppermute(value, axis, [(i, i ^ bit) for i in range(lax.axis_size(axis))])


def two_section_body(bounds, saved_inputs, w_in, w_out, top_grad):
    saved = saved_inputs[0, 0]
    proj_in = w_in[0, 0]
    proj_out = w_out[0, 0]
    tops = top_grad[0]
    model = saved.shape[2]
    inner = proj_in.shape[2]

    def across(value):
        return flipped(value, "pipe", 2)

    def core_swap(value):
        return flipped(value, "pipe", 1)

    def half_swap(value):
        return flipped(value, "section", 1)

    def column_swap(value):
        return flipped(value, "tensor", 1)

    half_axis = lax.axis_size("section") // 2

    def upward(value):
        return lax.ppermute(value, "section", [(i, i + half_axis) for i in range(half_axis)])

    def downward(value):
        return lax.ppermute(value, "section", [(i + half_axis, i) for i in range(half_axis)])

    def section_swap(value):
        return flipped(value, "section", 2)

    own_saved, own_top, given = staged(bounds, saved, tops)
    swapped = across(given)
    rows = saved.shape[1]
    grad_low, upload = chain(bounds, tops, saved, proj_in, proj_out)
    lifted = upward(upload)
    hopping = by_role(bounds, grad_low, swapped)
    late = downward(hopping)
    grad_other = across(grad_low)
    own = (own_saved, swapped)
    partner = tuple(core_swap(part) for part in own)
    early_part, unit_part, value = early_factors(bounds, own, partner, proj_in, proj_out)
    grad_early = by_role(bounds, grad_other, own_top)
    in_acc, out_acc = middle_partials(bounds, grad_early, core_swap(grad_early), unit_part, value, proj_out)
    other_low = core_swap(grad_low)
    other_lifted = core_swap(lifted)
    other_late = core_swap(late)
    part = model // 2
    pair = 2 * rows
    *in_parts, unit_late = small_call(
        late_in_kernel,
        (bounds, late, other_late, early_part, in_acc, proj_out),
        split_shapes(part, inner) + (low_shape(pair, model),),
        scratch=[pltpu.VMEM((pair, part), jnp.bfloat16), pltpu.VMEM((pair, inner), jnp.bfloat16)],
        flops=6 * rows * model * inner,
    )
    out_parts = small_call(
        late_out_kernel,
        (bounds, unit_late, own[1], partner[1], out_acc, proj_in)
        + (lifted, other_lifted, grad_low, other_low),
        split_shapes(part, model),
        scratch=[
            pltpu.VMEM((pair, part), jnp.bfloat16),
            pltpu.VMEM((pair, model), jnp.bfloat16),
            pltpu.VMEM((pair, part), jnp.bfloat16),
        ],
        flops=4 * rows * model * inner,
    )
    block = (model // (2 * BLOCKS), model // 2)
    sums = []
    for (x_send, x_keep, z_send, z_keep) in (in_parts, out_parts):
        pair_shapes = (full_shape(*block), low_shape(*block))
        x_land = column_swap(x_send)
        z_land = half_swap(z_send)
        far, far_next = small_call(x_add_kernel, (x_keep, x_land), pair_shapes)
        near, near_next = small_call(z_add_kernel, (z_keep, z_land), pair_shapes)
        far_land = half_swap(far_next)
        near_land = column_swap(near_next)
        far = small_call(last_add_kernel, (far, far_land), low_shape(*block))
        got = across(far)
        near = small_call(last_add_kernel, (near, near_land), full_shape(*block))
        sums.append((near, got))
    (in_near, in_got), (out_near, out_got) = sums
    give, lower = small_call(
        hand_on_kernel, (bounds, in_near, in_got), (low_shape(*block), full_shape(*block))
    )
    landed = section_swap(give)
    return (
        small_call(in_result_kernel, (lower, landed), full_shape(1, *block)),
        small_call(out_result_kernel, (bounds, out_near, out_got), full_shape(1, *block)),
    )


def body(bounds, saved_inputs, w_in, w_out, top_grad):
    two_sections = lax.axis_size("section") == 4 and lax.axis_size("pipe") == 4
    if two_sections and lax.axis_size("tensor") == 2:
        return two_section_body(bounds, saved_inputs, w_in, w_out, top_grad)
    return general_body(bounds, saved_inputs, w_in, w_out, top_grad)


def solution(mesh):
    placed = (
        P(),
        P("pipe", "section", None, "tensor", None),
        P("pipe", "section", None, None, None),
        P("pipe", "section", None, None, None),
        P("pipe", None, "tensor", None),
    )
    return jax.shard_map(
        body,
        mesh=mesh,
        in_specs=placed,
        out_specs=(P("section", "pipe", "tensor"), P("section", "pipe", "tensor")),
        check_vma=False,
    )
```

```python
import jax
import jax.numpy as jnp
from jax import lax
from jax.experimental import pallas as pl
from jax.experimental.pallas import tpu as pltpu
from jax.sharding import PartitionSpec as P

EPS = 1e-05


def shifted(value, axis, steps):
    count = lax.axis_size(axis)
    pairs = [(source, (source + steps) % count) for source in range(count)]
    return lax.ppermute(value, axis, pairs)


def for_sending(shard):

    def short(part):
        return part.astype(jnp.bfloat16) if part.dtype == jnp.float32 else part

    return jax.tree.map(short, shard)


def partner(block, axis, bit):
    count = lax.axis_size(axis)
    route = []
    for low in range(count):
        high = low | 1 << bit
        if high != low and high < count:
            route += [(low, high), (high, low)]
    return lax.ppermute(block, axis, route)


def normalize(saved_rows):
    floats = saved_rows.astype(jnp.float32)
    row_scale = jnp.sqrt(jnp.mean(floats * floats, axis=-1, keepdims=True) + EPS)
    return (floats / row_scale, row_scale)


def layer_back(grad_next, unit_rows, row_scale, proj_in, proj_out):
    err_low = jnp.dot(grad_next, proj_out.T, preferred_element_type=jnp.float32).astype(
        jnp.bfloat16
    )
    pulled = jnp.dot(err_low, proj_in.T, preferred_element_type=jnp.float32)
    inner_mean = jnp.mean(pulled * unit_rows, axis=-1, keepdims=True)
    grad_here = (
        grad_next.astype(jnp.float32) + (pulled - unit_rows * inner_mean) / row_scale
    ).astype(jnp.bfloat16)
    return (grad_here, err_low)


def route_items(members, shifter, offset, occupied, positions, here_section, levels, sections):
    for bit_level in reversed(range(levels)):
        stride = 2**bit_level
        passed = offset // (2 * stride) * (2 * stride)
        present = occupied & ((positions[:, None] + passed) % sections == here_section)
        rising = offset // stride % 2 == 1
        send_mask = jnp.any(present & rising, axis=0)
        keep_mask = jnp.any(present & jnp.logical_not(rising), axis=0)
        outgoing = tuple(
            (
                jnp.where(send_mask[:, None, None], member, jnp.zeros_like(member))
                for member in members
            )
        )
        arrived = shifter(outgoing, stride)
        members = tuple(
            (
                jnp.where(keep_mask[:, None, None], member, jnp.zeros_like(member)) + landed
                for member, landed in zip(members, arrived)
            )
        )
    return members


def general_body(bounds, saved_inputs, w_in, w_out, top_grad):
    sections = lax.axis_size("section") // 2
    tensors = lax.axis_size("tensor")
    pipe_index = lax.axis_index("pipe")
    section_index = lax.axis_index("section")
    tensor_index = lax.axis_index("tensor")
    position = section_index // 2
    token_half = section_index % 2
    boundary = lax.dynamic_index_in_dim(bounds, pipe_index // 2, 0, keepdims=False)
    counts = boundary[1:] - boundary[:-1]
    layers_here = lax.dynamic_index_in_dim(counts, position, 0, keepdims=False)
    saved_rows = saved_inputs[0, 0]
    proj_in = w_in[0, 0]
    proj_out = w_out[0, 0]
    slot_count = saved_rows.shape[0]
    row_count = saved_rows.shape[1]
    model_width = saved_rows.shape[2]
    inner_width = proj_in.shape[2]
    unit_rows, scales = normalize(saved_rows)
    unit_low = unit_rows.astype(jnp.bfloat16)
    value_low = jnp.einsum(
        "kre,kea->kra", unit_low, proj_in, preferred_element_type=jnp.float32
    ).astype(jnp.bfloat16)
    positions = jnp.arange(sections, dtype=jnp.int32)
    slot_ids = jnp.arange(slot_count, dtype=jnp.int32)
    occupied = slot_ids[None, :] < counts[:, None]
    layer_of = boundary[:-1, None] + slot_ids[None, :]
    offset = (layer_of + 1 - positions[:, None]) % sections
    levels = min((sections - 3 * sections // 4 + 1).bit_length(), (sections - 1).bit_length())
    top_rows = lax.dynamic_index_in_dim(top_grad[0], token_half, 0, keepdims=False)

    def run_section(incoming):

        def upper_layer(grad_top):
            return layer_back(grad_top, unit_rows[1], scales[1], proj_in[1], proj_out[1])

        def lower_layer(grad_top):
            return layer_back(grad_top, unit_rows[0], scales[0], proj_in[0], proj_out[0])

        def no_layer(grad_top):
            return (grad_top, jnp.zeros((row_count, inner_width), jnp.bfloat16))

        lower_start, upper_err = lax.cond(layers_here == 2, upper_layer, no_layer, incoming)
        result, lower_err = lax.cond(layers_here >= 1, lower_layer, no_layer, lower_start)
        return (result, jnp.stack([lower_start, incoming]), jnp.stack([lower_err, upper_err]))

    def loop_turn(turn_index, carried):
        incoming = shifted(carried[0], "section", -2)
        return lax.cond(
            position == sections - 1 - turn_index,
            lambda arriving, kept: run_section(arriving),
            lambda arriving, kept: kept,
            incoming,
            carried,
        )

    start_rows = jnp.where(position == 0, top_rows, jnp.zeros_like(top_rows))
    carried = (
        start_rows,
        jnp.zeros((slot_count, row_count, model_width), jnp.bfloat16),
        jnp.zeros((slot_count, row_count, inner_width), jnp.bfloat16),
    )
    carried = lax.fori_loop(0, sections, loop_turn, carried)
    grads_slots = carried[1]
    errors = carried[2]
    unit_got, value_got, err_got, grad_got = route_items(
        (unit_low, value_low, errors, grads_slots),
        lambda members, stride: jax.tree.map(
            lambda part, own: part.astype(own.dtype),
            shifted(for_sending(members), "section", 2 * stride),
            members,
        ),
        offset,
        occupied,
        positions,
        position,
        levels,
        sections,
    )
    owner_slot = jnp.sum(
        jnp.where(occupied & ((layer_of + 1) % sections == position), slot_ids[None, :], 0)
    )
    unit_own = lax.dynamic_index_in_dim(unit_got, owner_slot, 0, keepdims=False)
    value_own = lax.dynamic_index_in_dim(value_got, owner_slot, 0, keepdims=False)
    err_own = lax.dynamic_index_in_dim(err_got, owner_slot, 0, keepdims=False)
    grad_own = lax.dynamic_index_in_dim(grad_got, owner_slot, 0, keepdims=False)
    in_cols = inner_width // tensors
    out_cols = model_width // tensors
    unit_piece = lax.all_gather(unit_own, "tensor", axis=0, tiled=True)
    value_piece = lax.all_gather(value_own, "tensor", axis=0, tiled=True)
    err_piece = lax.all_gather(err_own, "tensor", axis=0, tiled=True)
    grad_piece = lax.all_gather(grad_own, "tensor", axis=0, tiled=True)
    err_cols = lax.dynamic_slice_in_dim(err_piece, tensor_index * in_cols, in_cols, 1)
    grad_cols = lax.dynamic_slice_in_dim(grad_piece, tensor_index * out_cols, out_cols, 1)
    totals = (
        jnp.dot(unit_piece.T, err_cols, preferred_element_type=jnp.float32),
        jnp.dot(value_piece.T, grad_cols, preferred_element_type=jnp.float32),
    )
    half_model = model_width // 2
    half_inner = inner_width // 2
    mine_in = lax.dynamic_slice_in_dim(totals[0], token_half * half_model, half_model, 0)
    other_in = lax.dynamic_slice_in_dim(totals[0], (1 - token_half) * half_model, half_model, 0)
    mine_out = lax.dynamic_slice_in_dim(totals[1], token_half * half_inner, half_inner, 0)
    other_out = lax.dynamic_slice_in_dim(totals[1], (1 - token_half) * half_inner, half_inner, 0)
    landed_in, landed_out = partner((other_in, other_out), "section", 0)
    grad_in_part, grad_out_part = (
        lax.psum_scatter(mine_in + landed_in, "pipe", scatter_dimension=0, tiled=True),
        lax.psum_scatter(mine_out + landed_out, "pipe", scatter_dimension=0, tiled=True),
    )
    return (grad_in_part[None], grad_out_part[None])


VMEM = pl.BlockSpec(memory_space=pltpu.VMEM)
SMEM = pl.BlockSpec(memory_space=pltpu.SMEM)
KERNEL_BYTES = 14 * 2**20
STAGE_FLOPS = 8 * 10**9


class Place:
    def __init__(self, short):
        pipe = lax.axis_index("pipe")
        section = lax.axis_index("section")
        self.column = lax.axis_index("tensor")
        self.relay = pipe // 2
        self.core = pipe % 2
        self.half = section % 2
        self.left = section < 2
        self.short = short
        self.slot = jnp.where(self.short, 1, 0)
        self.upper_slot = jnp.where(self.left, 1, 0)


def norm_rows(saved):
    floats = saved.astype(jnp.float32)
    row_scale = jnp.sqrt(jnp.mean(floats * floats, axis=-1, keepdims=True) + EPS)
    return floats / row_scale, row_scale


def nt_dot(left, right):
    return lax.dot_general(left, right, (((1,), (1,)), ((), ())), preferred_element_type=jnp.float32)


def tn_dot(left, right):
    return lax.dot_general(left, right, (((0,), (0,)), ((), ())), preferred_element_type=jnp.float32)


def chain_kernel(flag, tops, saved, w_in, w_out, grad_out, upward):
    place = Place(flag[0, 0] > 0)
    slot = place.upper_slot
    first_unit = norm_rows(saved[0])[0].astype(jnp.bfloat16)
    upward[0] = jnp.dot(first_unit, w_in[0], preferred_element_type=jnp.float32).astype(jnp.bfloat16)
    grad_next = tops[place.half]
    err = nt_dot(grad_next, w_out[slot]).astype(jnp.bfloat16)
    unit, row_scale = norm_rows(saved[slot])
    pulled = nt_dot(err, w_in[slot])
    inner_mean = jnp.mean(pulled * unit, axis=-1, keepdims=True)
    back = grad_next.astype(jnp.float32) + (pulled - unit * inner_mean) / row_scale
    grad_low = back.astype(jnp.bfloat16)
    grad_out[...] = grad_low
    upward[1] = grad_low


def chain(flag, tops, saved, w_in, w_out):
    rows, model = saved.shape[1:]
    inner = w_in.shape[2]
    return pl.pallas_call(
        chain_kernel,
        out_shape=(low_shape(rows, model), low_shape(2, rows, model)),
        in_specs=[VMEM] * 5,
        out_specs=(VMEM,) * 2,
        compiler_params=pltpu.CompilerParams(vmem_limit_bytes=KERNEL_BYTES),
        cost_estimate=pl.CostEstimate(
            flops=6 * rows * model * inner, bytes_accessed=4 * model * inner, transcendentals=0
        ),
        name="chain",
    )(flag, tops, saved, w_in, w_out)


def opening_kernel(mark):
    mark[...] = jnp.zeros_like(mark)


def opening():
    return pl.pallas_call(
        opening_kernel,
        out_shape=jax.ShapeDtypeStruct((8, 128), jnp.float32),
        out_specs=VMEM,
        compiler_params=pltpu.CompilerParams(vmem_limit_bytes=KERNEL_BYTES),
        cost_estimate=pl.CostEstimate(flops=STAGE_FLOPS, bytes_accessed=4096, transcendentals=0),
        name="opening",
    )()


def staged_kernel(bounds, mark, saved, tops, own_saved, own_top, given, flag):
    relay = lax.axis_index("pipe") // 2
    place = Place(bounds[relay, 1] - bounds[relay, 0] == 2)
    give_top = place.left & jnp.logical_not(place.short)
    flag[...] = jnp.full_like(flag, jnp.where(place.short, 1, 0))
    own_saved[...] = saved[place.slot]
    own_top[...] = tops[place.half]

    @pl.when(give_top)
    def _():
        given[...] = tops[place.half]

    @pl.when(jnp.logical_not(give_top))
    def _():
        given[...] = saved[0]


def staged(bounds, saved, tops):
    block = jax.ShapeDtypeStruct(saved.shape[1:], saved.dtype)
    return pl.pallas_call(
        staged_kernel,
        out_shape=(block,) * 3 + (jax.ShapeDtypeStruct((8, 128), jnp.int32),),
        in_specs=[SMEM, VMEM, VMEM, VMEM],
        out_specs=(VMEM,) * 4,
        compiler_params=pltpu.CompilerParams(vmem_limit_bytes=KERNEL_BYTES),
        cost_estimate=pl.CostEstimate(flops=STAGE_FLOPS, bytes_accessed=8 * saved.size, transcendentals=0),
        name="staged",
    )(bounds, opening(), saved, tops)


def by_role_kernel(flag, full_part, short_part, chosen):
    place = Place(flag[0, 0] > 0)

    @pl.when(place.short)
    def _():
        chosen[...] = short_part[...]

    @pl.when(jnp.logical_not(place.short))
    def _():
        chosen[...] = full_part[...]


def by_role(flag, full_part, short_part):
    return pl.pallas_call(
        by_role_kernel,
        out_shape=jax.ShapeDtypeStruct(full_part.shape, full_part.dtype),
        in_specs=[VMEM] * 3,
        out_specs=VMEM,
        compiler_params=pltpu.CompilerParams(vmem_limit_bytes=KERNEL_BYTES),
        name="by_role",
    )(flag, full_part, short_part)


BLOCKS = 4


def put_unit(unit, first, second):
    rows = first.shape[0]
    unit[:rows, :] = norm_rows(first[...])[0].astype(jnp.bfloat16)
    unit[rows:, :] = norm_rows(second[...])[0].astype(jnp.bfloat16)


def lane_block(j, place, lanes):
    owner = place.relay if j // 2 else 1 - place.relay
    return pl.ds(pl.multiple_of((4 * (j % 2) + 2 * owner + place.core) * lanes, lanes), lanes)


def unit_columns(place, unit, unit_part):
    lanes = unit.shape[1] // (2 * BLOCKS)
    for j in range(BLOCKS):
        unit_part[:, j * lanes : (j + 1) * lanes] = unit[:, lane_block(j, place, lanes)]


def core_columns(place, unit, w_in, unit_part, value):
    lanes = unit.shape[1] // (2 * BLOCKS)
    for j in range(BLOCKS):
        block = lane_block(j, place, lanes)
        where = pl.ds(j * lanes, lanes)
        unit_part[:, where] = unit[:, block]
        value[:, where] = jnp.dot(
            unit[...], w_in[place.slot, :, block], preferred_element_type=jnp.float32
        ).astype(jnp.bfloat16)


def early_kernel(flag, e1, e2, f1, f2, w_in, w_out, early_part, unit_part, value, unit):
    place = Place(flag[0, 0] > 0)

    @pl.when(jnp.logical_not(place.short))
    def _():
        put_unit(unit, e2, f2)
        unit_columns(place, unit, unit_part)
        value[...] = jnp.zeros_like(value)
        put_unit(unit, e1, f1)
        unit_columns(place, unit, early_part)

    @pl.when(place.short)
    def _():
        put_unit(unit, e1, f1)
        core_columns(place, unit, w_in, unit_part, value)
        both = jnp.concatenate([e2[...], f2[...]], axis=0)
        early_part[...] = nt_dot(both, w_out[place.slot]).astype(jnp.bfloat16)


def early_factors(flag, own, partner, w_in, w_out):
    rows, model = own[0].shape
    inner = w_in.shape[2]
    part = model // 2
    return pl.pallas_call(
        early_kernel,
        out_shape=(
            jax.ShapeDtypeStruct((2 * rows, model), jnp.bfloat16),
            jax.ShapeDtypeStruct((2 * rows, part), jnp.bfloat16),
            jax.ShapeDtypeStruct((2 * rows, part), jnp.bfloat16),
        ),
        in_specs=[VMEM] * 7,
        out_specs=(VMEM,) * 3,
        scratch_shapes=[pltpu.VMEM((2 * rows, model), jnp.bfloat16)],
        compiler_params=pltpu.CompilerParams(vmem_limit_bytes=KERNEL_BYTES),
        cost_estimate=pl.CostEstimate(
            flops=4 * rows * model * inner, bytes_accessed=3 * model * inner, transcendentals=0
        ),
        name="early",
    )(flag, *own, *partner, w_in, w_out)


def middle_kernel(flag, e3, f3, unit_part, value, w_out, in_acc, out_acc):
    place = Place(flag[0, 0] > 0)
    grads = jnp.concatenate([e3[...], f3[...]], axis=0)
    err = nt_dot(grads, w_out[place.slot]).astype(jnp.bfloat16)
    in_acc[...] = tn_dot(unit_part[...], err)
    out_acc[...] = tn_dot(value[...], grads)


def middle_partials(flag, e3, f3, unit_part, value, w_out):
    rows, model = e3.shape
    inner = w_out.shape[1]
    part = unit_part.shape[1]
    return pl.pallas_call(
        middle_kernel,
        out_shape=(
            jax.ShapeDtypeStruct((part, inner), jnp.float32),
            jax.ShapeDtypeStruct((part, model), jnp.float32),
        ),
        in_specs=[VMEM] * 6,
        out_specs=(VMEM,) * 2,
        compiler_params=pltpu.CompilerParams(vmem_limit_bytes=KERNEL_BYTES),
        cost_estimate=pl.CostEstimate(
            flops=8 * rows * model * inner, bytes_accessed=3 * model * inner, transcendentals=0
        ),
        name="middle",
    )(flag, e3, f3, unit_part, value, w_out)


def split_sums(place, left_part, right_part, acc, x_send, x_keep, z_send, z_keep):
    group = left_part.shape[1] // 2
    block = group // 2
    cols = right_part.shape[1] // 2

    def sums(rows_of, cols_of):
        new = tn_dot(left_part[:, rows_of], right_part[:, cols_of])
        return new if acc is None else acc[rows_of, cols_of] + new

    far = slice(0, group)
    every = slice(None)
    mine = pl.ds(pl.multiple_of(place.column * cols, cols), cols)
    other = pl.ds(pl.multiple_of((1 - place.column) * cols, cols), cols)
    kept = pl.ds(pl.multiple_of(group + place.half * block, block), block)
    sent = pl.ds(pl.multiple_of(group + (1 - place.half) * block, block), block)
    x_send[...] = sums(far, other).astype(jnp.bfloat16)
    x_keep[...] = sums(far, mine)
    z_send[...] = sums(sent, every).astype(jnp.bfloat16)
    z_keep[...] = sums(kept, every)


def late_in_kernel(
    flag, late, flate, early_part, in_acc, w_out, x_send, x_keep, z_send, z_keep, unit, unit_part, err,
):
    place = Place(flag[0, 0] > 0)
    part = unit_part.shape[1]

    @pl.when(jnp.logical_not(place.short))
    def _():
        grads = jnp.concatenate([late[...], flate[...]], axis=0)
        err[...] = nt_dot(grads, w_out[place.slot]).astype(jnp.bfloat16)
        unit_part[...] = early_part[:, :part]

    @pl.when(place.short)
    def _():
        put_unit(unit, late, flate)
        unit_columns(place, unit, unit_part)
        err[...] = early_part[...]

    split_sums(place, unit_part, err, in_acc, x_send, x_keep, z_send, z_keep)


def late_out_kernel(
    flag, unit, e2, f2, out_acc, w_in, up, fup, low, flow,
    x_send, x_keep, z_send, z_keep, value, grads, unit_part,
):
    place = Place(flag[0, 0] > 0)
    rows = e2.shape[0]
    part = value.shape[1]
    lanes = part // BLOCKS
    outs = (x_send, x_keep, z_send, z_keep)

    def put_grads(first, second):
        grads[:rows, :] = first[...]
        grads[rows:, :] = second[...]

    @pl.when(place.left)
    def _():
        core_columns(place, unit, w_in, unit_part, value)
        put_grads(e2, f2)
        split_sums(place, value, grads, out_acc, *outs)

    @pl.when(jnp.logical_not(place.left))
    def _():
        for j in range(BLOCKS):
            block = lane_block(j, place, lanes)
            where = pl.ds(j * lanes, lanes)
            value[:rows, where] = up[0, :, block]
            value[rows:, where] = fup[0, :, block]

        @pl.when(place.short)
        def _():
            put_grads(up.at[1], fup.at[1])

        @pl.when(jnp.logical_not(place.short))
        def _():
            put_grads(low, flow)

        split_sums(place, value, grads, None, *outs)


def split_shapes(part, width):
    return (
        low_shape(part // 2, width // 2),
        full_shape(part // 2, width // 2),
        low_shape(part // 4, width),
        full_shape(part // 4, width),
    )


def x_add_kernel(keep, land, mine, following):
    half = lax.axis_index("section") % 2
    rows = mine.shape[0]
    kept = pl.ds(pl.multiple_of(half * rows, rows), rows)
    sent = pl.ds(pl.multiple_of((1 - half) * rows, rows), rows)
    mine[...] = keep[kept, :] + land[kept, :].astype(jnp.float32)
    following[...] = (keep[sent, :] + land[sent, :].astype(jnp.float32)).astype(jnp.bfloat16)


def z_add_kernel(keep, land, mine, following):
    column = lax.axis_index("tensor")
    cols = mine.shape[1]
    kept = pl.ds(pl.multiple_of(column * cols, cols), cols)
    sent = pl.ds(pl.multiple_of((1 - column) * cols, cols), cols)
    mine[...] = keep[:, kept] + land[:, kept].astype(jnp.float32)
    following[...] = (keep[:, sent] + land[:, sent].astype(jnp.float32)).astype(jnp.bfloat16)


def last_add_kernel(mine, land, total):
    total[...] = (mine[...] + land[...].astype(jnp.float32)).astype(total.dtype)


def hand_on_kernel(flag, near, got, give, lower):
    place = Place(flag[0, 0] > 0)

    @pl.when(place.short)
    def _():
        give[...] = got[...]
        lower[...] = near[...]

    @pl.when(jnp.logical_not(place.short))
    def _():
        give[...] = near[...].astype(jnp.bfloat16)
        lower[...] = got[...].astype(jnp.float32)


def in_result_kernel(lower, landed, result):
    left = lax.axis_index("section") < 2

    @pl.when(left)
    def _():
        result[0] = lower[...]

    @pl.when(jnp.logical_not(left))
    def _():
        result[0] = landed[...].astype(jnp.float32)


def out_result_kernel(flag, near, got, result):
    place = Place(flag[0, 0] > 0)
    upper = jnp.logical_not(place.left)

    @pl.when(upper)
    def _():
        result[0] = near[...] + got[...].astype(jnp.float32)

    @pl.when(place.left & place.short)
    def _():
        result[0] = near[...]

    @pl.when(place.left & jnp.logical_not(place.short))
    def _():
        result[0] = got[...].astype(jnp.float32)


def small_call(kernel, operands, shapes, scratch=(), flops=0):
    cost = pl.CostEstimate(flops=flops, bytes_accessed=0, transcendentals=0) if flops else None
    return pl.pallas_call(
        kernel,
        out_shape=shapes,
        in_specs=[VMEM] * len(operands),
        out_specs=jax.tree.map(lambda _: VMEM, shapes),
        scratch_shapes=scratch,
        compiler_params=pltpu.CompilerParams(vmem_limit_bytes=KERNEL_BYTES),
        cost_estimate=cost,
    )(*operands)


def low_shape(*dims):
    return jax.ShapeDtypeStruct(dims, jnp.bfloat16)


def full_shape(*dims):
    return jax.ShapeDtypeStruct(dims, jnp.float32)


def flipped(value, axis, bit):
    return lax.ppermute(value, axis, [(i, i ^ bit) for i in range(lax.axis_size(axis))])


def two_section_body(bounds, saved_inputs, w_in, w_out, top_grad):
    saved = saved_inputs[0, 0]
    proj_in = w_in[0, 0]
    proj_out = w_out[0, 0]
    tops = top_grad[0]
    model = saved.shape[2]
    inner = proj_in.shape[2]

    def across(value):
        return flipped(value, "pipe", 2)

    def core_swap(value):
        return flipped(value, "pipe", 1)

    def half_swap(value):
        return flipped(value, "section", 1)

    def column_swap(value):
        return flipped(value, "tensor", 1)

    half_axis = lax.axis_size("section") // 2

    def upward(value):
        return lax.ppermute(value, "section", [(i, i + half_axis) for i in range(half_axis)])

    def downward(value):
        return lax.ppermute(value, "section", [(i + half_axis, i) for i in range(half_axis)])

    def section_swap(value):
        return flipped(value, "section", 2)

    own_saved, own_top, given, flag = staged(bounds, saved, tops)
    swapped = across(given)
    rows = saved.shape[1]
    grad_low, upload = chain(flag, tops, saved, proj_in, proj_out)
    lifted = upward(upload)
    hopping = by_role(flag, grad_low, swapped)
    late = downward(hopping)
    grad_other = across(grad_low)
    own = (own_saved, swapped)
    partner = tuple(core_swap(part) for part in own)
    early_part, unit_part, value = early_factors(flag, own, partner, proj_in, proj_out)
    grad_early = by_role(flag, grad_other, own_top)
    in_acc, out_acc = middle_partials(flag, grad_early, core_swap(grad_early), unit_part, value, proj_out)
    other_low = core_swap(grad_low)
    other_lifted = core_swap(lifted)
    other_late = core_swap(late)
    part = model // 2
    pair = 2 * rows
    *in_parts, unit_late = small_call(
        late_in_kernel,
        (flag, late, other_late, early_part, in_acc, proj_out),
        split_shapes(part, inner) + (low_shape(pair, model),),
        scratch=[pltpu.VMEM((pair, part), jnp.bfloat16), pltpu.VMEM((pair, inner), jnp.bfloat16)],
        flops=6 * rows * model * inner,
    )
    out_parts = small_call(
        late_out_kernel,
        (flag, unit_late, own[1], partner[1], out_acc, proj_in)
        + (lifted, other_lifted, grad_low, other_low),
        split_shapes(part, model),
        scratch=[
            pltpu.VMEM((pair, part), jnp.bfloat16),
            pltpu.VMEM((pair, model), jnp.bfloat16),
            pltpu.VMEM((pair, part), jnp.bfloat16),
        ],
        flops=4 * rows * model * inner,
    )
    block = (model // (2 * BLOCKS), model // 2)
    sums = []
    for (x_send, x_keep, z_send, z_keep) in (in_parts, out_parts):
        pair_shapes = (full_shape(*block), low_shape(*block))
        x_land = column_swap(x_send)
        z_land = half_swap(z_send)
        far, far_next = small_call(x_add_kernel, (x_keep, x_land), pair_shapes)
        near, near_next = small_call(z_add_kernel, (z_keep, z_land), pair_shapes)
        far_land = half_swap(far_next)
        near_land = column_swap(near_next)
        far = small_call(last_add_kernel, (far, far_land), low_shape(*block))
        got = across(far)
        near = small_call(last_add_kernel, (near, near_land), full_shape(*block))
        sums.append((near, got))
    (in_near, in_got), (out_near, out_got) = sums
    give, lower = small_call(
        hand_on_kernel, (flag, in_near, in_got), (low_shape(*block), full_shape(*block))
    )
    landed = section_swap(give)
    return (
        small_call(in_result_kernel, (lower, landed), full_shape(1, *block)),
        small_call(out_result_kernel, (flag, out_near, out_got), full_shape(1, *block)),
    )


def body(bounds, saved_inputs, w_in, w_out, top_grad):
    two_sections = lax.axis_size("section") == 4 and lax.axis_size("pipe") == 4
    if two_sections and lax.axis_size("tensor") == 2:
        return two_section_body(bounds, saved_inputs, w_in, w_out, top_grad)
    return general_body(bounds, saved_inputs, w_in, w_out, top_grad)


def solution(mesh):
    placed = (
        P(),
        P("pipe", "section", None, "tensor", None),
        P("pipe", "section", None, None, None),
        P("pipe", "section", None, None, None),
        P("pipe", None, "tensor", None),
    )
    return jax.shard_map(
        body,
        mesh=mesh,
        in_specs=placed,
        out_specs=(P("section", "pipe", "tensor"), P("section", "pipe", "tensor")),
        check_vma=False,
    )
```

```python
import jax
import jax.numpy as jnp
from jax import lax
from jax.experimental import pallas as pl
from jax.experimental.pallas import tpu as pltpu
from jax.sharding import PartitionSpec as P

EPS = 1e-05


def shifted(value, axis, steps):
    count = lax.axis_size(axis)
    pairs = [(source, (source + steps) % count) for source in range(count)]
    return lax.ppermute(value, axis, pairs)


def for_sending(shard):

    def short(part):
        return part.astype(jnp.bfloat16) if part.dtype == jnp.float32 else part

    return jax.tree.map(short, shard)


def partner(block, axis, bit):
    count = lax.axis_size(axis)
    route = []
    for low in range(count):
        high = low | 1 << bit
        if high != low and high < count:
            route += [(low, high), (high, low)]
    return lax.ppermute(block, axis, route)


def normalize(saved_rows):
    floats = saved_rows.astype(jnp.float32)
    row_scale = jnp.sqrt(jnp.mean(floats * floats, axis=-1, keepdims=True) + EPS)
    return (floats / row_scale, row_scale)


def layer_back(grad_next, unit_rows, row_scale, proj_in, proj_out):
    err_low = jnp.dot(grad_next, proj_out.T, preferred_element_type=jnp.float32).astype(
        jnp.bfloat16
    )
    pulled = jnp.dot(err_low, proj_in.T, preferred_element_type=jnp.float32)
    inner_mean = jnp.mean(pulled * unit_rows, axis=-1, keepdims=True)
    grad_here = (
        grad_next.astype(jnp.float32) + (pulled - unit_rows * inner_mean) / row_scale
    ).astype(jnp.bfloat16)
    return (grad_here, err_low)


def route_items(members, shifter, offset, occupied, positions, here_section, levels, sections):
    for bit_level in reversed(range(levels)):
        stride = 2**bit_level
        passed = offset // (2 * stride) * (2 * stride)
        present = occupied & ((positions[:, None] + passed) % sections == here_section)
        rising = offset // stride % 2 == 1
        send_mask = jnp.any(present & rising, axis=0)
        keep_mask = jnp.any(present & jnp.logical_not(rising), axis=0)
        outgoing = tuple(
            (
                jnp.where(send_mask[:, None, None], member, jnp.zeros_like(member))
                for member in members
            )
        )
        arrived = shifter(outgoing, stride)
        members = tuple(
            (
                jnp.where(keep_mask[:, None, None], member, jnp.zeros_like(member)) + landed
                for member, landed in zip(members, arrived)
            )
        )
    return members


def general_body(bounds, saved_inputs, w_in, w_out, top_grad):
    sections = lax.axis_size("section") // 2
    tensors = lax.axis_size("tensor")
    pipe_index = lax.axis_index("pipe")
    section_index = lax.axis_index("section")
    tensor_index = lax.axis_index("tensor")
    position = section_index // 2
    token_half = section_index % 2
    boundary = lax.dynamic_index_in_dim(bounds, pipe_index // 2, 0, keepdims=False)
    counts = boundary[1:] - boundary[:-1]
    layers_here = lax.dynamic_index_in_dim(counts, position, 0, keepdims=False)
    saved_rows = saved_inputs[0, 0]
    proj_in = w_in[0, 0]
    proj_out = w_out[0, 0]
    slot_count = saved_rows.shape[0]
    row_count = saved_rows.shape[1]
    model_width = saved_rows.shape[2]
    inner_width = proj_in.shape[2]
    unit_rows, scales = normalize(saved_rows)
    unit_low = unit_rows.astype(jnp.bfloat16)
    value_low = jnp.einsum(
        "kre,kea->kra", unit_low, proj_in, preferred_element_type=jnp.float32
    ).astype(jnp.bfloat16)
    positions = jnp.arange(sections, dtype=jnp.int32)
    slot_ids = jnp.arange(slot_count, dtype=jnp.int32)
    occupied = slot_ids[None, :] < counts[:, None]
    layer_of = boundary[:-1, None] + slot_ids[None, :]
    offset = (layer_of + 1 - positions[:, None]) % sections
    levels = min((sections - 3 * sections // 4 + 1).bit_length(), (sections - 1).bit_length())
    top_rows = lax.dynamic_index_in_dim(top_grad[0], token_half, 0, keepdims=False)

    def run_section(incoming):

        def upper_layer(grad_top):
            return layer_back(grad_top, unit_rows[1], scales[1], proj_in[1], proj_out[1])

        def lower_layer(grad_top):
            return layer_back(grad_top, unit_rows[0], scales[0], proj_in[0], proj_out[0])

        def no_layer(grad_top):
            return (grad_top, jnp.zeros((row_count, inner_width), jnp.bfloat16))

        lower_start, upper_err = lax.cond(layers_here == 2, upper_layer, no_layer, incoming)
        result, lower_err = lax.cond(layers_here >= 1, lower_layer, no_layer, lower_start)
        return (result, jnp.stack([lower_start, incoming]), jnp.stack([lower_err, upper_err]))

    def loop_turn(turn_index, carried):
        incoming = shifted(carried[0], "section", -2)
        return lax.cond(
            position == sections - 1 - turn_index,
            lambda arriving, kept: run_section(arriving),
            lambda arriving, kept: kept,
            incoming,
            carried,
        )

    start_rows = jnp.where(position == 0, top_rows, jnp.zeros_like(top_rows))
    carried = (
        start_rows,
        jnp.zeros((slot_count, row_count, model_width), jnp.bfloat16),
        jnp.zeros((slot_count, row_count, inner_width), jnp.bfloat16),
    )
    carried = lax.fori_loop(0, sections, loop_turn, carried)
    grads_slots = carried[1]
    errors = carried[2]
    unit_got, value_got, err_got, grad_got = route_items(
        (unit_low, value_low, errors, grads_slots),
        lambda members, stride: jax.tree.map(
            lambda part, own: part.astype(own.dtype),
            shifted(for_sending(members), "section", 2 * stride),
            members,
        ),
        offset,
        occupied,
        positions,
        position,
        levels,
        sections,
    )
    owner_slot = jnp.sum(
        jnp.where(occupied & ((layer_of + 1) % sections == position), slot_ids[None, :], 0)
    )
    unit_own = lax.dynamic_index_in_dim(unit_got, owner_slot, 0, keepdims=False)
    value_own = lax.dynamic_index_in_dim(value_got, owner_slot, 0, keepdims=False)
    err_own = lax.dynamic_index_in_dim(err_got, owner_slot, 0, keepdims=False)
    grad_own = lax.dynamic_index_in_dim(grad_got, owner_slot, 0, keepdims=False)
    in_cols = inner_width // tensors
    out_cols = model_width // tensors
    unit_piece = lax.all_gather(unit_own, "tensor", axis=0, tiled=True)
    value_piece = lax.all_gather(value_own, "tensor", axis=0, tiled=True)
    err_piece = lax.all_gather(err_own, "tensor", axis=0, tiled=True)
    grad_piece = lax.all_gather(grad_own, "tensor", axis=0, tiled=True)
    err_cols = lax.dynamic_slice_in_dim(err_piece, tensor_index * in_cols, in_cols, 1)
    grad_cols = lax.dynamic_slice_in_dim(grad_piece, tensor_index * out_cols, out_cols, 1)
    totals = (
        jnp.dot(unit_piece.T, err_cols, preferred_element_type=jnp.float32),
        jnp.dot(value_piece.T, grad_cols, preferred_element_type=jnp.float32),
    )
    half_model = model_width // 2
    half_inner = inner_width // 2
    mine_in = lax.dynamic_slice_in_dim(totals[0], token_half * half_model, half_model, 0)
    other_in = lax.dynamic_slice_in_dim(totals[0], (1 - token_half) * half_model, half_model, 0)
    mine_out = lax.dynamic_slice_in_dim(totals[1], token_half * half_inner, half_inner, 0)
    other_out = lax.dynamic_slice_in_dim(totals[1], (1 - token_half) * half_inner, half_inner, 0)
    landed_in, landed_out = partner((other_in, other_out), "section", 0)
    grad_in_part, grad_out_part = (
        lax.psum_scatter(mine_in + landed_in, "pipe", scatter_dimension=0, tiled=True),
        lax.psum_scatter(mine_out + landed_out, "pipe", scatter_dimension=0, tiled=True),
    )
    return (grad_in_part[None], grad_out_part[None])


VMEM = pl.BlockSpec(memory_space=pltpu.VMEM)
SMEM = pl.BlockSpec(memory_space=pltpu.SMEM)
KERNEL_BYTES = 14 * 2**20
STAGE_FLOPS = 8 * 10**9


class Place:
    def __init__(self, short):
        pipe = lax.axis_index("pipe")
        section = lax.axis_index("section")
        self.column = lax.axis_index("tensor")
        self.relay = pipe // 2
        self.core = pipe % 2
        self.half = section % 2
        self.left = section < 2
        self.short = short
        self.slot = jnp.where(self.short, 1, 0)
        self.upper_slot = jnp.where(self.left, 1, 0)


def norm_rows(saved):
    floats = saved.astype(jnp.float32)
    row_scale = jnp.sqrt(jnp.mean(floats * floats, axis=-1, keepdims=True) + EPS)
    return floats / row_scale, row_scale


def nt_dot(left, right):
    return lax.dot_general(left, right, (((1,), (1,)), ((), ())), preferred_element_type=jnp.float32)


def tn_dot(left, right):
    return lax.dot_general(left, right, (((0,), (0,)), ((), ())), preferred_element_type=jnp.float32)


def chain_kernel(flag, tops, saved, w_in, w_out, grad_out, upward):
    place = Place(flag[0, 0] > 0)
    slot = place.upper_slot
    first_unit = norm_rows(saved[0])[0].astype(jnp.bfloat16)
    upward[0] = jnp.dot(first_unit, w_in[0], preferred_element_type=jnp.float32).astype(jnp.bfloat16)
    grad_next = tops[place.half]
    err = nt_dot(grad_next, w_out[slot]).astype(jnp.bfloat16)
    unit, row_scale = norm_rows(saved[slot])
    pulled = nt_dot(err, w_in[slot])
    inner_mean = jnp.mean(pulled * unit, axis=-1, keepdims=True)
    back = grad_next.astype(jnp.float32) + (pulled - unit * inner_mean) / row_scale
    grad_low = back.astype(jnp.bfloat16)
    grad_out[...] = grad_low
    upward[1] = grad_low


def chain(flag, tops, saved, w_in, w_out):
    rows, model = saved.shape[1:]
    inner = w_in.shape[2]
    return pl.pallas_call(
        chain_kernel,
        out_shape=(low_shape(rows, model), low_shape(2, rows, model)),
        in_specs=[VMEM] * 5,
        out_specs=(VMEM,) * 2,
        compiler_params=pltpu.CompilerParams(vmem_limit_bytes=KERNEL_BYTES),
        cost_estimate=pl.CostEstimate(
            flops=6 * rows * model * inner, bytes_accessed=4 * model * inner, transcendentals=0
        ),
        name="chain",
    )(flag, tops, saved, w_in, w_out)


def opening_kernel(mark):
    mark[...] = jnp.zeros_like(mark)


def opening():
    return pl.pallas_call(
        opening_kernel,
        out_shape=jax.ShapeDtypeStruct((8, 128), jnp.float32),
        out_specs=VMEM,
        compiler_params=pltpu.CompilerParams(vmem_limit_bytes=KERNEL_BYTES),
        cost_estimate=pl.CostEstimate(flops=STAGE_FLOPS, bytes_accessed=4096, transcendentals=0),
        name="opening",
    )()


def staged_kernel(bounds, mark, saved, tops, own_saved, own_top, given, flag):
    relay = lax.axis_index("pipe") // 2
    place = Place(bounds[relay, 1] - bounds[relay, 0] == 2)
    give_top = place.left & jnp.logical_not(place.short)
    flag[...] = jnp.full_like(flag, jnp.where(place.short, 1, 0))
    own_saved[...] = saved[place.slot]
    own_top[...] = tops[place.half]

    @pl.when(give_top)
    def _():
        given[...] = tops[place.half]

    @pl.when(jnp.logical_not(give_top))
    def _():
        given[...] = saved[0]


def staged(bounds, saved, tops):
    block = jax.ShapeDtypeStruct(saved.shape[1:], saved.dtype)
    return pl.pallas_call(
        staged_kernel,
        out_shape=(block,) * 3 + (jax.ShapeDtypeStruct((8, 128), jnp.int32),),
        in_specs=[SMEM, VMEM, VMEM, VMEM],
        out_specs=(VMEM,) * 4,
        compiler_params=pltpu.CompilerParams(vmem_limit_bytes=KERNEL_BYTES),
        cost_estimate=pl.CostEstimate(flops=STAGE_FLOPS, bytes_accessed=8 * saved.size, transcendentals=0),
        name="staged",
    )(bounds, opening(), saved, tops)


def by_role_kernel(flag, full_part, short_part, chosen):
    place = Place(flag[0, 0] > 0)

    @pl.when(place.short)
    def _():
        chosen[...] = short_part[...]

    @pl.when(jnp.logical_not(place.short))
    def _():
        chosen[...] = full_part[...]


def by_role(flag, full_part, short_part):
    return pl.pallas_call(
        by_role_kernel,
        out_shape=jax.ShapeDtypeStruct(full_part.shape, full_part.dtype),
        in_specs=[VMEM] * 3,
        out_specs=VMEM,
        compiler_params=pltpu.CompilerParams(vmem_limit_bytes=KERNEL_BYTES),
        name="by_role",
    )(flag, full_part, short_part)


BLOCKS = 4


def put_unit(unit, first, second):
    rows = first.shape[0]
    unit[:rows, :] = norm_rows(first[...])[0].astype(jnp.bfloat16)
    unit[rows:, :] = norm_rows(second[...])[0].astype(jnp.bfloat16)


def lane_block(j, place, lanes):
    owner = place.relay if j // 2 else 1 - place.relay
    return pl.ds(pl.multiple_of((4 * (j % 2) + 2 * owner + place.core) * lanes, lanes), lanes)


def unit_columns(place, unit, unit_part):
    lanes = unit.shape[1] // (2 * BLOCKS)
    for j in range(BLOCKS):
        unit_part[:, j * lanes : (j + 1) * lanes] = unit[:, lane_block(j, place, lanes)]


def core_columns(place, unit, w_in, unit_part, value):
    lanes = unit.shape[1] // (2 * BLOCKS)
    for j in range(BLOCKS):
        block = lane_block(j, place, lanes)
        where = pl.ds(j * lanes, lanes)
        unit_part[:, where] = unit[:, block]
        value[:, where] = jnp.dot(
            unit[...], w_in[place.slot, :, block], preferred_element_type=jnp.float32
        ).astype(jnp.bfloat16)


def early_kernel(flag, e1, e2, f1, f2, w_in, w_out, early_part, unit_part, value, unit):
    place = Place(flag[0, 0] > 0)

    @pl.when(jnp.logical_not(place.short))
    def _():
        put_unit(unit, e2, f2)
        unit_columns(place, unit, unit_part)
        value[...] = jnp.zeros_like(value)
        put_unit(unit, e1, f1)
        unit_columns(place, unit, early_part)

    @pl.when(place.short)
    def _():
        put_unit(unit, e1, f1)
        core_columns(place, unit, w_in, unit_part, value)
        both = jnp.concatenate([e2[...], f2[...]], axis=0)
        early_part[...] = nt_dot(both, w_out[place.slot]).astype(jnp.bfloat16)


def early_factors(flag, own, partner, w_in, w_out):
    rows, model = own[0].shape
    inner = w_in.shape[2]
    part = model // 2
    return pl.pallas_call(
        early_kernel,
        out_shape=(
            jax.ShapeDtypeStruct((2 * rows, model), jnp.bfloat16),
            jax.ShapeDtypeStruct((2 * rows, part), jnp.bfloat16),
            jax.ShapeDtypeStruct((2 * rows, part), jnp.bfloat16),
        ),
        in_specs=[VMEM] * 7,
        out_specs=(VMEM,) * 3,
        scratch_shapes=[pltpu.VMEM((2 * rows, model), jnp.bfloat16)],
        compiler_params=pltpu.CompilerParams(vmem_limit_bytes=KERNEL_BYTES),
        cost_estimate=pl.CostEstimate(
            flops=4 * rows * model * inner, bytes_accessed=3 * model * inner, transcendentals=0
        ),
        name="early",
    )(flag, *own, *partner, w_in, w_out)


def middle_kernel(flag, e3, f3, unit_part, value, w_out, in_acc, out_acc):
    place = Place(flag[0, 0] > 0)
    grads = jnp.concatenate([e3[...], f3[...]], axis=0)
    err = nt_dot(grads, w_out[place.slot]).astype(jnp.bfloat16)
    in_acc[...] = tn_dot(unit_part[...], err)
    out_acc[...] = tn_dot(value[...], grads)


def middle_partials(flag, e3, f3, unit_part, value, w_out):
    rows, model = e3.shape
    inner = w_out.shape[1]
    part = unit_part.shape[1]
    return pl.pallas_call(
        middle_kernel,
        out_shape=(
            jax.ShapeDtypeStruct((part, inner), jnp.float32),
            jax.ShapeDtypeStruct((part, model), jnp.float32),
        ),
        in_specs=[VMEM] * 6,
        out_specs=(VMEM,) * 2,
        compiler_params=pltpu.CompilerParams(vmem_limit_bytes=KERNEL_BYTES),
        cost_estimate=pl.CostEstimate(
            flops=8 * rows * model * inner, bytes_accessed=3 * model * inner, transcendentals=0
        ),
        name="middle",
    )(flag, e3, f3, unit_part, value, w_out)


def split_sums(place, left_part, right_part, acc, x_send, x_keep, z_send, z_keep):
    group = left_part.shape[1] // 2
    block = group // 2
    cols = right_part.shape[1] // 2

    def sums(rows_of, cols_of):
        new = tn_dot(left_part[:, rows_of], right_part[:, cols_of])
        return new if acc is None else acc[rows_of, cols_of] + new

    far = slice(0, group)
    every = slice(None)
    mine = pl.ds(pl.multiple_of(place.column * cols, cols), cols)
    other = pl.ds(pl.multiple_of((1 - place.column) * cols, cols), cols)
    kept = pl.ds(pl.multiple_of(group + place.half * block, block), block)
    sent = pl.ds(pl.multiple_of(group + (1 - place.half) * block, block), block)
    x_send[...] = sums(far, other).astype(jnp.bfloat16)
    x_keep[...] = sums(far, mine)
    z_send[...] = sums(sent, every).astype(jnp.bfloat16)
    z_keep[...] = sums(kept, every)


def late_in_kernel(
    flag, late, flate, early_part, in_acc, w_out, x_send, x_keep, z_send, z_keep, unit, unit_part, err,
):
    place = Place(flag[0, 0] > 0)
    part = unit_part.shape[1]

    @pl.when(jnp.logical_not(place.short))
    def _():
        grads = jnp.concatenate([late[...], flate[...]], axis=0)
        err[...] = nt_dot(grads, w_out[place.slot]).astype(jnp.bfloat16)
        unit_part[...] = early_part[:, :part]

    @pl.when(place.short)
    def _():
        put_unit(unit, late, flate)
        unit_columns(place, unit, unit_part)
        err[...] = early_part[...]

    split_sums(place, unit_part, err, in_acc, x_send, x_keep, z_send, z_keep)


def late_out_kernel(
    flag, unit, e2, f2, out_acc, w_in, up, fup, low, flow,
    x_send, x_keep, z_send, z_keep, value, grads, unit_part,
):
    place = Place(flag[0, 0] > 0)
    rows = e2.shape[0]
    part = value.shape[1]
    lanes = part // BLOCKS
    outs = (x_send, x_keep, z_send, z_keep)

    def put_grads(first, second):
        grads[:rows, :] = first[...]
        grads[rows:, :] = second[...]

    @pl.when(place.left)
    def _():
        core_columns(place, unit, w_in, unit_part, value)
        put_grads(e2, f2)
        split_sums(place, value, grads, out_acc, *outs)

    @pl.when(jnp.logical_not(place.left))
    def _():
        for j in range(BLOCKS):
            block = lane_block(j, place, lanes)
            where = pl.ds(j * lanes, lanes)
            value[:rows, where] = up[0, :, block]
            value[rows:, where] = fup[0, :, block]

        @pl.when(place.short)
        def _():
            put_grads(up.at[1], fup.at[1])

        @pl.when(jnp.logical_not(place.short))
        def _():
            put_grads(low, flow)

        split_sums(place, value, grads, None, *outs)


def split_shapes(part, width):
    return (
        low_shape(part // 2, width // 2),
        full_shape(part // 2, width // 2),
        low_shape(part // 4, width),
        full_shape(part // 4, width),
    )


def x_add_kernel(keep, land, mine, following):
    half = lax.axis_index("section") % 2
    rows = mine.shape[0]
    kept = pl.ds(pl.multiple_of(half * rows, rows), rows)
    sent = pl.ds(pl.multiple_of((1 - half) * rows, rows), rows)
    mine[...] = keep[kept, :] + land[kept, :].astype(jnp.float32)
    following[...] = (keep[sent, :] + land[sent, :].astype(jnp.float32)).astype(jnp.bfloat16)


def z_add_kernel(keep, land, mine, following):
    column = lax.axis_index("tensor")
    cols = mine.shape[1]
    kept = pl.ds(pl.multiple_of(column * cols, cols), cols)
    sent = pl.ds(pl.multiple_of((1 - column) * cols, cols), cols)
    mine[...] = keep[:, kept] + land[:, kept].astype(jnp.float32)
    following[...] = (keep[:, sent] + land[:, sent].astype(jnp.float32)).astype(jnp.bfloat16)


def last_add_kernel(mine, land, total):
    total[...] = (mine[...] + land[...].astype(jnp.float32)).astype(total.dtype)


def hand_on_kernel(flag, near, got, give, lower):
    place = Place(flag[0, 0] > 0)

    @pl.when(place.short)
    def _():
        give[...] = got[...]
        lower[...] = near[...]

    @pl.when(jnp.logical_not(place.short))
    def _():
        give[...] = near[...].astype(jnp.bfloat16)
        lower[...] = got[...].astype(jnp.float32)


def results_kernel(flag, lower, landed, near, got, in_result, out_result):
    place = Place(flag[0, 0] > 0)

    @pl.when(place.left)
    def _():
        in_result[0] = lower[...]

    @pl.when(jnp.logical_not(place.left))
    def _():
        in_result[0] = landed[...].astype(jnp.float32)
        out_result[0] = near[...] + got[...].astype(jnp.float32)

    @pl.when(place.left & place.short)
    def _():
        out_result[0] = near[...]

    @pl.when(place.left & jnp.logical_not(place.short))
    def _():
        out_result[0] = got[...].astype(jnp.float32)


def small_call(kernel, operands, shapes, scratch=(), flops=0):
    cost = pl.CostEstimate(flops=flops, bytes_accessed=0, transcendentals=0) if flops else None
    return pl.pallas_call(
        kernel,
        out_shape=shapes,
        in_specs=[VMEM] * len(operands),
        out_specs=jax.tree.map(lambda _: VMEM, shapes),
        scratch_shapes=scratch,
        compiler_params=pltpu.CompilerParams(vmem_limit_bytes=KERNEL_BYTES),
        cost_estimate=cost,
    )(*operands)


def low_shape(*dims):
    return jax.ShapeDtypeStruct(dims, jnp.bfloat16)


def full_shape(*dims):
    return jax.ShapeDtypeStruct(dims, jnp.float32)


def flipped(value, axis, bit):
    return lax.ppermute(value, axis, [(i, i ^ bit) for i in range(lax.axis_size(axis))])


def two_section_body(bounds, saved_inputs, w_in, w_out, top_grad):
    saved = saved_inputs[0, 0]
    proj_in = w_in[0, 0]
    proj_out = w_out[0, 0]
    tops = top_grad[0]
    model = saved.shape[2]
    inner = proj_in.shape[2]

    def across(value):
        return flipped(value, "pipe", 2)

    def core_swap(value):
        return flipped(value, "pipe", 1)

    def half_swap(value):
        return flipped(value, "section", 1)

    def column_swap(value):
        return flipped(value, "tensor", 1)

    half_axis = lax.axis_size("section") // 2

    def upward(value):
        return lax.ppermute(value, "section", [(i, i + half_axis) for i in range(half_axis)])

    def downward(value):
        return lax.ppermute(value, "section", [(i + half_axis, i) for i in range(half_axis)])

    def section_swap(value):
        return flipped(value, "section", 2)

    own_saved, own_top, given, flag = staged(bounds, saved, tops)
    swapped = across(given)
    rows = saved.shape[1]
    grad_low, upload = chain(flag, tops, saved, proj_in, proj_out)
    lifted = upward(upload)
    hopping = by_role(flag, grad_low, swapped)
    late = downward(hopping)
    grad_other = across(grad_low)
    own = (own_saved, swapped)
    partner = tuple(core_swap(part) for part in own)
    early_part, unit_part, value = early_factors(flag, own, partner, proj_in, proj_out)
    grad_early = by_role(flag, grad_other, own_top)
    in_acc, out_acc = middle_partials(flag, grad_early, core_swap(grad_early), unit_part, value, proj_out)
    other_low = core_swap(grad_low)
    other_lifted = core_swap(lifted)
    other_late = core_swap(late)
    part = model // 2
    pair = 2 * rows
    *in_parts, unit_late = small_call(
        late_in_kernel,
        (flag, late, other_late, early_part, in_acc, proj_out),
        split_shapes(part, inner) + (low_shape(pair, model),),
        scratch=[pltpu.VMEM((pair, part), jnp.bfloat16), pltpu.VMEM((pair, inner), jnp.bfloat16)],
        flops=6 * rows * model * inner,
    )
    out_parts = small_call(
        late_out_kernel,
        (flag, unit_late, own[1], partner[1], out_acc, proj_in)
        + (lifted, other_lifted, grad_low, other_low),
        split_shapes(part, model),
        scratch=[
            pltpu.VMEM((pair, part), jnp.bfloat16),
            pltpu.VMEM((pair, model), jnp.bfloat16),
            pltpu.VMEM((pair, part), jnp.bfloat16),
        ],
        flops=4 * rows * model * inner,
    )
    block = (model // (2 * BLOCKS), model // 2)
    sums = []
    for (x_send, x_keep, z_send, z_keep) in (in_parts, out_parts):
        pair_shapes = (full_shape(*block), low_shape(*block))
        x_land = column_swap(x_send)
        z_land = half_swap(z_send)
        far, far_next = small_call(x_add_kernel, (x_keep, x_land), pair_shapes)
        near, near_next = small_call(z_add_kernel, (z_keep, z_land), pair_shapes)
        far_land = half_swap(far_next)
        near_land = column_swap(near_next)
        far = small_call(last_add_kernel, (far, far_land), low_shape(*block))
        got = across(far)
        near = small_call(last_add_kernel, (near, near_land), full_shape(*block))
        sums.append((near, got))
    (in_near, in_got), (out_near, out_got) = sums
    give, lower = small_call(
        hand_on_kernel, (flag, in_near, in_got), (low_shape(*block), full_shape(*block))
    )
    landed = section_swap(give)
    return small_call(
        results_kernel, (flag, lower, landed, out_near, out_got), (full_shape(1, *block),) * 2
    )


def body(bounds, saved_inputs, w_in, w_out, top_grad):
    two_sections = lax.axis_size("section") == 4 and lax.axis_size("pipe") == 4
    if two_sections and lax.axis_size("tensor") == 2:
        return two_section_body(bounds, saved_inputs, w_in, w_out, top_grad)
    return general_body(bounds, saved_inputs, w_in, w_out, top_grad)


def solution(mesh):
    placed = (
        P(),
        P("pipe", "section", None, "tensor", None),
        P("pipe", "section", None, None, None),
        P("pipe", "section", None, None, None),
        P("pipe", None, "tensor", None),
    )
    return jax.shard_map(
        body,
        mesh=mesh,
        in_specs=placed,
        out_specs=(P("section", "pipe", "tensor"), P("section", "pipe", "tensor")),
        check_vma=False,
    )
```

```python
import jax
import jax.numpy as jnp
from jax import lax
from jax.experimental import pallas as pl
from jax.experimental.pallas import tpu as pltpu
from jax.sharding import PartitionSpec as P

EPS = 1e-05


def shifted(value, axis, steps):
    count = lax.axis_size(axis)
    pairs = [(source, (source + steps) % count) for source in range(count)]
    return lax.ppermute(value, axis, pairs)


def for_sending(shard):

    def short(part):
        return part.astype(jnp.bfloat16) if part.dtype == jnp.float32 else part

    return jax.tree.map(short, shard)


def partner(block, axis, bit):
    count = lax.axis_size(axis)
    route = []
    for low in range(count):
        high = low | 1 << bit
        if high != low and high < count:
            route += [(low, high), (high, low)]
    return lax.ppermute(block, axis, route)


def normalize(saved_rows):
    floats = saved_rows.astype(jnp.float32)
    row_scale = jnp.sqrt(jnp.mean(floats * floats, axis=-1, keepdims=True) + EPS)
    return (floats / row_scale, row_scale)


def layer_back(grad_next, unit_rows, row_scale, proj_in, proj_out):
    err_low = jnp.dot(grad_next, proj_out.T, preferred_element_type=jnp.float32).astype(
        jnp.bfloat16
    )
    pulled = jnp.dot(err_low, proj_in.T, preferred_element_type=jnp.float32)
    inner_mean = jnp.mean(pulled * unit_rows, axis=-1, keepdims=True)
    grad_here = (
        grad_next.astype(jnp.float32) + (pulled - unit_rows * inner_mean) / row_scale
    ).astype(jnp.bfloat16)
    return (grad_here, err_low)


def route_items(members, shifter, offset, occupied, positions, here_section, levels, sections):
    for bit_level in reversed(range(levels)):
        stride = 2**bit_level
        passed = offset // (2 * stride) * (2 * stride)
        present = occupied & ((positions[:, None] + passed) % sections == here_section)
        rising = offset // stride % 2 == 1
        send_mask = jnp.any(present & rising, axis=0)
        keep_mask = jnp.any(present & jnp.logical_not(rising), axis=0)
        outgoing = tuple(
            (
                jnp.where(send_mask[:, None, None], member, jnp.zeros_like(member))
                for member in members
            )
        )
        arrived = shifter(outgoing, stride)
        members = tuple(
            (
                jnp.where(keep_mask[:, None, None], member, jnp.zeros_like(member)) + landed
                for member, landed in zip(members, arrived)
            )
        )
    return members


def general_body(bounds, saved_inputs, w_in, w_out, top_grad):
    sections = lax.axis_size("section") // 2
    tensors = lax.axis_size("tensor")
    pipe_index = lax.axis_index("pipe")
    section_index = lax.axis_index("section")
    tensor_index = lax.axis_index("tensor")
    position = section_index // 2
    token_half = section_index % 2
    boundary = lax.dynamic_index_in_dim(bounds, pipe_index // 2, 0, keepdims=False)
    counts = boundary[1:] - boundary[:-1]
    layers_here = lax.dynamic_index_in_dim(counts, position, 0, keepdims=False)
    saved_rows = saved_inputs[0, 0]
    proj_in = w_in[0, 0]
    proj_out = w_out[0, 0]
    slot_count = saved_rows.shape[0]
    row_count = saved_rows.shape[1]
    model_width = saved_rows.shape[2]
    inner_width = proj_in.shape[2]
    unit_rows, scales = normalize(saved_rows)
    unit_low = unit_rows.astype(jnp.bfloat16)
    value_low = jnp.einsum(
        "kre,kea->kra", unit_low, proj_in, preferred_element_type=jnp.float32
    ).astype(jnp.bfloat16)
    positions = jnp.arange(sections, dtype=jnp.int32)
    slot_ids = jnp.arange(slot_count, dtype=jnp.int32)
    occupied = slot_ids[None, :] < counts[:, None]
    layer_of = boundary[:-1, None] + slot_ids[None, :]
    offset = (layer_of + 1 - positions[:, None]) % sections
    levels = min((sections - 3 * sections // 4 + 1).bit_length(), (sections - 1).bit_length())
    top_rows = lax.dynamic_index_in_dim(top_grad[0], token_half, 0, keepdims=False)

    def run_section(incoming):

        def upper_layer(grad_top):
            return layer_back(grad_top, unit_rows[1], scales[1], proj_in[1], proj_out[1])

        def lower_layer(grad_top):
            return layer_back(grad_top, unit_rows[0], scales[0], proj_in[0], proj_out[0])

        def no_layer(grad_top):
            return (grad_top, jnp.zeros((row_count, inner_width), jnp.bfloat16))

        lower_start, upper_err = lax.cond(layers_here == 2, upper_layer, no_layer, incoming)
        result, lower_err = lax.cond(layers_here >= 1, lower_layer, no_layer, lower_start)
        return (result, jnp.stack([lower_start, incoming]), jnp.stack([lower_err, upper_err]))

    def loop_turn(turn_index, carried):
        incoming = shifted(carried[0], "section", -2)
        return lax.cond(
            position == sections - 1 - turn_index,
            lambda arriving, kept: run_section(arriving),
            lambda arriving, kept: kept,
            incoming,
            carried,
        )

    start_rows = jnp.where(position == 0, top_rows, jnp.zeros_like(top_rows))
    carried = (
        start_rows,
        jnp.zeros((slot_count, row_count, model_width), jnp.bfloat16),
        jnp.zeros((slot_count, row_count, inner_width), jnp.bfloat16),
    )
    carried = lax.fori_loop(0, sections, loop_turn, carried)
    grads_slots = carried[1]
    errors = carried[2]
    unit_got, value_got, err_got, grad_got = route_items(
        (unit_low, value_low, errors, grads_slots),
        lambda members, stride: jax.tree.map(
            lambda part, own: part.astype(own.dtype),
            shifted(for_sending(members), "section", 2 * stride),
            members,
        ),
        offset,
        occupied,
        positions,
        position,
        levels,
        sections,
    )
    owner_slot = jnp.sum(
        jnp.where(occupied & ((layer_of + 1) % sections == position), slot_ids[None, :], 0)
    )
    unit_own = lax.dynamic_index_in_dim(unit_got, owner_slot, 0, keepdims=False)
    value_own = lax.dynamic_index_in_dim(value_got, owner_slot, 0, keepdims=False)
    err_own = lax.dynamic_index_in_dim(err_got, owner_slot, 0, keepdims=False)
    grad_own = lax.dynamic_index_in_dim(grad_got, owner_slot, 0, keepdims=False)
    in_cols = inner_width // tensors
    out_cols = model_width // tensors
    unit_piece = lax.all_gather(unit_own, "tensor", axis=0, tiled=True)
    value_piece = lax.all_gather(value_own, "tensor", axis=0, tiled=True)
    err_piece = lax.all_gather(err_own, "tensor", axis=0, tiled=True)
    grad_piece = lax.all_gather(grad_own, "tensor", axis=0, tiled=True)
    err_cols = lax.dynamic_slice_in_dim(err_piece, tensor_index * in_cols, in_cols, 1)
    grad_cols = lax.dynamic_slice_in_dim(grad_piece, tensor_index * out_cols, out_cols, 1)
    totals = (
        jnp.dot(unit_piece.T, err_cols, preferred_element_type=jnp.float32),
        jnp.dot(value_piece.T, grad_cols, preferred_element_type=jnp.float32),
    )
    half_model = model_width // 2
    half_inner = inner_width // 2
    mine_in = lax.dynamic_slice_in_dim(totals[0], token_half * half_model, half_model, 0)
    other_in = lax.dynamic_slice_in_dim(totals[0], (1 - token_half) * half_model, half_model, 0)
    mine_out = lax.dynamic_slice_in_dim(totals[1], token_half * half_inner, half_inner, 0)
    other_out = lax.dynamic_slice_in_dim(totals[1], (1 - token_half) * half_inner, half_inner, 0)
    landed_in, landed_out = partner((other_in, other_out), "section", 0)
    grad_in_part, grad_out_part = (
        lax.psum_scatter(mine_in + landed_in, "pipe", scatter_dimension=0, tiled=True),
        lax.psum_scatter(mine_out + landed_out, "pipe", scatter_dimension=0, tiled=True),
    )
    return (grad_in_part[None], grad_out_part[None])


VMEM = pl.BlockSpec(memory_space=pltpu.VMEM)
SMEM = pl.BlockSpec(memory_space=pltpu.SMEM)
KERNEL_BYTES = 14 * 2**20
STAGE_FLOPS = 8 * 10**9


class Place:
    def __init__(self, short):
        pipe = lax.axis_index("pipe")
        section = lax.axis_index("section")
        self.column = lax.axis_index("tensor")
        self.relay = pipe // 2
        self.core = pipe % 2
        self.half = section % 2
        self.left = section < 2
        self.short = short
        self.slot = jnp.where(self.short, 1, 0)
        self.upper_slot = jnp.where(self.left, 1, 0)


def norm_rows(saved):
    floats = saved.astype(jnp.float32)
    row_scale = jnp.sqrt(jnp.mean(floats * floats, axis=-1, keepdims=True) + EPS)
    return floats / row_scale, row_scale


def nt_dot(left, right):
    return lax.dot_general(left, right, (((1,), (1,)), ((), ())), preferred_element_type=jnp.float32)


def tn_dot(left, right):
    return lax.dot_general(left, right, (((0,), (0,)), ((), ())), preferred_element_type=jnp.float32)


def chain_kernel(flag, tops, saved, w_in, w_out, grad_out, upward):
    place = Place(flag[0, 0] > 0)
    slot = place.upper_slot
    first_unit = norm_rows(saved[0])[0].astype(jnp.bfloat16)
    upward[0] = jnp.dot(first_unit, w_in[0], preferred_element_type=jnp.float32).astype(jnp.bfloat16)
    grad_next = tops[place.half]
    err = nt_dot(grad_next, w_out[slot]).astype(jnp.bfloat16)
    unit, row_scale = norm_rows(saved[slot])
    pulled = nt_dot(err, w_in[slot])
    inner_mean = jnp.mean(pulled * unit, axis=-1, keepdims=True)
    back = grad_next.astype(jnp.float32) + (pulled - unit * inner_mean) / row_scale
    grad_low = back.astype(jnp.bfloat16)
    grad_out[...] = grad_low
    upward[1] = grad_low


def chain(flag, tops, saved, w_in, w_out):
    rows, model = saved.shape[1:]
    inner = w_in.shape[2]
    return pl.pallas_call(
        chain_kernel,
        out_shape=(low_shape(rows, model), low_shape(2, rows, model)),
        in_specs=[VMEM] * 5,
        out_specs=(VMEM,) * 2,
        compiler_params=pltpu.CompilerParams(vmem_limit_bytes=KERNEL_BYTES),
        cost_estimate=pl.CostEstimate(
            flops=6 * rows * model * inner, bytes_accessed=4 * model * inner, transcendentals=0
        ),
        name="chain",
    )(flag, tops, saved, w_in, w_out)


def opening_kernel(mark):
    mark[...] = jnp.zeros_like(mark)


def opening():
    return pl.pallas_call(
        opening_kernel,
        out_shape=jax.ShapeDtypeStruct((8, 128), jnp.float32),
        out_specs=VMEM,
        compiler_params=pltpu.CompilerParams(vmem_limit_bytes=KERNEL_BYTES),
        cost_estimate=pl.CostEstimate(flops=STAGE_FLOPS, bytes_accessed=4096, transcendentals=0),
        name="opening",
    )()


def staged_kernel(bounds, mark, saved, tops, own_saved, own_top, given, flag):
    relay = lax.axis_index("pipe") // 2
    place = Place(bounds[relay, 1] - bounds[relay, 0] == 2)
    give_top = place.left & jnp.logical_not(place.short)
    flag[...] = jnp.full_like(flag, jnp.where(place.short, 1, 0))
    own_saved[...] = saved[place.slot]
    own_top[...] = tops[place.half]

    @pl.when(give_top)
    def _():
        given[...] = tops[place.half]

    @pl.when(jnp.logical_not(give_top))
    def _():
        given[...] = saved[0]


def staged(bounds, saved, tops):
    block = jax.ShapeDtypeStruct(saved.shape[1:], saved.dtype)
    return pl.pallas_call(
        staged_kernel,
        out_shape=(block,) * 3 + (jax.ShapeDtypeStruct((8, 128), jnp.int32),),
        in_specs=[SMEM, VMEM, VMEM, VMEM],
        out_specs=(VMEM,) * 4,
        compiler_params=pltpu.CompilerParams(vmem_limit_bytes=KERNEL_BYTES),
        cost_estimate=pl.CostEstimate(flops=STAGE_FLOPS, bytes_accessed=8 * saved.size, transcendentals=0),
        name="staged",
    )(bounds, opening(), saved, tops)


def by_role_kernel(flag, full_part, short_part, chosen):
    place = Place(flag[0, 0] > 0)

    @pl.when(place.short)
    def _():
        chosen[...] = short_part[...]

    @pl.when(jnp.logical_not(place.short))
    def _():
        chosen[...] = full_part[...]


def by_role(flag, full_part, short_part):
    return pl.pallas_call(
        by_role_kernel,
        out_shape=jax.ShapeDtypeStruct(full_part.shape, full_part.dtype),
        in_specs=[VMEM] * 3,
        out_specs=VMEM,
        compiler_params=pltpu.CompilerParams(vmem_limit_bytes=KERNEL_BYTES),
        name="by_role",
    )(flag, full_part, short_part)


BLOCKS = 4


def put_unit(unit, first, second):
    rows = first.shape[0]
    unit[:rows, :] = norm_rows(first[...])[0].astype(jnp.bfloat16)
    unit[rows:, :] = norm_rows(second[...])[0].astype(jnp.bfloat16)


def lane_block(j, place, lanes):
    owner = place.relay if j // 2 else 1 - place.relay
    return pl.ds(pl.multiple_of((4 * (j % 2) + 2 * owner + place.core) * lanes, lanes), lanes)


def unit_columns(place, unit, unit_part):
    lanes = unit.shape[1] // (2 * BLOCKS)
    for j in range(BLOCKS):
        unit_part[:, j * lanes : (j + 1) * lanes] = unit[:, lane_block(j, place, lanes)]


def core_columns(place, unit, w_in, unit_part, value):
    lanes = unit.shape[1] // (2 * BLOCKS)
    for j in range(BLOCKS):
        block = lane_block(j, place, lanes)
        where = pl.ds(j * lanes, lanes)
        unit_part[:, where] = unit[:, block]
        value[:, where] = jnp.dot(
            unit[...], w_in[place.slot, :, block], preferred_element_type=jnp.float32
        ).astype(jnp.bfloat16)


def early_kernel(flag, e1, e2, f1, f2, w_in, w_out, early_part, unit_part, value, unit):
    place = Place(flag[0, 0] > 0)

    @pl.when(jnp.logical_not(place.short))
    def _():
        put_unit(unit, e2, f2)
        unit_columns(place, unit, unit_part)
        value[...] = jnp.zeros_like(value)
        put_unit(unit, e1, f1)
        unit_columns(place, unit, early_part)

    @pl.when(place.short)
    def _():
        put_unit(unit, e1, f1)
        core_columns(place, unit, w_in, unit_part, value)
        both = jnp.concatenate([e2[...], f2[...]], axis=0)
        early_part[...] = nt_dot(both, w_out[place.slot]).astype(jnp.bfloat16)


def early_factors(flag, own, partner, w_in, w_out):
    rows, model = own[0].shape
    inner = w_in.shape[2]
    part = model // 2
    return pl.pallas_call(
        early_kernel,
        out_shape=(
            jax.ShapeDtypeStruct((2 * rows, model), jnp.bfloat16),
            jax.ShapeDtypeStruct((2 * rows, part), jnp.bfloat16),
            jax.ShapeDtypeStruct((2 * rows, part), jnp.bfloat16),
        ),
        in_specs=[VMEM] * 7,
        out_specs=(VMEM,) * 3,
        scratch_shapes=[pltpu.VMEM((2 * rows, model), jnp.bfloat16)],
        compiler_params=pltpu.CompilerParams(vmem_limit_bytes=KERNEL_BYTES),
        cost_estimate=pl.CostEstimate(
            flops=4 * rows * model * inner, bytes_accessed=3 * model * inner, transcendentals=0
        ),
        name="early",
    )(flag, *own, *partner, w_in, w_out)


def middle_kernel(flag, e3, f3, unit_part, value, w_out, in_acc, out_acc):
    place = Place(flag[0, 0] > 0)
    grads = jnp.concatenate([e3[...], f3[...]], axis=0)
    err = nt_dot(grads, w_out[place.slot]).astype(jnp.bfloat16)
    in_acc[...] = tn_dot(unit_part[...], err)
    out_acc[...] = tn_dot(value[...], grads)


def middle_partials(flag, e3, f3, unit_part, value, w_out):
    rows, model = e3.shape
    inner = w_out.shape[1]
    part = unit_part.shape[1]
    return pl.pallas_call(
        middle_kernel,
        out_shape=(
            jax.ShapeDtypeStruct((part, inner), jnp.float32),
            jax.ShapeDtypeStruct((part, model), jnp.float32),
        ),
        in_specs=[VMEM] * 6,
        out_specs=(VMEM,) * 2,
        compiler_params=pltpu.CompilerParams(vmem_limit_bytes=KERNEL_BYTES),
        cost_estimate=pl.CostEstimate(
            flops=8 * rows * model * inner, bytes_accessed=3 * model * inner, transcendentals=0
        ),
        name="middle",
    )(flag, e3, f3, unit_part, value, w_out)


def split_sums(place, left_part, right_part, acc, x_sum, z_sum, keep):
    group = left_part.shape[1] // 2
    block = group // 2
    cols = right_part.shape[1] // 2
    column = place.column if keep else 1 - place.column
    half = place.half if keep else 1 - place.half

    def sums(rows_of, cols_of):
        new = tn_dot(left_part[:, rows_of], right_part[:, cols_of])
        return new if acc is None else acc[rows_of, cols_of] + new

    cols_of = pl.ds(pl.multiple_of(column * cols, cols), cols)
    rows_of = pl.ds(pl.multiple_of(group + half * block, block), block)
    x_sum[...] = sums(slice(0, group), cols_of).astype(x_sum.dtype)
    z_sum[...] = sums(rows_of, slice(None)).astype(z_sum.dtype)


def late_in_kernel(flag, late, flate, early_part, in_acc, w_out, x_send, z_send, unit_part, err, unit):
    place = Place(flag[0, 0] > 0)
    part = unit_part.shape[1]

    @pl.when(jnp.logical_not(place.short))
    def _():
        grads = jnp.concatenate([late[...], flate[...]], axis=0)
        err[...] = nt_dot(grads, w_out[place.slot]).astype(jnp.bfloat16)
        unit_part[...] = early_part[:, :part]

    @pl.when(place.short)
    def _():
        put_unit(unit, late, flate)
        unit_columns(place, unit, unit_part)
        err[...] = early_part[...]

    split_sums(place, unit_part, err, in_acc, x_send, z_send, False)


def in_keep_kernel(flag, unit_part, err, in_acc, x_keep, z_keep):
    split_sums(Place(flag[0, 0] > 0), unit_part, err, in_acc, x_keep, z_keep, True)


def late_out_kernel(
    flag, unit, e2, f2, out_acc, w_in, up, fup, low, flow, x_send, z_send, value, grads, unit_part,
):
    place = Place(flag[0, 0] > 0)
    rows = e2.shape[0]
    part = value.shape[1]
    lanes = part // BLOCKS

    def put_grads(first, second):
        grads[:rows, :] = first[...]
        grads[rows:, :] = second[...]

    @pl.when(place.left)
    def _():
        core_columns(place, unit, w_in, unit_part, value)
        put_grads(e2, f2)
        split_sums(place, value, grads, out_acc, x_send, z_send, False)

    @pl.when(jnp.logical_not(place.left))
    def _():
        for j in range(BLOCKS):
            block = lane_block(j, place, lanes)
            where = pl.ds(j * lanes, lanes)
            value[:rows, where] = up[0, :, block]
            value[rows:, where] = fup[0, :, block]

        @pl.when(place.short)
        def _():
            put_grads(up.at[1], fup.at[1])

        @pl.when(jnp.logical_not(place.short))
        def _():
            put_grads(low, flow)

        split_sums(place, value, grads, None, x_send, z_send, False)


def out_keep_kernel(flag, value, grads, out_acc, x_keep, z_keep):
    place = Place(flag[0, 0] > 0)

    @pl.when(place.left)
    def _():
        split_sums(place, value, grads, out_acc, x_keep, z_keep, True)

    @pl.when(jnp.logical_not(place.left))
    def _():
        split_sums(place, value, grads, None, x_keep, z_keep, True)


def split_shapes(part, width, kind):
    return (kind(part // 2, width // 2), kind(part // 4, width))


def x_add_kernel(keep, land, mine, following):
    half = lax.axis_index("section") % 2
    rows = mine.shape[0]
    kept = pl.ds(pl.multiple_of(half * rows, rows), rows)
    sent = pl.ds(pl.multiple_of((1 - half) * rows, rows), rows)
    mine[...] = keep[kept, :] + land[kept, :].astype(jnp.float32)
    following[...] = (keep[sent, :] + land[sent, :].astype(jnp.float32)).astype(jnp.bfloat16)


def z_add_kernel(keep, land, mine, following):
    column = lax.axis_index("tensor")
    cols = mine.shape[1]
    kept = pl.ds(pl.multiple_of(column * cols, cols), cols)
    sent = pl.ds(pl.multiple_of((1 - column) * cols, cols), cols)
    mine[...] = keep[:, kept] + land[:, kept].astype(jnp.float32)
    following[...] = (keep[:, sent] + land[:, sent].astype(jnp.float32)).astype(jnp.bfloat16)


def last_add_kernel(mine, land, total):
    total[...] = (mine[...] + land[...].astype(jnp.float32)).astype(total.dtype)


def hand_on_kernel(flag, near, got, give, lower):
    place = Place(flag[0, 0] > 0)

    @pl.when(place.short)
    def _():
        give[...] = got[...]
        lower[...] = near[...]

    @pl.when(jnp.logical_not(place.short))
    def _():
        give[...] = near[...].astype(jnp.bfloat16)
        lower[...] = got[...].astype(jnp.float32)


def results_kernel(flag, lower, landed, near, got, in_result, out_result):
    place = Place(flag[0, 0] > 0)

    @pl.when(place.left)
    def _():
        in_result[0] = lower[...]

    @pl.when(jnp.logical_not(place.left))
    def _():
        in_result[0] = landed[...].astype(jnp.float32)
        out_result[0] = near[...] + got[...].astype(jnp.float32)

    @pl.when(place.left & place.short)
    def _():
        out_result[0] = near[...]

    @pl.when(place.left & jnp.logical_not(place.short))
    def _():
        out_result[0] = got[...].astype(jnp.float32)


def small_call(kernel, operands, shapes, scratch=(), flops=0):
    cost = pl.CostEstimate(flops=flops, bytes_accessed=0, transcendentals=0) if flops else None
    return pl.pallas_call(
        kernel,
        out_shape=shapes,
        in_specs=[VMEM] * len(operands),
        out_specs=jax.tree.map(lambda _: VMEM, shapes),
        scratch_shapes=scratch,
        compiler_params=pltpu.CompilerParams(vmem_limit_bytes=KERNEL_BYTES),
        cost_estimate=cost,
    )(*operands)


def low_shape(*dims):
    return jax.ShapeDtypeStruct(dims, jnp.bfloat16)


def full_shape(*dims):
    return jax.ShapeDtypeStruct(dims, jnp.float32)


def flipped(value, axis, bit):
    return lax.ppermute(value, axis, [(i, i ^ bit) for i in range(lax.axis_size(axis))])


def two_section_body(bounds, saved_inputs, w_in, w_out, top_grad):
    saved = saved_inputs[0, 0]
    proj_in = w_in[0, 0]
    proj_out = w_out[0, 0]
    tops = top_grad[0]
    model = saved.shape[2]
    inner = proj_in.shape[2]

    def across(value):
        return flipped(value, "pipe", 2)

    def core_swap(value):
        return flipped(value, "pipe", 1)

    def half_swap(value):
        return flipped(value, "section", 1)

    def column_swap(value):
        return flipped(value, "tensor", 1)

    half_axis = lax.axis_size("section") // 2

    def upward(value):
        return lax.ppermute(value, "section", [(i, i + half_axis) for i in range(half_axis)])

    def downward(value):
        return lax.ppermute(value, "section", [(i + half_axis, i) for i in range(half_axis)])

    def section_swap(value):
        return flipped(value, "section", 2)

    own_saved, own_top, given, flag = staged(bounds, saved, tops)
    swapped = across(given)
    rows = saved.shape[1]
    grad_low, upload = chain(flag, tops, saved, proj_in, proj_out)
    lifted = upward(upload)
    hopping = by_role(flag, grad_low, swapped)
    late = downward(hopping)
    grad_other = across(grad_low)
    own = (own_saved, swapped)
    partner = tuple(core_swap(part) for part in own)
    early_part, unit_part, value = early_factors(flag, own, partner, proj_in, proj_out)
    grad_early = by_role(flag, grad_other, own_top)
    in_acc, out_acc = middle_partials(flag, grad_early, core_swap(grad_early), unit_part, value, proj_out)
    other_low = core_swap(grad_low)
    other_lifted = core_swap(lifted)
    other_late = core_swap(late)
    part = model // 2
    pair = 2 * rows
    *in_sends, unit_part, err, unit_late = small_call(
        late_in_kernel,
        (flag, late, other_late, early_part, in_acc, proj_out),
        split_shapes(part, inner, low_shape) + (low_shape(pair, part), low_shape(pair, inner), low_shape(pair, model)),
        flops=5 * rows * model * inner,
    )
    in_keeps = small_call(
        in_keep_kernel, (flag, unit_part, err, in_acc), split_shapes(part, inner, full_shape)
    )
    *out_sends, value, grads = small_call(
        late_out_kernel,
        (flag, unit_late, own[1], partner[1], out_acc, proj_in)
        + (lifted, other_lifted, grad_low, other_low),
        split_shapes(part, model, low_shape) + (low_shape(pair, part), low_shape(pair, model)),
        scratch=[pltpu.VMEM((pair, part), jnp.bfloat16)],
        flops=3 * rows * model * inner,
    )
    out_keeps = small_call(
        out_keep_kernel, (flag, value, grads, out_acc), split_shapes(part, model, full_shape)
    )
    block = (model // (2 * BLOCKS), model // 2)
    sums = []
    for (x_send, z_send), (x_keep, z_keep) in ((in_sends, in_keeps), (out_sends, out_keeps)):
        pair_shapes = (full_shape(*block), low_shape(*block))
        x_land = column_swap(x_send)
        z_land = half_swap(z_send)
        far, far_next = small_call(x_add_kernel, (x_keep, x_land), pair_shapes)
        near, near_next = small_call(z_add_kernel, (z_keep, z_land), pair_shapes)
        far_land = half_swap(far_next)
        near_land = column_swap(near_next)
        far = small_call(last_add_kernel, (far, far_land), low_shape(*block))
        got = across(far)
        near = small_call(last_add_kernel, (near, near_land), full_shape(*block))
        sums.append((near, got))
    (in_near, in_got), (out_near, out_got) = sums
    give, lower = small_call(
        hand_on_kernel, (flag, in_near, in_got), (low_shape(*block), full_shape(*block))
    )
    landed = section_swap(give)
    return small_call(
        results_kernel, (flag, lower, landed, out_near, out_got), (full_shape(1, *block),) * 2
    )


def body(bounds, saved_inputs, w_in, w_out, top_grad):
    two_sections = lax.axis_size("section") == 4 and lax.axis_size("pipe") == 4
    if two_sections and lax.axis_size("tensor") == 2:
        return two_section_body(bounds, saved_inputs, w_in, w_out, top_grad)
    return general_body(bounds, saved_inputs, w_in, w_out, top_grad)


def solution(mesh):
    placed = (
        P(),
        P("pipe", "section", None, "tensor", None),
        P("pipe", "section", None, None, None),
        P("pipe", "section", None, None, None),
        P("pipe", None, "tensor", None),
    )
    return jax.shard_map(
        body,
        mesh=mesh,
        in_specs=placed,
        out_specs=(P("section", "pipe", "tensor"), P("section", "pipe", "tensor")),
        check_vma=False,
    )
```
